32 devices in a mesh: beams: 2 (over y), wind: 4 (over z), cross: 4 (over x, core).
Axes of the slice: x: 2, y: 2, z: 4, core: 2. Of those that a mesh axis runs over, the one named last changes fastest.
Arguments:
- field_real: float32 [2048, 2048], P(('beams', 'wind'), 'cross'), parts along dimension 0, may hold values from -6 to 6
- field_imag: float32 [2048, 2048], P(('beams', 'wind'), 'cross'), parts along dimension 0, may hold values from -6 to 6
- absorb_index: int32 [2, 2048], P(None, 'cross'), may hold values from 0 to 7
- absorb_table: float32 [2, 8], replicated, may hold values from 0.3 to 3
- zone_map: int32 [1024, 2048], P('wind', 'cross'), may hold values from 0 to 7
- zone_conductivity: float32 [8], replicated, may hold values from 0.1 to 1
Outputs:
- field_real: float32 [2048, 2048], P(('beams', 'wind'), 'cross'), parts along dimension 0
- field_imag: float32 [2048, 2048], P(('beams', 'wind'), 'cross'), parts along dimension 0
- screen: float32 [2048, 2048], P(('beams', 'wind'), 'cross'), parts along dimension 0
The draws below stay inside these ranges and needn't reach their ends.
There are 2 independent parts, one for each index of `beams`. The reference program is written for one: setup_inputs(seed, part) draws one part's arguments, and reference() takes and returns one part's arrays. A program takes and returns all parts, laid end to end along the dimension named above; an argument that names none is the same for every part. Nothing has to cross between parts.
All inputs are finite; a program needn't handle non-finite values.
Results may differ from the reference program's by a relative error of at most 0.0003.
Values sent between devices are 32-bit elements; how exact they have to be, the bound alone decides.
No kernel may reach another device: no remote copies, remote signals or barrier semaphores. Data moves between devices by JAX's collectives and lax.ppermute only.
A program may use at most 192 MiB of HBM per device.

```python
import math
import jax
import jax.numpy as jnp

NROW = 1024
NCOL = 2048
LAYERS = 2
ITERS = 2
SMOOTH = 2
LEVELS = 8
ZONES = 8


def place_ends(entries, key, low, largest):
    longest = entries.shape.index(max(entries.shape))
    spots = []
    for shift in (0, 1):
        where = [jax.random.randint(jax.random.fold_in(key, axis), (), 0, length) for axis, length in enumerate(entries.shape)]
        where[longest] = (where[longest] + shift) % entries.shape[longest]
        spots.append(tuple(where))
    return entries.at[spots[0]].set(low).at[spots[1]].set(largest)


def block_scale(own_key, shape, cuts, low, top_value):
    def one(position, parts):
        steps = jax.random.uniform(jax.random.fold_in(jax.random.fold_in(own_key, 6), position), (parts,), jnp.float32, low / len(cuts), top_value / len(cuts))
        return jnp.repeat(jnp.exp(steps), shape[position] // parts).reshape((-1,) + (1,) * (len(shape) - position - 1))

    gain = one(*cuts[0])
    for cut in cuts[1:]:
        gain = gain * one(*cut)
    return gain


def noise(stream_key, extent, scale, reach, pieces=(), held_as=jnp.bfloat16):
    entries = scale * jax.random.normal(stream_key, extent, jnp.float32)
    if pieces:
        entries = entries * block_scale(stream_key, extent, pieces, -0.22, 0.18)
    return jnp.clip(entries, -reach, reach).astype(held_as)


def setup_inputs(seed: int = 0, part: int = 0) -> dict:
    key_of = jax.random.split(jax.random.key(seed), 7)
    part_keys = jax.random.split(jax.random.fold_in(key_of[6], part), 7)
    return {
        "field_real": noise(part_keys[0], (NROW, NCOL), 1.0, 6.0, ((0, 4), (1, 4)), jnp.float32),
        "field_imag": noise(part_keys[1], (NROW, NCOL), 1.0, 6.0, ((0, 4), (1, 4)), jnp.float32),
        "absorb_index": place_ends(jax.random.randint(key_of[2], (LAYERS, NCOL), 0, LEVELS), jax.random.fold_in(key_of[2], 1), 0, LEVELS - 1).astype(jnp.int32),
        "absorb_table": jnp.clip(jnp.exp(jax.random.uniform(key_of[3], (LAYERS, LEVELS), jnp.float32, math.log(0.3), math.log(3.0))), 0.3, 3.0),
        "zone_map": place_ends(jax.random.randint(key_of[4], (NROW, NCOL), 0, ZONES), jax.random.fold_in(key_of[4], 1), 0, ZONES - 1).astype(jnp.int32),
        "zone_conductivity": jnp.clip(jnp.exp(jax.random.uniform(key_of[5], (ZONES,), jnp.float32, math.log(0.1), math.log(1.0))), 0.1, 1.0),
    }


diffraction = 2000.0
conduct_rate = 0.24


def signed_freq(length):
    counter = jnp.arange(length, dtype=jnp.int32)
    shifted = jnp.where(counter < length // 2, counter, counter - length)
    return shifted.astype(jnp.float32) / length


def propagate(field, share_step):
    row_freq = signed_freq(NROW)
    col_freq = signed_freq(NCOL)
    phase_angle = -(share_step * diffraction) * (row_freq[:, None] * row_freq[:, None] + col_freq[None, :] * col_freq[None, :])
    spectrum = jnp.fft.fft2(field)
    return jnp.fft.ifft2(spectrum * (jnp.cos(phase_angle) + 1j * jnp.sin(phase_angle)))


def conduct_core(padded, kappa_pad):
    height = padded.shape[0] - 2
    breadth = padded.shape[1] - 2
    center = padded[1:-1, 1:-1]
    kappa_mid = kappa_pad[1:-1, 1:-1]
    flux_sum = jnp.zeros_like(center)
    for offset_row, offset_col in ((0, 1), (2, 1), (1, 0), (1, 2)):
        neighbour = padded[offset_row:offset_row + height, offset_col:offset_col + breadth]
        kappa_side = kappa_pad[offset_row:offset_row + height, offset_col:offset_col + breadth]
        flux_sum = flux_sum + 0.5 * (kappa_mid + kappa_side) * (neighbour - center)
    return center + conduct_rate * flux_sum


def reference(field_real, field_imag, absorb_index, absorb_table, zone_map, zone_conductivity):
    conductivity = zone_conductivity[zone_map]
    kappa_pad = jnp.pad(conductivity, 1)
    field = field_real + 1j * field_imag
    screen_phase = jnp.zeros((NROW, NCOL), jnp.float32)
    for layer_no in range(LAYERS):
        absorption = absorb_table[layer_no][absorb_index[layer_no]]
        screen_phase = jnp.zeros((NROW, NCOL), jnp.float32)
        for round_no in range(ITERS):
            screened = field * (jnp.cos(screen_phase) + 1j * jnp.sin(screen_phase))
            middle = propagate(screened, 0.5)
            middle_re = jnp.real(middle)
            middle_im = jnp.imag(middle)
            intensity = middle_re * middle_re + middle_im * middle_im
            deposit = absorption[None, :] * intensity * (1.0 / NROW)
            heat_field = jnp.cumsum(deposit, axis=0)
            for smooth_no in range(SMOOTH):
                heat_field = conduct_core(jnp.pad(heat_field, 1), kappa_pad)
            screen_phase = -heat_field
        field = propagate(field * (jnp.cos(screen_phase) + 1j * jnp.sin(screen_phase)), 1.0)
    return jnp.real(field), jnp.imag(field), screen_phase
```

```python
import functools
import math

import jax
import jax.numpy as jnp
import numpy as np
from jax import lax
from jax.experimental import pallas as pl
from jax.experimental.pallas import tpu as pltpu
from jax.sharding import PartitionSpec as P

LAYERS = 2
ITERS = 2
SMOOTH = 2
INNER = 128
CHUNK = 16

diffraction = 2000.0
conduct_rate = 0.24

F32 = jnp.float32
BF16 = jnp.bfloat16
WHOLE = pl.BlockSpec(memory_space=pltpu.VMEM)
SCALAR = pl.BlockSpec(memory_space=pltpu.SMEM)


def split_np(values):
    high = values.astype(np.float32).astype(jnp.bfloat16)
    low = (values - high.astype(np.float64)).astype(np.float32).astype(jnp.bfloat16)
    return high, low


def dft_matrices():
    ids = np.arange(INNER)
    angle = 2.0 * np.pi * (np.outer(ids, ids) % INNER) / INNER
    cosine, sine = np.cos(angle), np.sin(angle)
    left = np.block([[cosine, sine], [-sine, cosine]])
    return np.stack([*split_np(left), *split_np(left.T)])


def chirp_columns(length, shares):
    outer = length // INNER
    k = np.arange(outer)[:, None]
    m = np.arange(INNER)[None, :]
    twist = -2.0 * np.pi * ((k * m) % length) / length
    tables = [np.cos(twist), np.sin(twist)]
    p = k + outer * m
    freq = np.where(p < length // 2, p, p - length) / length
    for share in shares:
        angle = -share * diffraction * freq * freq
        tables += [np.cos(angle) / length, np.sin(angle) / length]
    return np.concatenate(tables, axis=0).astype(np.float32)


def row_table(length, shares):
    cols = chirp_columns(length, shares).T
    return np.pad(cols, ((0, 0), (0, -cols.shape[1] % 128)))


def split(x):
    high = x.astype(BF16)
    return high, (x - high.astype(F32)).astype(BF16)


def times(a, b):
    return (a[0] * b[0] - a[1] * b[1], a[0] * b[1] + a[1] * b[0])


def small_fft(points, sign):
    count = len(points)
    if count == 1:
        return points
    even = small_fft(points[0::2], sign)
    odd = small_fft(points[1::2], sign)
    half = count // 2
    out = [None] * count
    for k in range(half):
        re, im = odd[k]
        if k == 0:
            turn = (re, im)
        elif 4 * k == count:
            turn = (-im, re) if sign > 0 else (im, -re)
        elif 8 * k == count:
            root = math.sqrt(0.5)
            turn = (root * (re - im), root * (im + re)) if sign > 0 else (root * (re + im), root * (im - re))
        elif 8 * k == 3 * count:
            root = math.sqrt(0.5)
            turn = (-root * (re + im), root * (re - im)) if sign > 0 else (root * (im - re), -root * (re + im))
        else:
            c = math.cos(2.0 * math.pi * k / count)
            s = sign * math.sin(2.0 * math.pi * k / count)
            turn = (c * re - s * im, s * re + c * im)
        out[k] = (even[k][0] + turn[0], even[k][1] + turn[1])
        out[k + half] = (even[k][0] - turn[0], even[k][1] - turn[1])
    return out


def cos_sin(x):
    turns = jnp.floor(x * (2.0 / math.pi) + 0.5)
    r = ((x - turns * 1.5703125) - turns * 4.837512969970703125e-4) - turns * 7.549789954891882e-8
    quad = turns.astype(jnp.int32)
    z = r * r
    s = r + r * z * (-1.6666654611e-1 + z * (8.3321608736e-3 - z * 1.9515295891e-4))
    c = 1.0 - 0.5 * z + z * z * (4.166664568298827e-2 + z * (-1.388731625493765e-3 + z * 2.443315711809948e-5))
    odd = (quad & 1) == 1
    sin_x = jnp.where(odd, c, s)
    cos_x = jnp.where(odd, s, c)
    sin_x = jnp.where((quad & 2) == 2, -sin_x, sin_x)
    cos_x = jnp.where(((quad + 1) & 2) == 2, -cos_x, cos_x)
    return cos_x, sin_x


def screened(value, screen):
    return times(value, cos_sin(screen))


def triple(a_high, a_low, b_high, b_low):
    dot = functools.partial(jnp.dot, preferred_element_type=F32)
    return dot(a_high, b_high) + dot(a_high, b_low) + dot(a_low, b_high)


def lower_ones(size):
    r = lax.broadcasted_iota(jnp.int32, (size, size), 0)
    c = lax.broadcasted_iota(jnp.int32, (size, size), 1)
    return jnp.where(r >= c, 1.0, 0.0).astype(BF16)


def chunks(count, body):
    def step(i, carry):
        body(pl.multiple_of(i * CHUNK, CHUNK))
        return carry

    lax.fori_loop(0, count // CHUNK, step, 0)


def along_rows(read, writes, dft, table, xh, xl, y, z):
    outer = xh.shape[1] // 128
    rows = lambda k: pl.ds(k * 128, 128)
    col = lambda part, off: table[pl.ds(off, CHUNK), part : part + 1]

    def put(k, off, value):
        for at, v in ((0, value[0]), (INNER, value[1])):
            xh[pl.ds(at + off, CHUNK), rows(k)], xl[pl.ds(at + off, CHUNK), rows(k)] = split(v)

    def first(off):
        for k, value in enumerate(small_fft([read(a, off) for a in range(outer)], -1)):
            if k:
                value = times(value, (col(k, off), col(outer + k, off)))
            put(k, off, value)

    chunks(INNER, first)
    y[...] = triple(dft[0], dft[1], xh[...], xl[...])
    for n, write in enumerate(writes):

        def middle(off, n=n):
            for k in range(outer):
                value = (y[pl.ds(off, CHUNK), rows(k)], y[pl.ds(INNER + off, CHUNK), rows(k)])
                base = (2 + 2 * n) * outer + k
                put(k, off, times(value, (col(base, off), col(base + outer, off))))

        chunks(INNER, middle)
        z[...] = triple(dft[2], dft[3], xh[...], xl[...])

        def last(off, write=write):
            values = []
            for k in range(outer):
                value = (z[pl.ds(off, CHUNK), rows(k)], z[pl.ds(INNER + off, CHUNK), rows(k)])
                if k:
                    value = times(value, (col(k, off), -col(outer + k, off)))
                values.append(value)
            for a, value in enumerate(small_fft(values, 1)):
                write(a, off, value)

        chunks(INNER, last)


def along_cols(read, writes, dft, table, xh, xl, y, z):
    outer = table.shape[0] // (2 * (1 + len(writes)))
    height = xh.shape[0] // outer
    row = lambda part: table[part : part + 1, :]

    def put(k, off, value):
        for at, v in ((0, value[0]), (INNER, value[1])):
            spot = (pl.ds(k * height + off, CHUNK), pl.ds(at, INNER))
            xh[spot], xl[spot] = split(v)

    def get(ref, k, off):
        return tuple(ref[pl.ds(k * height + off, CHUNK), pl.ds(at, INNER)] for at in (0, INNER))

    def first(off):
        for k, value in enumerate(small_fft([read(b, off) for b in range(outer)], -1)):
            if k:
                value = times(value, (row(k), row(outer + k)))
            put(k, off, value)

    chunks(height, first)
    y[...] = triple(xh[...], xl[...], dft[2], dft[3])
    for n, write in enumerate(writes):

        def middle(off, n=n):
            for k in range(outer):
                base = (2 + 2 * n) * outer + k
                put(k, off, times(get(y, k, off), (row(base), row(base + outer))))

        chunks(height, middle)
        z[...] = triple(xh[...], xl[...], dft[0], dft[1])

        def last(off, write=write):
            values = []
            for k in range(outer):
                value = get(z, k, off)
                if k:
                    value = times(value, (row(k), -row(outer + k)))
                values.append(value)
            for b, value in enumerate(small_fft(values, 1)):
                write(b, off, value)

        chunks(height, last)


class Plan:
    def __init__(self, rows_here, cols_here, wind, cross):
        self.wind, self.cross = wind, cross
        self.devices = wind * cross
        self.rows_here, self.cols_here = rows_here, cols_here
        self.height = rows_here // cross
        self.width = cols_here // wind
        self.rows, self.cols = rows_here * wind, cols_here * cross

    def slot(self, block):
        return (block % self.wind) * self.cross + block // self.wind

    def home_a(self, ref, a, off):
        n = a * INNER
        src, at = n // self.rows_here, n % self.rows_here
        return tuple(ref[src, p, pl.ds(at + off, CHUNK), :] for p in (0, 1))

    def spot_a(self, a, off):
        per = INNER // self.height
        return a * per + off // self.height, lax.rem(off, self.height)

    def flip_a(self, ref, a, off):
        s, at = self.spot_a(a, off)
        at = pl.multiple_of(at, CHUNK)
        return tuple(ref[s, pl.ds(p * self.height + at, CHUNK), :] for p in (0, 1))

    def send_a(self, ref, a, off, value):
        s, at = self.spot_a(a, off)
        at = pl.multiple_of(at, CHUNK)
        for p in (0, 1):
            ref[s, pl.ds(p * self.height + at, CHUNK), :] = value[p]

    def home_b(self, ref, b, off):
        per = self.cols_here // INNER
        return tuple(ref[b // per, pl.ds(p * self.height + off, CHUNK), pl.ds((b % per) * INNER, INNER)] for p in (0, 1))

    def flip_b(self, ref, b, off):
        return tuple(ref[self.slot(b), pl.ds(p * self.height + off, CHUNK), :] for p in (0, 1))

    def send_b(self, ref, b, off, value):
        for p in (0, 1):
            ref[self.slot(b), pl.ds(p * self.height + off, CHUNK), :] = value[p]

    def back_b(self, ref, b, off, value):
        per = self.cols_here // INNER
        for p in (0, 1):
            ref[b // per, pl.ds(p * self.height + off, CHUNK), pl.ds((b % per) * INNER, INNER)] = value[p]

    @property
    def sent(self):
        return jax.ShapeDtypeStruct((self.devices, 2 * self.height, self.width), F32)

    def work_a(self):
        wide = (self.rows // INNER) * self.width
        return [
            pltpu.VMEM((2 * INNER, wide), BF16),
            pltpu.VMEM((2 * INNER, wide), BF16),
            pltpu.VMEM((2 * INNER, wide), F32),
            pltpu.VMEM((2 * INNER, wide), F32),
        ]

    def work_b(self):
        tall = (self.cols // INNER) * self.height
        return [
            pltpu.VMEM((tall, 2 * INNER), BF16),
            pltpu.VMEM((tall, 2 * INNER), BF16),
            pltpu.VMEM((tall, 2 * INNER), F32),
            pltpu.VMEM((tall, 2 * INNER), F32),
        ]


def call(body, outs, scratch, specs=None, name=None):
    def run(*args):
        in_specs = [SCALAR if a.dtype == jnp.int32 else WHOLE for a in args]
        return pl.pallas_call(
            body,
            out_shape=outs,
            in_specs=in_specs,
            out_specs=[WHOLE] * len(outs),
            scratch_shapes=scratch,
            name=name,
        )(*args)

    return run


def rows_send(plan, read_field, dft, table, field):
    def body(dft, table, field, out, *work):
        along_rows(functools.partial(read_field, field), [functools.partial(plan.send_a, out)], dft, table, *work)

    return call(body, [plan.sent], plan.work_a(), name="rows_send")(dft, table, field)[0]


def cols_send(plan, read_field, back, dft, table, field):
    out = jax.ShapeDtypeStruct((plan.cross, 2 * plan.height, plan.cols_here), F32) if back else plan.sent

    def body(dft, table, field, out, *work):
        put = plan.back_b if back else plan.send_b
        along_cols(functools.partial(read_field, field), [functools.partial(put, out)], dft, table, *work)

    return call(body, [out], plan.work_b(), name="cols_send")(dft, table, field)[0]


def cols_heat(plan, layer, dft, table, received, home):
    blocks = plan.cols // INNER
    h = plan.height
    per = plan.cols_here // INNER

    def full(dft, table, received, home, part, totals, first, last, xh, xl, y, z, dep, dh, dl):
        def write(b, off, value):
            alpha = home[b // per, 3 * h + layer : 3 * h + layer + 1, pl.ds((b % per) * INNER, INNER)]
            deposit = alpha * (value[0] * value[0] + value[1] * value[1])
            spot = (pl.ds(off, CHUNK), pl.ds(b * INNER, INNER))
            dep[spot] = deposit
            dh[spot], dl[spot] = split(deposit)

        along_cols(functools.partial(plan.flip_b, received), [write], dft, table, xh, xl, y, z)
        ones = lower_ones(h)
        dot = functools.partial(jnp.dot, preferred_element_type=F32)
        part[...] = dot(ones, dh[...]) + dot(ones, dl[...])
        for b in range(blocks):
            lanes = slice(b * INNER, (b + 1) * INNER)
            at = (b % per) * INNER
            first[b, 0:8, :] = dep[0:8, lanes]
            last[b, 0:8, :] = dep[h - 8 : h, lanes]
            first[b, 8:16, :] = home[b // per, 2 * h : 2 * h + 8, at : at + INNER]
            last[b, 8:16, :] = home[b // per, 3 * h - 8 : 3 * h, at : at + INNER]
            total = part[h - 1 : h, lanes]
            for d in range(plan.devices):
                totals[d, b : b + 1, :] = total

    edge = jax.ShapeDtypeStruct((blocks, 16, INNER), F32)
    outs = [
        jax.ShapeDtypeStruct((h, plan.cols), F32),
        jax.ShapeDtypeStruct((plan.devices, blocks, INNER), F32),
        edge,
        edge,
    ]
    scratch = plan.work_b() + [pltpu.VMEM((h, plan.cols), F32), pltpu.VMEM((h, plan.cols), BF16), pltpu.VMEM((h, plan.cols), BF16)]
    return call(full, outs, scratch, name="cols_heat")(dft, table, received, home)


def conducted(mid, up, down, left, right, k_mid, k_up, k_down, k_left, k_right):
    flux = (k_mid + k_up) * (up - mid) + (k_mid + k_down) * (down - mid)
    flux = flux + (k_mid + k_left) * (left - mid) + (k_mid + k_right) * (right - mid)
    return mid + (0.5 * conduct_rate) * flux


def cols_screen(plan, read_field, dft, table, field, home, part, totals, above, below, me):
    blocks = plan.cols // INNER
    h = plan.height
    per = plan.cols_here // INNER
    PAD = 16

    def body(dft, table, field, home, part, totals, above, below, me, out, xh, xl, y, z, h0, h1, kx):
        place = me[0]
        zeros = jnp.zeros((PAD, plan.cols), F32)
        for ref in (h0, kx, h1):
            ref[0:PAD, :] = zeros
            ref[h + PAD : h + 2 * PAD, :] = zeros
        upstream = jnp.zeros((blocks, INNER), F32)
        for d in range(plan.devices):
            upstream = upstream + jnp.where(d < place, totals[d], 0.0)
        inner_low = jnp.where(place < plan.devices - 1, 1.0, 0.0)
        for b in range(blocks):
            lanes = slice(b * INNER, (b + 1) * INNER)
            at = (b % per) * INNER
            base = upstream[b : b + 1, :]
            h0[PAD : PAD + h, lanes] = part[:, lanes] + base
            value = base
            for j in range(SMOOTH):
                h0[PAD - 1 - j : PAD - j, lanes] = value
                value = value - above[b, 7 - j : 8 - j, :]
            value = base + part[h - 1 : h, lanes]
            for j in range(SMOOTH):
                value = value + below[b, j : j + 1, :]
                h0[PAD + h + j : PAD + h + j + 1, lanes] = value * inner_low
            kx[PAD - 8 : PAD, lanes] = above[b, 8:16, :]
            kx[PAD : PAD + h, lanes] = home[b // per, 2 * h : 3 * h, at : at + INNER]
            kx[PAD + h : PAD + h + 8, lanes] = below[b, 8:16, :]
        lane = lax.broadcasted_iota(jnp.int32, (8, plan.cols), 1)
        row = lax.broadcasted_iota(jnp.int32, (8, plan.cols), 0)

        def sides(x):
            left = jnp.where(lane == 0, 0.0, pltpu.roll(x, 1, 1))
            right = jnp.where(lane == plan.cols - 1, 0.0, pltpu.roll(x, plan.cols - 1, 1))
            return left, right

        def smooth(src, dst, low, count, masked):
            def step(i, carry):
                base = pl.multiple_of(low + i * 8, 8)
                value = src[pl.ds(base - 8, 24), :]
                kap = kx[pl.ds(base - 8, 24), :]
                mid, k_mid = value[8:16], kap[8:16]
                left, right = sides(mid)
                k_left, k_right = sides(k_mid)
                new = conducted(
                    mid, value[7:15], value[9:17], left, right, k_mid, kap[7:15], kap[9:17], k_left, k_right
                )
                if masked:
                    n = row + base
                    bad = ((n < PAD) & (place == 0)) | ((n >= PAD + h) & (place == plan.devices - 1))
                    new = jnp.where(bad, 0.0, new)
                dst[pl.ds(base, 8), :] = new
                return carry

            lax.fori_loop(0, count, step, 0)

        refs = [h0, h1]
        for n in range(SMOOTH):
            if n < SMOOTH - 1:
                smooth(refs[n % 2], refs[(n + 1) % 2], PAD - 8, (h + 16) // 8, True)
            else:
                smooth(refs[n % 2], refs[(n + 1) % 2], PAD, h // 8, False)
        final = refs[SMOOTH % 2]

        def read(b, off):
            screen = -final[pl.ds(PAD + off, CHUNK), pl.ds(b * INNER, INNER)]
            return screened(read_field(field, b, off), screen)

        along_cols(read, [functools.partial(plan.send_b, out)], dft, table, xh, xl, y, z)

    tall = pltpu.VMEM((h + 2 * PAD, plan.cols), F32)
    return call(body, [plan.sent], plan.work_b() + [tall] * 3, name="cols_screen")(
        dft, table, field, home, part, totals, above, below, me
    )[0]


def rows_heat(plan, dft, table, received, alpha, home):
    width = plan.width

    def body(dft, table, received, alpha, home, heat, edge_left, edge_right, xh, xl, y, z, dep):
        def write(a, off, value):
            deposit = alpha[...] * (value[0] * value[0] + value[1] * value[1])
            rows = pl.ds(a * INNER + off, CHUNK)
            dep[rows, 0:width], dep[rows, width : 2 * width] = split(deposit)

        along_rows(functools.partial(plan.flip_a, received), [write], dft, table, xh, xl, y, z)
        tile = 2 * INNER
        ones = lower_ones(tile)
        carry = jnp.zeros((1, width), F32)
        for g in range(plan.rows // tile):
            both = jnp.dot(ones, dep[g * tile : (g + 1) * tile, :], preferred_element_type=F32)
            value = both[:, :width] + both[:, width:] + carry
            heat[g * tile : (g + 1) * tile, :] = value
            carry = value[tile - 1 : tile, :]
        lane = lax.broadcasted_iota(jnp.int32, (INNER, width), 1)
        for g in range(plan.rows // INNER):
            n = g * INNER
            src, at = n // plan.rows_here, n % plan.rows_here
            value = heat[n : n + INNER, :]
            kap = home[src, 2, at : at + INNER, :]
            mixed = jnp.where((lane >= 8) & (lane < 64), pltpu.roll(kap, 8, 1), value)
            mixed = jnp.where((lane >= 64) & (lane < width - 8), pltpu.roll(kap, width - 8, 1), mixed)
            turned = mixed.T
            edge_left[:, n : n + INNER] = turned[0:16, :]
            edge_right[:, n : n + INNER] = turned[width - 16 : width, :]

    edge = jax.ShapeDtypeStruct((16, plan.rows), F32)
    outs = [jax.ShapeDtypeStruct((plan.rows, width), F32), edge, edge]
    scratch = plan.work_a() + [pltpu.VMEM((plan.rows, 2 * width), BF16)]
    return call(body, outs, scratch, name="rows_heat")(dft, table, received, alpha, home)


def rows_screen(plan, read_field, sets, keep, dft, table, field, heat, home, from_left, from_right, me):
    width = plan.width
    PAD = 8
    step_rows = 32

    def body(dft, table, field, heat, home, from_left, from_right, me, *refs):
        outs, rest = refs[:sets], refs[sets:]
        screen, rest = (rest[0], rest[1:]) if keep else (rest[-1], rest[:-1])
        xh, xl, y, z, h0, h1, kx = rest
        place = me[0]
        zeros = jnp.zeros((PAD, 2 * width), F32)
        for ref in (h0, h1, kx):
            ref[0:PAD, :] = zeros
            ref[plan.rows + PAD : plan.rows + 2 * PAD, :] = zeros
        lane = lax.broadcasted_iota(jnp.int32, (INNER, width), 1)
        for g in range(plan.rows // INNER):
            n = g * INNER
            src, at = n // plan.rows_here, n % plan.rows_here
            spot = slice(PAD + n, PAD + n + INNER)
            h0[spot, 0:width] = heat[n : n + INNER, :]
            kx[spot, 0:width] = home[src, 2, at : at + INNER, :]
            turned = jnp.concatenate(
                [from_right[:, n : n + INNER], jnp.zeros((width - 32, INNER), F32), from_left[:, n : n + INNER]], axis=0
            ).T
            h0[spot, width : 2 * width] = jnp.where((lane < 8) | (lane >= width - 8), turned, 0.0)
            kap = jnp.where(lane < 8, pltpu.roll(turned, width - 8, 1), 0.0)
            kx[spot, width : 2 * width] = jnp.where(lane >= width - 8, pltpu.roll(turned, 8, 1), kap)
        wide = lax.broadcasted_iota(jnp.int32, (step_rows, 2 * width), 1)
        bad = (wide >= width) & (wide < width + width // 2) & (place == plan.devices - 1)
        bad = bad | ((wide >= width + width // 2) & (place == 0))

        def smooth(src, dst):
            def step(i, carry):
                base = pl.multiple_of(i * step_rows, step_rows)
                value = src[pl.ds(base, step_rows + 16), :]
                kap = kx[pl.ds(base, step_rows + 16), :]
                mid, k_mid = value[8:-8], kap[8:-8]
                new = conducted(
                    mid, value[7:-9], value[9:-7], pltpu.roll(mid, 1, 1), pltpu.roll(mid, 2 * width - 1, 1),
                    k_mid, kap[7:-9], kap[9:-7], pltpu.roll(k_mid, 1, 1), pltpu.roll(k_mid, 2 * width - 1, 1),
                )
                dst(base, jnp.where(bad, 0.0, new))
                return carry

            lax.fori_loop(0, plan.rows // step_rows, step, 0)

        def into(ref):
            def put(base, value):
                ref[pl.ds(base + PAD, step_rows), :] = value

            return put

        def into_screen(base, value):
            screen[pl.ds(base, step_rows), :] = -value[:, :width]

        refs = [h0, h1]
        for n in range(SMOOTH):
            smooth(refs[n % 2], into(refs[(n + 1) % 2]) if n < SMOOTH - 1 else into_screen)

        def read(a, off):
            return screened(read_field(field, a, off), screen[pl.ds(a * INNER + off, CHUNK), :])

        along_rows(read, [functools.partial(plan.send_a, out) for out in outs], dft, table, xh, xl, y, z)

    outs = [plan.sent] * sets
    flat = (plan.rows, width)
    tall = pltpu.VMEM((plan.rows + 2 * PAD, 2 * width), F32)
    scratch = plan.work_a() + [tall] * 3
    if keep:
        outs = outs + [jax.ShapeDtypeStruct(flat, F32)]
    else:
        scratch = scratch + [pltpu.VMEM(flat, F32)]
    return call(body, outs, scratch, name="rows_screen")(dft, table, field, heat, home, from_left, from_right, me)


def next_prev(value_up, value_down, axes, order):
    up = list(zip(order[:-1], order[1:]))
    down = [(j, i) for i, j in up]
    return lax.ppermute(value_up, axes, up), lax.ppermute(value_down, axes, down)


def extended(shard, sides, width):
    for axis, dim in sides:
        size, length = (lax.axis_size(axis), shard.shape[dim])
        up = [(i, (i + 1) % size) for i in range(size - 1)]
        down = [(j, i) for i, j in up]
        last = lax.slice_in_dim(shard, length - width, length, axis=dim)
        initial = lax.slice_in_dim(shard, 0, width, axis=dim)
        before = lax.ppermute(last, axis, up)
        after = lax.ppermute(initial, axis, down)
        shard = jnp.concatenate([before, shard, after], axis=dim)
    return shard


def carried_in(part, axis, combine, identity):
    place = lax.axis_index(axis)
    gathered = lax.all_gather(part, axis)
    state = jnp.zeros_like(part) + jnp.asarray(identity, part.dtype)

    def one(turn, state):
        return combine(state, lax.dynamic_index_in_dim(gathered, turn, 0, False))

    return lax.fori_loop(0, place, one, state)


def signed_freq(indices, length):
    shifted = jnp.where(indices < length // 2, indices, indices - length)
    return shifted.astype(jnp.float32) / length


def trig_table(first_ids, second_ids, length, sign_value):
    product = first_ids * second_ids % length
    phase_angle = product.astype(jnp.float32) * (sign_value * 2.0 * math.pi / length)
    return (jnp.cos(phase_angle), jnp.sin(phase_angle))


def complex_product(formula, real_part, imag_part, cosine, sine):
    highest = lax.Precision.HIGHEST
    out_real = jnp.einsum(formula, real_part, cosine, precision=highest) - jnp.einsum(
        formula, imag_part, sine, precision=highest
    )
    out_imag = jnp.einsum(formula, real_part, sine, precision=highest) + jnp.einsum(
        formula, imag_part, cosine, precision=highest
    )
    return (out_real, out_imag)


def transform(stacked, axis_dim, inverse):
    full_shape = stacked.shape
    length = full_shape[axis_dim]
    inner_len = math.gcd(length, 128)
    outer_len = length // inner_len
    leading = full_shape[1] if axis_dim == 2 else 1
    trailing = full_shape[2] if axis_dim == 1 else 1
    blocks = stacked.reshape(2, leading, outer_len, inner_len, trailing)
    sign_value = 1.0 if inverse else -1.0
    outer_ids = jnp.arange(outer_len, dtype=jnp.int32)
    inner_ids = jnp.arange(inner_len, dtype=jnp.int32)
    cos_outer, sin_outer = trig_table(outer_ids[:, None], outer_ids[None, :], outer_len, sign_value)
    first_real, first_imag = complex_product(
        "pabq,ak->pkbq", blocks[0], blocks[1], cos_outer, sin_outer
    )
    cos_twist, sin_twist = trig_table(outer_ids[:, None], inner_ids[None, :], length, sign_value)
    cos_twist = cos_twist[None, :, :, None]
    sin_twist = sin_twist[None, :, :, None]
    twist_real = first_real * cos_twist - first_imag * sin_twist
    twist_imag = first_real * sin_twist + first_imag * cos_twist
    cos_inner, sin_inner = trig_table(inner_ids[:, None], inner_ids[None, :], inner_len, sign_value)
    second_real, second_imag = complex_product(
        "pkbq,bm->pkmq", twist_real, twist_imag, cos_inner, sin_inner
    )
    result = jnp.stack([second_real, second_imag]).transpose(0, 1, 3, 2, 4).reshape(full_shape)
    if inverse:
        result = result * (1.0 / length)
    return result


def apply_phase(stacked, phase_angle):
    cosine = jnp.cos(phase_angle)
    sine = jnp.sin(phase_angle)
    return jnp.stack(
        [stacked[0] * cosine - stacked[1] * sine, stacked[0] * sine + stacked[1] * cosine]
    )


def along_joint(stacked, phase_rate, row_freq, col_freq):
    cross_count = lax.axis_size("cross")
    stacked = lax.all_to_all(stacked, ("wind", "cross"), split_axis=2, concat_axis=1, tiled=True)
    stacked = transform(stacked, 1, False)
    col_width = stacked.shape[2]
    joint_block = lax.axis_index("wind") * cross_count + lax.axis_index("cross")
    cols_held = lax.dynamic_slice_in_dim(col_freq, joint_block * col_width, col_width)
    phase_angle = -phase_rate * (
        row_freq[:, None] * row_freq[:, None] + cols_held[None, :] * cols_held[None, :]
    )
    stacked = apply_phase(stacked, phase_angle)
    stacked = transform(stacked, 1, True)
    return lax.all_to_all(stacked, ("wind", "cross"), split_axis=1, concat_axis=2, tiled=True)


def propagate_slab(slab_pair, share_step):
    rows_total = slab_pair.shape[1] * lax.axis_size("wind") * lax.axis_size("cross")
    cols_total = slab_pair.shape[2]
    phase_rate = share_step * diffraction
    row_freq = signed_freq(jnp.arange(rows_total, dtype=jnp.int32), rows_total)
    col_freq = signed_freq(jnp.arange(cols_total, dtype=jnp.int32), cols_total)
    stacked = transform(slab_pair, 2, False)
    stacked = along_joint(stacked, phase_rate, row_freq, col_freq)
    return transform(stacked, 2, True)


def conduct_core(padded, kappa_pad):
    height = padded.shape[0] - 2
    breadth = padded.shape[1] - 2
    center = padded[1:-1, 1:-1]
    kappa_mid = kappa_pad[1:-1, 1:-1]
    flux_sum = jnp.zeros_like(center)
    for offset_row, offset_col in ((0, 1), (2, 1), (1, 0), (1, 2)):
        neighbour = padded[offset_row : offset_row + height, offset_col : offset_col + breadth]
        kappa_side = kappa_pad[offset_row : offset_row + height, offset_col : offset_col + breadth]
        flux_sum = flux_sum + 0.5 * (kappa_mid + kappa_side) * (neighbour - center)
    return center + conduct_rate * flux_sum


def add_terms(earlier, later_term):
    return earlier + later_term


def layer_absorption(index_row, table_row, level_ids):
    one_hot = (index_row[:, None] == level_ids[None, :]).astype(jnp.float32)
    return jnp.sum(one_hot * table_row[None, :], axis=1)


def wide_device(field_real, field_imag, absorb_index, absorb_table, zone_map, zone_conductivity):
    rows_here, cols_here = field_real.shape
    conductivity = jnp.zeros((rows_here, cols_here), jnp.float32)
    for zone_no in range(zone_conductivity.shape[0]):
        conductivity = jnp.where(zone_map == zone_no, zone_conductivity[zone_no], conductivity)
    level_ids = jnp.arange(absorb_table.shape[1], dtype=jnp.int32)
    combined = lax.all_to_all(
        jnp.stack([field_real, field_imag, conductivity]),
        "cross",
        split_axis=1,
        concat_axis=2,
        tiled=True,
    )
    slab_pair = combined[:2]
    kappa_rows = extended(combined[2], ((("wind", "cross"), 0),), 1)
    kappa_pad = jnp.pad(kappa_rows, ((0, 0), (1, 1)))
    index_full = lax.all_gather(absorb_index, "cross", axis=1, tiled=True)
    slab_rows = slab_pair.shape[1]
    rows_total = slab_rows * lax.axis_size("wind") * lax.axis_size("cross")
    slab_ids = jnp.arange(slab_rows, dtype=jnp.int32)
    lower_slab = (slab_ids[:, None] >= slab_ids[None, :]).astype(jnp.float32)
    screen_phase = jnp.zeros((slab_rows, slab_pair.shape[2]), jnp.float32)
    for layer_no in range(LAYERS):
        absorption = layer_absorption(index_full[layer_no], absorb_table[layer_no], level_ids)
        screen_phase = jnp.zeros((slab_rows, slab_pair.shape[2]), jnp.float32)
        for round_no in range(ITERS):
            middle = propagate_slab(apply_phase(slab_pair, screen_phase), 0.5)
            intensity = middle[0] * middle[0] + middle[1] * middle[1]
            deposit = absorption[None, :] * intensity * (1.0 / rows_total)
            partial_heat = jnp.dot(lower_slab, deposit, precision=lax.Precision.HIGHEST)
            totals = partial_heat[-1]
            upstream = carried_in(totals, ("wind", "cross"), add_terms, jnp.zeros_like(totals))
            heat_field = partial_heat + upstream[None, :]
            for smooth_no in range(SMOOTH):
                padded = extended(heat_field, ((("wind", "cross"), 0),), 1)
                padded = jnp.pad(padded, ((0, 0), (1, 1)))
                heat_field = conduct_core(padded, kappa_pad)
            screen_phase = -heat_field
        slab_pair = propagate_slab(apply_phase(slab_pair, screen_phase), 1.0)
    returned = lax.all_to_all(
        jnp.stack([slab_pair[0], slab_pair[1], screen_phase]),
        "cross",
        split_axis=2,
        concat_axis=1,
        tiled=True,
    )
    return (returned[0], returned[1], returned[2])


def on_device(field_real, field_imag, absorb_index, absorb_table, zone_map, zone_conductivity):
    plan = Plan(*field_real.shape, lax.axis_size("wind"), lax.axis_size("cross"))
    fits = plan.width == INNER and INNER % plan.height == 0 and plan.height % CHUNK == 0
    if not fits or plan.rows_here % INNER or plan.rows % (2 * INNER):
        return wide_device(field_real, field_imag, absorb_index, absorb_table, zone_map, zone_conductivity)
    wind, cross = plan.wind, plan.cross
    w, c = lax.axis_index("wind"), lax.axis_index("cross")
    row_place = jnp.reshape(w * cross + c, (1,)).astype(jnp.int32)
    col_place = jnp.reshape(c * wind + w, (1,)).astype(jnp.int32)
    grid_axes = ("wind", "cross")

    conductivity = jnp.zeros(field_real.shape, F32)
    for zone_no in range(zone_conductivity.shape[0]):
        conductivity = jnp.where(zone_map == zone_no, zone_conductivity[zone_no], conductivity)
    alpha = jnp.zeros(absorb_index.shape, F32)
    for level in range(absorb_table.shape[1]):
        alpha = jnp.where(absorb_index == level, absorb_table[:, level : level + 1], alpha)
    alpha = alpha * (1.0 / plan.rows)
    alpha_a = lax.dynamic_slice_in_dim(alpha, w * plan.width, plan.width, axis=1)

    stacked = jnp.stack([field_real, field_imag, conductivity])
    to_a = stacked.reshape(3, plan.rows_here, wind, plan.width).transpose(2, 0, 1, 3)
    home_a = lax.all_to_all(to_a, "wind", split_axis=0, concat_axis=0, tiled=True)
    to_b = [s.reshape(cross, plan.height, plan.cols_here) for s in (field_real, field_imag, conductivity)]
    alpha_rows = jnp.pad(alpha, ((0, -LAYERS % 8), (0, 0)))
    to_b.append(jnp.broadcast_to(alpha_rows[None], (cross,) + alpha_rows.shape))
    home_b = lax.all_to_all(jnp.concatenate(to_b, axis=1), "cross", split_axis=0, concat_axis=0, tiled=True)

    dft = jnp.asarray(dft_matrices())
    tab_a = lambda *shares: jnp.asarray(row_table(plan.rows, shares))
    tab_b = lambda *shares: jnp.asarray(chirp_columns(plan.cols, shares))

    def flip(x):
        return lax.all_to_all(x, grid_axes, split_axis=0, concat_axis=0, tiled=True)

    def heat_b(layer, share, received):
        part, totals, first, last = cols_heat(plan, layer, dft, tab_b(share), received, home_b)
        totals = lax.all_to_all(totals, grid_axes, split_axis=0, concat_axis=0, tiled=True)
        above, below = next_prev(last, first, grid_axes, list(range(plan.devices)))
        return part, totals, above, below, row_place

    def heat_a(layer, share, received):
        heat, left, right = rows_heat(plan, dft, tab_a(share), received, alpha_a[layer : layer + 1], home_a)
        from_left, from_right = next_prev(right, left, grid_axes, [plan.slot(i) for i in range(plan.devices)])
        return heat, home_a, from_left, from_right, col_place

    sent = rows_send(plan, plan.home_a, dft, tab_a(0.5), home_a)
    parts = heat_b(0, 0.5, flip(sent))
    sent = cols_screen(plan, plan.home_b, dft, tab_b(0.5), home_b, home_b, *parts)
    parts = heat_a(0, 0.5, flip(sent))
    sent_middle, sent_field = rows_screen(plan, plan.home_a, 2, False, dft, tab_a(1.5, 1.0), home_a, *parts)
    middle = flip(sent_middle)
    field_b = cols_send(plan, plan.flip_b, False, dft, tab_b(1.0), flip(sent_field))
    field_a = flip(field_b)
    parts = heat_b(1, 1.5, middle)
    sent = cols_screen(plan, plan.flip_b, dft, tab_b(0.5), field_b, home_b, *parts)
    parts = heat_a(1, 0.5, flip(sent))
    sent, screen = rows_screen(plan, plan.flip_a, 1, True, dft, tab_a(1.0), field_a, *parts)
    back = cols_send(plan, plan.flip_b, True, dft, tab_b(1.0), flip(sent))
    back = lax.all_to_all(back, "cross", split_axis=0, concat_axis=0, tiled=True)
    out_real = back[:, : plan.height].reshape(field_real.shape)
    out_imag = back[:, plan.height :].reshape(field_real.shape)
    screen = screen.reshape(wind, plan.rows_here, plan.width)
    screen = lax.all_to_all(screen, "wind", split_axis=0, concat_axis=0, tiled=True)
    screen = screen.transpose(1, 0, 2).reshape(field_real.shape)
    return (out_real, out_imag, screen)


def solution(mesh):
    in_specs = (
        P(("beams", "wind"), "cross"),
        P(("beams", "wind"), "cross"),
        P(None, "cross"),
        P(),
        P("wind", "cross"),
        P(),
    )
    out_specs = (
        P(("beams", "wind"), "cross"),
        P(("beams", "wind"), "cross"),
        P(("beams", "wind"), "cross"),
    )
    return jax.shard_map(
        on_device, mesh=mesh, in_specs=in_specs, out_specs=out_specs, check_vma=False
    )
```

```python
import functools
import math

import jax
import jax.numpy as jnp
import numpy as np
from jax import lax
from jax.experimental import pallas as pl
from jax.experimental.pallas import tpu as pltpu
from jax.sharding import PartitionSpec as P

LAYERS = 2
ITERS = 2
SMOOTH = 2
INNER = 128
CHUNK = 16

diffraction = 2000.0
conduct_rate = 0.24

F32 = jnp.float32
BF16 = jnp.bfloat16
WHOLE = pl.BlockSpec(memory_space=pltpu.VMEM)
SCALAR = pl.BlockSpec(memory_space=pltpu.SMEM)


def split_np(values):
    high = values.astype(np.float32).astype(jnp.bfloat16)
    low = (values - high.astype(np.float64)).astype(np.float32).astype(jnp.bfloat16)
    return high, low


def dft_matrices():
    ids = np.arange(INNER)
    angle = 2.0 * np.pi * (np.outer(ids, ids) % INNER) / INNER
    cosine, sine = np.cos(angle), np.sin(angle)
    left = np.block([[cosine, sine], [-sine, cosine]])
    return np.stack([*split_np(left), *split_np(left.T)])


def chirp_columns(length, shares):
    outer = length // INNER
    k = np.arange(outer)[:, None]
    m = np.arange(INNER)[None, :]
    twist = -2.0 * np.pi * ((k * m) % length) / length
    tables = [np.cos(twist), np.sin(twist)]
    p = k + outer * m
    freq = np.where(p < length // 2, p, p - length) / length
    for share in shares:
        angle = -share * diffraction * freq * freq
        tables += [np.cos(angle) / length, np.sin(angle) / length]
    return np.concatenate(tables, axis=0).astype(np.float32)


def row_table(length, shares):
    cols = chirp_columns(length, shares).T
    return np.pad(cols, ((0, 0), (0, -cols.shape[1] % 128)))


def split(x):
    high = x.astype(BF16)
    return high, (x - high.astype(F32)).astype(BF16)


def times(a, b):
    return (a[0] * b[0] - a[1] * b[1], a[0] * b[1] + a[1] * b[0])


def small_fft(points, sign):
    count = len(points)
    if count == 1:
        return points
    even = small_fft(points[0::2], sign)
    odd = small_fft(points[1::2], sign)
    half = count // 2
    out = [None] * count
    for k in range(half):
        re, im = odd[k]
        if k == 0:
            turn = (re, im)
        elif 4 * k == count:
            turn = (-im, re) if sign > 0 else (im, -re)
        elif 8 * k == count:
            root = math.sqrt(0.5)
            turn = (root * (re - im), root * (im + re)) if sign > 0 else (root * (re + im), root * (im - re))
        elif 8 * k == 3 * count:
            root = math.sqrt(0.5)
            turn = (-root * (re + im), root * (re - im)) if sign > 0 else (root * (im - re), -root * (re + im))
        else:
            c = math.cos(2.0 * math.pi * k / count)
            s = sign * math.sin(2.0 * math.pi * k / count)
            turn = (c * re - s * im, s * re + c * im)
        out[k] = (even[k][0] + turn[0], even[k][1] + turn[1])
        out[k + half] = (even[k][0] - turn[0], even[k][1] - turn[1])
    return out


def cos_sin(x):
    turns = jnp.floor(x * (2.0 / math.pi) + 0.5)
    r = ((x - turns * 1.5703125) - turns * 4.837512969970703125e-4) - turns * 7.549789954891882e-8
    quad = turns.astype(jnp.int32)
    z = r * r
    s = r + r * z * (-1.6666654611e-1 + z * (8.3321608736e-3 - z * 1.9515295891e-4))
    c = 1.0 - 0.5 * z + z * z * (4.166664568298827e-2 + z * (-1.388731625493765e-3 + z * 2.443315711809948e-5))
    odd = (quad & 1) == 1
    sin_x = jnp.where(odd, c, s)
    cos_x = jnp.where(odd, s, c)
    sin_x = jnp.where((quad & 2) == 2, -sin_x, sin_x)
    cos_x = jnp.where(((quad + 1) & 2) == 2, -cos_x, cos_x)
    return cos_x, sin_x


def screened(value, screen):
    return times(value, cos_sin(screen))


def triple(a_high, a_low, b_high, b_low):
    dot = functools.partial(jnp.dot, preferred_element_type=F32)
    return dot(a_high, b_high) + dot(a_high, b_low) + dot(a_low, b_high)


def lower_ones(size):
    r = lax.broadcasted_iota(jnp.int32, (size, size), 0)
    c = lax.broadcasted_iota(jnp.int32, (size, size), 1)
    return jnp.where(r >= c, 1.0, 0.0).astype(BF16)


def chunks(count, body):
    def step(i, carry):
        body(pl.multiple_of(i * CHUNK, CHUNK))
        return carry

    lax.fori_loop(0, count // CHUNK, step, 0)


def along_rows(read, writes, dft, table, xh, xl, y, z):
    outer = xh.shape[1] // 128
    rows = lambda k: pl.ds(k * 128, 128)
    col = lambda part, off: table[pl.ds(off, CHUNK), part : part + 1]

    def put(k, off, value):
        for at, v in ((0, value[0]), (INNER, value[1])):
            xh[pl.ds(at + off, CHUNK), rows(k)], xl[pl.ds(at + off, CHUNK), rows(k)] = split(v)

    def first(off):
        for k, value in enumerate(small_fft([read(a, off) for a in range(outer)], -1)):
            if k:
                value = times(value, (col(k, off), col(outer + k, off)))
            put(k, off, value)

    chunks(INNER, first)
    y[...] = triple(dft[0], dft[1], xh[...], xl[...])
    for n, write in enumerate(writes):

        def middle(off, n=n):
            for k in range(outer):
                value = (y[pl.ds(off, CHUNK), rows(k)], y[pl.ds(INNER + off, CHUNK), rows(k)])
                base = (2 + 2 * n) * outer + k
                put(k, off, times(value, (col(base, off), col(base + outer, off))))

        chunks(INNER, middle)
        z[...] = triple(dft[2], dft[3], xh[...], xl[...])

        def last(off, write=write):
            values = []
            for k in range(outer):
                value = (z[pl.ds(off, CHUNK), rows(k)], z[pl.ds(INNER + off, CHUNK), rows(k)])
                if k:
                    value = times(value, (col(k, off), -col(outer + k, off)))
                values.append(value)
            for a, value in enumerate(small_fft(values, 1)):
                write(a, off, value)

        chunks(INNER, last)


def along_cols(main, read, writes, dft, table, xh, xl, y, z):
    outer = table.shape[0] // (2 * (1 + len(writes)))
    height = xh.shape[0] // outer

    def every(body):
        chunks(main, body)
        if height > main:
            body(main)

    row = lambda part: table[part : part + 1, :]

    def put(k, off, value):
        for at, v in ((0, value[0]), (INNER, value[1])):
            spot = (pl.ds(k * height + off, CHUNK), pl.ds(at, INNER))
            xh[spot], xl[spot] = split(v)

    def get(ref, k, off):
        return tuple(ref[pl.ds(k * height + off, CHUNK), pl.ds(at, INNER)] for at in (0, INNER))

    def first(off):
        for k, value in enumerate(small_fft([read(b, off) for b in range(outer)], -1)):
            if k:
                value = times(value, (row(k), row(outer + k)))
            put(k, off, value)

    every(first)
    y[...] = triple(xh[...], xl[...], dft[2], dft[3])
    for n, write in enumerate(writes):

        def middle(off, n=n):
            for k in range(outer):
                base = (2 + 2 * n) * outer + k
                put(k, off, times(get(y, k, off), (row(base), row(base + outer))))

        every(middle)
        z[...] = triple(xh[...], xl[...], dft[0], dft[1])

        def last(off, write=write):
            values = []
            for k in range(outer):
                value = get(z, k, off)
                if k:
                    value = times(value, (row(k), -row(outer + k)))
                values.append(value)
            for b, value in enumerate(small_fft(values, 1)):
                write(b, off, value)

        every(last)


class Plan:
    def __init__(self, rows_here, cols_here, wind, cross):
        self.wind, self.cross = wind, cross
        self.devices = wind * cross
        self.rows_here, self.cols_here = rows_here, cols_here
        self.height = rows_here // cross
        self.width = cols_here // wind
        self.rows, self.cols = rows_here * wind, cols_here * cross

    def local(self, w, c):
        return w + (c % 2) * (self.wind - 1 - 2 * w)

    def slot(self, block):
        c, i = block // self.wind, block % self.wind
        return self.local(i, c) * self.cross + c

    def home_a(self, ref, a, off):
        n = a * INNER
        src, at = n // self.rows_here, n % self.rows_here
        return tuple(ref[src, pl.ds(p * self.rows_here + at + off, CHUNK), :] for p in (0, 1))

    def spot_a(self, a, off):
        per = INNER // self.height
        return a * per + off // self.height, lax.rem(off, self.height)

    def flip_a(self, ref, a, off):
        s, at = self.spot_a(a, off)
        at = pl.multiple_of(at, CHUNK)
        return tuple(ref[s, pl.ds(p * self.height + at, CHUNK), :] for p in (0, 1))

    def send_a(self, ref, a, off, value):
        s, at = self.spot_a(a, off)
        at = pl.multiple_of(at, CHUNK)
        for p in (0, 1):
            ref[s, pl.ds(p * self.height + at, CHUNK), :] = value[p]

    def send_edges(self, ref):
        h = self.height
        for d in range(self.devices):
            for p in (0, 1):
                at = 2 * h + 4 * p
                before = ref[d - 1, p * h + h - 2 : p * h + h, :] if d else jnp.zeros((2, self.width), F32)
                after = ref[d + 1, p * h : p * h + 2, :] if d + 1 < self.devices else jnp.zeros((2, self.width), F32)
                ref[d, at : at + 2, :] = before
                ref[d, at + 2 : at + 4, :] = after

    def home_b(self, ref, b, off):
        per = self.cols_here // INNER
        return tuple(ref[b // per, pl.ds(p * self.height + off, CHUNK), pl.ds((b % per) * INNER, INNER)] for p in (0, 1))

    def wide_b(self, ref, b, off):
        if isinstance(off, int):
            extra = ref[self.slot(b), 2 * self.height : 2 * self.height + 8, :]
            turned = jnp.concatenate([extra[4:8], extra[0:4]], axis=0)
            return jnp.concatenate([extra, extra], axis=0), jnp.concatenate([turned, turned], axis=0)
        return self.flip_b(ref, b, off)

    def flip_b(self, ref, b, off):
        return tuple(ref[self.slot(b), pl.ds(p * self.height + off, CHUNK), :] for p in (0, 1))

    def send_b(self, ref, b, off, value):
        for p in (0, 1):
            ref[self.slot(b), pl.ds(p * self.height + off, CHUNK), :] = value[p]

    def back_b(self, ref, b, off, value):
        per = self.cols_here // INNER
        for p in (0, 1):
            ref[b // per, pl.ds(p * self.height + off, CHUNK), pl.ds((b % per) * INNER, INNER)] = value[p]

    @property
    def sent(self):
        return jax.ShapeDtypeStruct((self.devices, 2 * self.height, self.width), F32)

    def work_a(self):
        wide = (self.rows // INNER) * self.width
        return [
            pltpu.VMEM((2 * INNER, wide), BF16),
            pltpu.VMEM((2 * INNER, wide), BF16),
            pltpu.VMEM((2 * INNER, wide), F32),
            pltpu.VMEM((2 * INNER, wide), F32),
        ]

    @property
    def sent_wide(self):
        return jax.ShapeDtypeStruct((self.devices, 2 * self.height + 8, self.width), F32)

    def work_b(self, extra=0):
        tall = (self.cols // INNER) * (self.height + extra)
        return [
            pltpu.VMEM((tall, 2 * INNER), BF16),
            pltpu.VMEM((tall, 2 * INNER), BF16),
            pltpu.VMEM((tall, 2 * INNER), F32),
            pltpu.VMEM((tall, 2 * INNER), F32),
        ]


def call(body, outs, scratch, name, near=(), near_outs=(), far=()):
    def run(*args):
        specs = [SCALAR if a.size <= 8 else WHOLE for a in args]
        spaces = [pltpu.VMEM if i in near else pltpu.HBM if i in far else None for i in range(len(args))]
        args = [pltpu.with_memory_space_constraint(a, space) if space else a for a, space in zip(args, spaces)]
        return pl.pallas_call(
            body,
            out_shape=[pltpu.VMEM(o.shape, o.dtype) if i in near_outs else o for i, o in enumerate(outs)],
            in_specs=specs,
            out_specs=[WHOLE] * len(outs),
            scratch_shapes=scratch,
            name=name,
            compiler_params=pltpu.CompilerParams(vmem_limit_bytes=24 * 1024 * 1024),
        )(*args)

    return run


def prepare(plan, field_real, field_imag, zone_map, alpha, zone_conductivity, place):
    h = plan.height

    def body(real, imag, zones, alpha, levels, place, field_a, *refs):
        to_b, to_a, kappa = refs[: plan.cross], refs[plan.cross : -1], refs[-1]
        w, c = place[0], place[1]
        for n in range(plan.wind):
            lanes = pl.ds(pl.multiple_of(plan.local(n, c) * plan.width, plan.width), plan.width)
            field_a[n, 0 : plan.rows_here, :] = real[:, lanes]
            field_a[n, plan.rows_here : 2 * plan.rows_here, :] = imag[:, lanes]

        def step(off):
            ids = zones[pl.ds(off, CHUNK), :]
            value = jnp.zeros(ids.shape, F32)
            for n in range(levels.shape[0]):
                value = jnp.where(ids == n, levels[n], value)
            kappa[pl.ds(off, CHUNK), :] = value

        chunks(plan.rows_here, step)
        for s, out in enumerate(to_b):
            at = pl.multiple_of(lax.rem(c + s, plan.cross) * h, h)
            out[0:h, :] = real[pl.ds(at, h), :]
            out[h : 2 * h, :] = imag[pl.ds(at, h), :]
            out[2 * h : 3 * h, :] = kappa[pl.ds(at, h), :]
            out[3 * h :, :] = alpha[...]
        for t, out in enumerate(to_a):
            n = lax.rem(w + t, plan.wind)
            lanes = pl.ds(pl.multiple_of(plan.local(n, c) * plan.width, plan.width), plan.width)
            out[...] = kappa[:, lanes]

    outs = [jax.ShapeDtypeStruct((plan.wind, 2 * plan.rows_here, plan.width), F32)]
    outs += [jax.ShapeDtypeStruct((3 * h + 8, plan.cols_here), F32)] * plan.cross
    outs += [jax.ShapeDtypeStruct((plan.rows_here, plan.width), F32)] * plan.wind
    scratch = [pltpu.VMEM(field_real.shape, F32)]
    return call(body, outs, scratch, "prepare", (), (0,), (0, 1, 2))(
        field_real, field_imag, zone_map, alpha, zone_conductivity, place
    )


def home_rows(plan, parts, place):
    h = plan.height

    def body(*refs):
        place, field, kappa, alpha = refs[plan.cross :]
        for s, ref in enumerate(refs[: plan.cross]):
            c = lax.rem(place[1] + plan.cross - s, plan.cross)
            lanes = pl.ds(pl.multiple_of(c * plan.cols_here, plan.cols_here), plan.cols_here)
            field[c] = ref[0 : 2 * h, :]
            kappa[:, lanes] = ref[2 * h : 3 * h, :]
            alpha[:, lanes] = ref[3 * h :, :]

    outs = [
        jax.ShapeDtypeStruct((plan.cross, 2 * h, plan.cols_here), F32),
        jax.ShapeDtypeStruct((h, plan.cols), F32),
        jax.ShapeDtypeStruct((8, plan.cols), F32),
    ]
    return call(body, outs, [], "home_rows", range(plan.cross))(*parts, place)


def shifted(parts, axis):
    size = lax.axis_size(axis)
    return [parts[0]] + [lax.ppermute(parts[s], axis, [(i, (i + s) % size) for i in range(size)]) for s in range(1, size)]


def in_order(parts, place, which, name):
    size = len(parts)

    def body(*refs):
        place, out = refs[size], refs[-1]
        for s, ref in enumerate(refs[:size]):
            out[lax.rem(place[which] + size - s, size)] = ref[...]

    out = jax.ShapeDtypeStruct((size,) + parts[0].shape, F32)
    return call(body, [out], [], name, range(size))(*parts, place)[0]


def home_screen(plan, parts, place):
    def body(*refs):
        place, out = refs[plan.wind], refs[-1]
        for t, ref in enumerate(refs[: plan.wind]):
            w = lax.rem(place[0] + plan.wind - t, plan.wind)
            out[:, pl.ds(pl.multiple_of(plan.local(w, place[1]) * plan.width, plan.width), plan.width)] = ref[...]

    out = jax.ShapeDtypeStruct((plan.rows_here, plan.cols_here), F32)
    return call(body, [out], [], "home_screen", range(plan.wind))(*parts, place)[0]


def rows_send(plan, read_field, dft, table, field):
    def body(dft, table, field, out, *work):
        along_rows(functools.partial(read_field, field), [functools.partial(plan.send_a, out)], dft, table, *work)
        plan.send_edges(out)

    return call(body, [plan.sent_wide], plan.work_a(), "rows_send", (0, 1, 2), (0,))(dft, table, field)[0]


def cols_send(plan, read_field, back, dft, table, field):
    out = jax.ShapeDtypeStruct((plan.cross, 2 * plan.height, plan.cols_here), F32) if back else plan.sent

    def body(dft, table, field, out, *work):
        put = plan.back_b if back else plan.send_b
        along_cols(plan.height, functools.partial(read_field, field), [functools.partial(put, out)], dft, table, *work)

    return call(body, [out], plan.work_b(), "cols_send", (0, 1, 2), () if back else (0,))(dft, table, field)[0]


def cols_heat(plan, layer, copies, dft, table, received, absorption):
    blocks = plan.cols // INNER
    h = plan.height

    def body(dft, table, received, absorption, part, beside, totals, xh, xl, y, z, dh, dl):
        def write(b, off, value):
            alpha = absorption[layer : layer + 1, pl.ds(b * INNER, INNER)]
            deposit = alpha * (value[0] * value[0] + value[1] * value[1])
            lanes = pl.ds(b * INNER, INNER)
            if isinstance(off, int):
                beside[:, lanes] = deposit[0:8]
                return
            spot = (pl.ds(off, CHUNK), lanes)
            dh[spot], dl[spot] = split(deposit)

        along_cols(h, functools.partial(plan.wide_b, received), [write], dft, table, xh, xl, y, z)
        ones = lower_ones(h)
        dot = functools.partial(jnp.dot, preferred_element_type=F32)
        part[...] = dot(ones, dh[...]) + dot(ones, dl[...])
        for b in range(blocks):
            total = part[h - 1 : h, b * INNER : (b + 1) * INNER]
            for d in range(copies):
                totals[d, b : b + 1, :] = total

    outs = [
        jax.ShapeDtypeStruct((h, plan.cols), F32),
        jax.ShapeDtypeStruct((8, plan.cols), F32),
        jax.ShapeDtypeStruct((copies, blocks, INNER), F32),
    ]
    scratch = plan.work_b(CHUNK) + [pltpu.VMEM((h, plan.cols), BF16), pltpu.VMEM((h, plan.cols), BF16)]
    return call(body, outs, scratch, "cols_heat", (0, 1, 2), ())(dft, table, received, absorption)


def conducted(mid, up, down, left, right, k_mid, k_up, k_down, k_left, k_right):
    flux = (k_mid + k_up) * (up - mid) + (k_mid + k_down) * (down - mid)
    flux = flux + (k_mid + k_left) * (left - mid) + (k_mid + k_right) * (right - mid)
    return mid + (0.5 * conduct_rate) * flux


def cols_turn(plan, read_field, dft, table, screen, field):
    def body(dft, table, screen, field, out, *work):
        def read(b, off):
            return screened(read_field(field, b, off), screen[pl.ds(off, CHUNK), pl.ds(b * INNER, INNER)])

        along_cols(plan.height, read, [functools.partial(plan.send_b, out)], dft, table, *work)

    return call(body, [plan.sent], plan.work_b(), "cols_turn", (0, 1, 2), (0,))(dft, table, screen, field)[0]


def cols_smooth(plan, kappa, above, below, part, beside, *rest):
    blocks = plan.cols // INNER
    h = plan.height
    PAD = 16
    first, last = 0, plan.devices - 1

    def body(kappa, above, below, part, beside, *refs):
        sums, (me, screen, h0, h1, kx) = refs[:-5], refs[-5:]
        place = me[0] * plan.cross + me[1]
        zeros = jnp.zeros((PAD, plan.cols), F32)
        for ref in (h0, kx, h1):
            ref[0:PAD, :] = zeros
            ref[h + PAD : h + 2 * PAD, :] = zeros
        kx[PAD - 8 : PAD, :] = above[...]
        kx[PAD : PAD + h, :] = kappa[...]
        kx[PAD + h : PAD + h + 8, :] = below[...]
        upstream = jnp.zeros((blocks, INNER), F32)
        if len(sums) == 1:
            for d in range(plan.devices):
                upstream = upstream + jnp.where(d < place, sums[0][d], 0.0)
        else:
            for s in range(1, plan.cross):
                upstream = upstream + jnp.where(s <= me[1], sums[s - 1][...], 0.0)
            for t in range(1, plan.wind):
                upstream = upstream + jnp.where(t <= me[0], sums[plan.cross + t - 2][...], 0.0)
        has_next = jnp.where(place < last, 1.0, 0.0)
        for b in range(blocks):
            lanes = slice(b * INNER, (b + 1) * INNER)
            base = upstream[b : b + 1, :]
            h0[PAD : PAD + h, lanes] = part[:, lanes] + base
            h0[PAD - 1 : PAD, lanes] = base
            h0[PAD - 2 : PAD - 1, lanes] = base - beside[1:2, lanes]
            value = base + part[h - 1 : h, lanes] + beside[2:3, lanes]
            h0[PAD + h : PAD + h + 1, lanes] = value * has_next
            h0[PAD + h + 1 : PAD + h + 2, lanes] = (value + beside[3:4, lanes]) * has_next
        lane = lax.broadcasted_iota(jnp.int32, (8, plan.cols), 1)
        row = lax.broadcasted_iota(jnp.int32, (8, plan.cols), 0)

        def sides(x):
            left = jnp.where(lane == 0, 0.0, pltpu.roll(x, 1, 1))
            right = jnp.where(lane == plan.cols - 1, 0.0, pltpu.roll(x, plan.cols - 1, 1))
            return left, right

        def smooth(src, dst, low, count, masked):
            def step(i, carry):
                base = pl.multiple_of(low + i * 8, 8)
                value = src[pl.ds(base - 8, 24), :]
                kap = kx[pl.ds(base - 8, 24), :]
                mid, k_mid = value[8:16], kap[8:16]
                left, right = sides(mid)
                k_left, k_right = sides(k_mid)
                new = conducted(
                    mid, value[7:15], value[9:17], left, right, k_mid, kap[7:15], kap[9:17], k_left, k_right
                )
                if masked:
                    n = row + base
                    bad = ((n < PAD) & (place == first)) | ((n >= PAD + h) & (place == last))
                    new = jnp.where(bad, 0.0, new)
                if masked:
                    dst[pl.ds(base, 8), :] = new
                else:
                    screen[pl.ds(base - PAD, 8), :] = -new
                return carry

            lax.fori_loop(0, count, step, 0)

        refs = [h0, h1]
        for n in range(SMOOTH):
            if n < SMOOTH - 1:
                smooth(refs[n % 2], refs[(n + 1) % 2], PAD - 8, (h + 16) // 8, True)
            else:
                smooth(refs[n % 2], refs[(n + 1) % 2], PAD, h // 8, False)

    tall = pltpu.VMEM((h + 2 * PAD, plan.cols), F32)
    out = jax.ShapeDtypeStruct((h, plan.cols), F32)
    return call(body, [out], [tall] * 3, "cols_smooth", (), (0,))(kappa, above, below, part, beside, *rest)[0]


def rows_heat(plan, dft, table, received, alpha, kappa):
    width = plan.width

    def body(dft, table, received, alpha, kappa, heat, edge_left, edge_right, xh, xl, y, z, dep):
        def write(a, off, value):
            deposit = alpha[...] * (value[0] * value[0] + value[1] * value[1])
            rows = pl.ds(a * INNER + off, CHUNK)
            dep[rows, 0:width], dep[rows, width : 2 * width] = split(deposit)

        along_rows(functools.partial(plan.flip_a, received), [write], dft, table, xh, xl, y, z)
        tile = 2 * INNER
        ones = lower_ones(tile)
        carry = jnp.zeros((1, width), F32)
        for g in range(plan.rows // tile):
            both = jnp.dot(ones, dep[g * tile : (g + 1) * tile, :], preferred_element_type=F32)
            value = both[:, :width] + both[:, width:] + carry
            heat[g * tile : (g + 1) * tile, :] = value
            carry = value[tile - 1 : tile, :]
        lane = lax.broadcasted_iota(jnp.int32, (INNER, width), 1)
        for g in range(plan.rows // INNER):
            n = g * INNER
            src, at = n // plan.rows_here, n % plan.rows_here
            value = heat[n : n + INNER, :]
            kap = kappa[src, at : at + INNER, :]
            mixed = jnp.where((lane >= 4) & (lane < 64), pltpu.roll(kap, 4, 1), value)
            mixed = jnp.where((lane >= 64) & (lane < width - 4), pltpu.roll(kap, width - 4, 1), mixed)
            turned = mixed.T
            edge_left[:, n : n + INNER] = turned[0:8, :]
            edge_right[:, n : n + INNER] = turned[width - 8 : width, :]

    edge = jax.ShapeDtypeStruct((8, plan.rows), F32)
    outs = [jax.ShapeDtypeStruct((plan.rows, width), F32), edge, edge]
    scratch = plan.work_a() + [pltpu.VMEM((plan.rows, 2 * width), BF16)]
    return call(body, outs, scratch, "rows_heat", (0, 1, 2), ())(dft, table, received, alpha, kappa)


def rows_turn(plan, read_field, sets, wide, dft, table, screen, field):
    def body(dft, table, screen, field, *refs):
        outs, work = refs[:sets], refs[sets:]

        def read(a, off):
            return screened(read_field(field, a, off), screen[pl.ds(a * INNER + off, CHUNK), :])

        along_rows(read, [functools.partial(plan.send_a, out) for out in outs], dft, table, *work)
        if wide:
            plan.send_edges(outs[0])

    outs = [plan.sent_wide if wide and n == 0 else plan.sent for n in range(sets)]
    return call(body, outs, plan.work_a(), "rows_turn", (0, 1, 2), range(sets))(dft, table, screen, field)


def rows_smooth(plan, keep, heat, kappa, from_left, from_right, me):
    width = plan.width
    PAD = 8
    step_rows = 32

    def body(heat, kappa, from_left, from_right, me, screen, *refs):
        home_parts, h0, h1, kx = (refs[0] if keep else None, *refs[-3:])
        place = me[1] * plan.wind + plan.local(me[0], me[1])
        zeros = jnp.zeros((PAD, 2 * width), F32)
        for ref in (h0, h1, kx):
            ref[0:PAD, :] = zeros
            ref[plan.rows + PAD : plan.rows + 2 * PAD, :] = zeros
        lane = lax.broadcasted_iota(jnp.int32, (INNER, width), 1)
        for g in range(plan.rows // INNER):
            n = g * INNER
            src, at = n // plan.rows_here, n % plan.rows_here
            spot = slice(PAD + n, PAD + n + INNER)
            h0[spot, 0:width] = heat[n : n + INNER, :]
            kx[spot, 0:width] = kappa[src, at : at + INNER, :]
            turned = jnp.concatenate(
                [from_right[:, n : n + INNER], jnp.zeros((width - 16, INNER), F32), from_left[:, n : n + INNER]], axis=0
            ).T
            h0[spot, width : 2 * width] = jnp.where((lane < 4) | (lane >= width - 4), turned, 0.0)
            kap = jnp.where(lane < 4, pltpu.roll(turned, width - 4, 1), 0.0)
            kx[spot, width : 2 * width] = jnp.where(lane >= width - 4, pltpu.roll(turned, 4, 1), kap)
        wide = lax.broadcasted_iota(jnp.int32, (step_rows, 2 * width), 1)
        bad = (wide >= width) & (wide < width + width // 2) & (place == plan.devices - 1)
        bad = bad | ((wide >= width + width // 2) & (place == 0))

        def smooth(src, dst):
            def one(base):
                value = src[pl.ds(base, step_rows + 16), :]
                kap = kx[pl.ds(base, step_rows + 16), :]
                mid, k_mid = value[8:-8], kap[8:-8]
                new = conducted(
                    mid, value[7:-9], value[9:-7], pltpu.roll(mid, 1, 1), pltpu.roll(mid, 2 * width - 1, 1),
                    k_mid, kap[7:-9], kap[9:-7], pltpu.roll(k_mid, 1, 1), pltpu.roll(k_mid, 2 * width - 1, 1),
                )
                dst(base, jnp.where(bad, 0.0, new))

            def step(i, carry):
                for n in range(4):
                    one(pl.multiple_of((4 * i + n) * step_rows, step_rows))
                return carry

            lax.fori_loop(0, plan.rows // (4 * step_rows), step, 0)

        def into(ref):
            def put(base, value):
                ref[pl.ds(base + PAD, step_rows), :] = value

            return put

        def into_screen(base, value):
            screen[pl.ds(base, step_rows), :] = -value[:, :width]
            if keep:
                block = lax.rem(base // plan.rows_here + plan.wind - me[0], plan.wind)
                at = pl.multiple_of(lax.rem(base, plan.rows_here), step_rows)
                home_parts[block, pl.ds(at, step_rows), :] = -value[:, :width]

        refs = [h0, h1]
        for n in range(SMOOTH):
            smooth(refs[n % 2], into(refs[(n + 1) % 2]) if n < SMOOTH - 1 else into_screen)

    tall = pltpu.VMEM((plan.rows + 2 * PAD, 2 * width), F32)
    outs = [jax.ShapeDtypeStruct((plan.rows, width), F32)]
    if keep:
        outs.append(jax.ShapeDtypeStruct((plan.wind, plan.rows_here, width), F32))
    return call(body, outs, [tall] * 3, "rows_smooth", (), (0,))(heat, kappa, from_left, from_right, me)


def next_prev(value_up, value_down, axes, order):
    up = list(zip(order[:-1], order[1:]))
    down = [(j, i) for i, j in up]
    return lax.ppermute(value_up, axes, up), lax.ppermute(value_down, axes, down)


def extended(shard, sides, width):
    for axis, dim in sides:
        size, length = (lax.axis_size(axis), shard.shape[dim])
        up = [(i, (i + 1) % size) for i in range(size - 1)]
        down = [(j, i) for i, j in up]
        last = lax.slice_in_dim(shard, length - width, length, axis=dim)
        initial = lax.slice_in_dim(shard, 0, width, axis=dim)
        before = lax.ppermute(last, axis, up)
        after = lax.ppermute(initial, axis, down)
        shard = jnp.concatenate([before, shard, after], axis=dim)
    return shard


def carried_in(part, axis, combine, identity):
    place = lax.axis_index(axis)
    gathered = lax.all_gather(part, axis)
    state = jnp.zeros_like(part) + jnp.asarray(identity, part.dtype)

    def one(turn, state):
        return combine(state, lax.dynamic_index_in_dim(gathered, turn, 0, False))

    return lax.fori_loop(0, place, one, state)


def signed_freq(indices, length):
    shifted = jnp.where(indices < length // 2, indices, indices - length)
    return shifted.astype(jnp.float32) / length


def trig_table(first_ids, second_ids, length, sign_value):
    product = first_ids * second_ids % length
    phase_angle = product.astype(jnp.float32) * (sign_value * 2.0 * math.pi / length)
    return (jnp.cos(phase_angle), jnp.sin(phase_angle))


def complex_product(formula, real_part, imag_part, cosine, sine):
    highest = lax.Precision.HIGHEST
    out_real = jnp.einsum(formula, real_part, cosine, precision=highest) - jnp.einsum(
        formula, imag_part, sine, precision=highest
    )
    out_imag = jnp.einsum(formula, real_part, sine, precision=highest) + jnp.einsum(
        formula, imag_part, cosine, precision=highest
    )
    return (out_real, out_imag)


def transform(stacked, axis_dim, inverse):
    full_shape = stacked.shape
    length = full_shape[axis_dim]
    inner_len = math.gcd(length, 128)
    outer_len = length // inner_len
    leading = full_shape[1] if axis_dim == 2 else 1
    trailing = full_shape[2] if axis_dim == 1 else 1
    blocks = stacked.reshape(2, leading, outer_len, inner_len, trailing)
    sign_value = 1.0 if inverse else -1.0
    outer_ids = jnp.arange(outer_len, dtype=jnp.int32)
    inner_ids = jnp.arange(inner_len, dtype=jnp.int32)
    cos_outer, sin_outer = trig_table(outer_ids[:, None], outer_ids[None, :], outer_len, sign_value)
    first_real, first_imag = complex_product(
        "pabq,ak->pkbq", blocks[0], blocks[1], cos_outer, sin_outer
    )
    cos_twist, sin_twist = trig_table(outer_ids[:, None], inner_ids[None, :], length, sign_value)
    cos_twist = cos_twist[None, :, :, None]
    sin_twist = sin_twist[None, :, :, None]
    twist_real = first_real * cos_twist - first_imag * sin_twist
    twist_imag = first_real * sin_twist + first_imag * cos_twist
    cos_inner, sin_inner = trig_table(inner_ids[:, None], inner_ids[None, :], inner_len, sign_value)
    second_real, second_imag = complex_product(
        "pkbq,bm->pkmq", twist_real, twist_imag, cos_inner, sin_inner
    )
    result = jnp.stack([second_real, second_imag]).transpose(0, 1, 3, 2, 4).reshape(full_shape)
    if inverse:
        result = result * (1.0 / length)
    return result


def apply_phase(stacked, phase_angle):
    cosine = jnp.cos(phase_angle)
    sine = jnp.sin(phase_angle)
    return jnp.stack(
        [stacked[0] * cosine - stacked[1] * sine, stacked[0] * sine + stacked[1] * cosine]
    )


def along_joint(stacked, phase_rate, row_freq, col_freq):
    cross_count = lax.axis_size("cross")
    stacked = lax.all_to_all(stacked, ("wind", "cross"), split_axis=2, concat_axis=1, tiled=True)
    stacked = transform(stacked, 1, False)
    col_width = stacked.shape[2]
    joint_block = lax.axis_index("wind") * cross_count + lax.axis_index("cross")
    cols_held = lax.dynamic_slice_in_dim(col_freq, joint_block * col_width, col_width)
    phase_angle = -phase_rate * (
        row_freq[:, None] * row_freq[:, None] + cols_held[None, :] * cols_held[None, :]
    )
    stacked = apply_phase(stacked, phase_angle)
    stacked = transform(stacked, 1, True)
    return lax.all_to_all(stacked, ("wind", "cross"), split_axis=1, concat_axis=2, tiled=True)


def propagate_slab(slab_pair, share_step):
    rows_total = slab_pair.shape[1] * lax.axis_size("wind") * lax.axis_size("cross")
    cols_total = slab_pair.shape[2]
    phase_rate = share_step * diffraction
    row_freq = signed_freq(jnp.arange(rows_total, dtype=jnp.int32), rows_total)
    col_freq = signed_freq(jnp.arange(cols_total, dtype=jnp.int32), cols_total)
    stacked = transform(slab_pair, 2, False)
    stacked = along_joint(stacked, phase_rate, row_freq, col_freq)
    return transform(stacked, 2, True)


def conduct_core(padded, kappa_pad):
    height = padded.shape[0] - 2
    breadth = padded.shape[1] - 2
    center = padded[1:-1, 1:-1]
    kappa_mid = kappa_pad[1:-1, 1:-1]
    flux_sum = jnp.zeros_like(center)
    for offset_row, offset_col in ((0, 1), (2, 1), (1, 0), (1, 2)):
        neighbour = padded[offset_row : offset_row + height, offset_col : offset_col + breadth]
        kappa_side = kappa_pad[offset_row : offset_row + height, offset_col : offset_col + breadth]
        flux_sum = flux_sum + 0.5 * (kappa_mid + kappa_side) * (neighbour - center)
    return center + conduct_rate * flux_sum


def add_terms(earlier, later_term):
    return earlier + later_term


def layer_absorption(index_row, table_row, level_ids):
    one_hot = (index_row[:, None] == level_ids[None, :]).astype(jnp.float32)
    return jnp.sum(one_hot * table_row[None, :], axis=1)


def wide_device(field_real, field_imag, absorb_index, absorb_table, zone_map, zone_conductivity):
    rows_here, cols_here = field_real.shape
    conductivity = jnp.zeros((rows_here, cols_here), jnp.float32)
    for zone_no in range(zone_conductivity.shape[0]):
        conductivity = jnp.where(zone_map == zone_no, zone_conductivity[zone_no], conductivity)
    level_ids = jnp.arange(absorb_table.shape[1], dtype=jnp.int32)
    combined = lax.all_to_all(
        jnp.stack([field_real, field_imag, conductivity]),
        "cross",
        split_axis=1,
        concat_axis=2,
        tiled=True,
    )
    slab_pair = combined[:2]
    kappa_rows = extended(combined[2], ((("wind", "cross"), 0),), 1)
    kappa_pad = jnp.pad(kappa_rows, ((0, 0), (1, 1)))
    index_full = lax.all_gather(absorb_index, "cross", axis=1, tiled=True)
    slab_rows = slab_pair.shape[1]
    rows_total = slab_rows * lax.axis_size("wind") * lax.axis_size("cross")
    slab_ids = jnp.arange(slab_rows, dtype=jnp.int32)
    lower_slab = (slab_ids[:, None] >= slab_ids[None, :]).astype(jnp.float32)
    screen_phase = jnp.zeros((slab_rows, slab_pair.shape[2]), jnp.float32)
    for layer_no in range(LAYERS):
        absorption = layer_absorption(index_full[layer_no], absorb_table[layer_no], level_ids)
        screen_phase = jnp.zeros((slab_rows, slab_pair.shape[2]), jnp.float32)
        for round_no in range(ITERS):
            middle = propagate_slab(apply_phase(slab_pair, screen_phase), 0.5)
            intensity = middle[0] * middle[0] + middle[1] * middle[1]
            deposit = absorption[None, :] * intensity * (1.0 / rows_total)
            partial_heat = jnp.dot(lower_slab, deposit, precision=lax.Precision.HIGHEST)
            totals = partial_heat[-1]
            upstream = carried_in(totals, ("wind", "cross"), add_terms, jnp.zeros_like(totals))
            heat_field = partial_heat + upstream[None, :]
            for smooth_no in range(SMOOTH):
                padded = extended(heat_field, ((("wind", "cross"), 0),), 1)
                padded = jnp.pad(padded, ((0, 0), (1, 1)))
                heat_field = conduct_core(padded, kappa_pad)
            screen_phase = -heat_field
        slab_pair = propagate_slab(apply_phase(slab_pair, screen_phase), 1.0)
    returned = lax.all_to_all(
        jnp.stack([slab_pair[0], slab_pair[1], screen_phase]),
        "cross",
        split_axis=2,
        concat_axis=1,
        tiled=True,
    )
    return (returned[0], returned[1], returned[2])


def on_device(field_real, field_imag, absorb_index, absorb_table, zone_map, zone_conductivity):
    plan = Plan(*field_real.shape, lax.axis_size("wind"), lax.axis_size("cross"))
    fits = plan.width == INNER and INNER % plan.height == 0 and plan.height % CHUNK == 0
    if not fits or plan.rows_here % INNER or plan.rows % (2 * INNER):
        return wide_device(field_real, field_imag, absorb_index, absorb_table, zone_map, zone_conductivity)
    wind, cross = plan.wind, plan.cross
    w, c = lax.axis_index("wind"), lax.axis_index("cross")
    place = jnp.stack([w, c]).astype(jnp.int32)
    grid_axes = ("wind", "cross")
    columns_order = [plan.slot(i) for i in range(plan.devices)]

    def exchange(x, axes):
        return lax.all_to_all(x, axes, split_axis=0, concat_axis=0, tiled=True)

    def flip(x):
        return exchange(x, grid_axes)

    alpha = jnp.zeros(absorb_index.shape, F32)
    for level in range(absorb_table.shape[1]):
        alpha = jnp.where(absorb_index == level, absorb_table[:, level : level + 1], alpha)
    alpha = alpha * (1.0 / plan.rows)
    alpha_a = lax.dynamic_slice_in_dim(alpha, plan.local(w, c) * plan.width, plan.width, axis=1)
    alpha = jnp.pad(alpha, ((0, 8 - LAYERS), (0, 0)))
    to_a, *blocks = prepare(plan, field_real, field_imag, zone_map, alpha, zone_conductivity, place)
    home_a = exchange(to_a, "wind")
    home_b, kappa_b, alpha_b = home_rows(plan, shifted(blocks[:cross], "cross"), place)

    dft = jnp.asarray(dft_matrices())
    tab_a = lambda *shares: jnp.asarray(row_table(plan.rows, shares))
    tab_b = lambda *shares: jnp.asarray(chirp_columns(plan.cols, shares))

    def smooth_a(layer, share, keep, received):
        heat, left, right = rows_heat(plan, dft, tab_a(share), received, alpha_a[layer : layer + 1], kappa_a)
        from_left, from_right = next_prev(right, left, grid_axes, columns_order)
        return rows_smooth(plan, keep, heat, kappa_a, from_left, from_right, place)

    home_a, home_b = lax.optimization_barrier((home_a, home_b))
    sent = rows_send(plan, plan.home_a, dft, tab_a(0.5), home_a)
    received, kappa_blocks = lax.optimization_barrier((flip(sent), blocks[cross:]))
    kappa_blocks = shifted(kappa_blocks, "wind")
    above, below = next_prev(kappa_b[-8:], kappa_b[:8], grid_axes, list(range(plan.devices)))
    part, beside, totals = cols_heat(plan, 0, plan.devices, dft, tab_b(0.5), received, alpha_b)
    screen = cols_smooth(plan, kappa_b, above, below, part, beside, flip(totals), place)
    sent = cols_turn(plan, plan.home_b, dft, tab_b(0.5), screen, home_b)
    sent, kappa_blocks = lax.optimization_barrier((sent, kappa_blocks))
    kappa_a = in_order(kappa_blocks, place, 0, "kappa_a")
    (screen,) = smooth_a(0, 0.5, False, flip(sent))
    sent_middle, sent_field = rows_turn(plan, plan.home_a, 2, True, dft, tab_a(1.5, 1.0), screen, home_a)
    middle = flip(sent_middle)
    field_b = cols_send(plan, plan.flip_b, False, dft, tab_b(1.0), flip(sent_field))
    field_a = flip(field_b)
    part, beside, totals = cols_heat(plan, 1, 1, dft, tab_b(1.5), middle, alpha_b)
    across = shifted([totals[0]] * cross, "cross")
    along = shifted([sum(across[1:], across[0])] * wind, "wind")
    screen = cols_smooth(plan, kappa_b, above, below, part, beside, *across[1:], *along[1:], place)
    sent = cols_turn(plan, plan.flip_b, dft, tab_b(0.5), screen, field_b)
    screen, home_parts = smooth_a(1, 0.5, True, flip(sent))
    (sent,) = rows_turn(plan, plan.flip_a, 1, False, dft, tab_a(1.0), screen, field_a)
    received, home_parts = lax.optimization_barrier((flip(sent), home_parts))
    back = cols_send(plan, plan.flip_b, True, dft, tab_b(1.0), received)
    screen = home_screen(plan, shifted([home_parts[t] for t in range(wind)], "wind"), place)
    back = exchange(back, "cross")
    out_real = back[:, : plan.height].reshape(field_real.shape)
    out_imag = back[:, plan.height :].reshape(field_real.shape)
    return (out_real, out_imag, screen)


def solution(mesh):
    in_specs = (
        P(("beams", "wind"), "cross"),
        P(("beams", "wind"), "cross"),
        P(None, "cross"),
        P(),
        P("wind", "cross"),
        P(),
    )
    out_specs = (
        P(("beams", "wind"), "cross"),
        P(("beams", "wind"), "cross"),
        P(("beams", "wind"), "cross"),
    )
    return jax.shard_map(
        on_device, mesh=mesh, in_specs=in_specs, out_specs=out_specs, check_vma=False
    )
```

```python
import functools
import math

import jax
import jax.numpy as jnp
import numpy as np
from jax import lax
from jax.experimental import pallas as pl
from jax.experimental.pallas import tpu as pltpu
from jax.sharding import PartitionSpec as P


LAYERS = 2
ITERS = 2
SMOOTH = 2
INNER = 128
CHUNK = 16

diffraction = 2000.0
conduct_rate = 0.24

F32 = jnp.float32
BF16 = jnp.bfloat16
WHOLE = pl.BlockSpec(memory_space=pltpu.VMEM)
SCALAR = pl.BlockSpec(memory_space=pltpu.SMEM)


def split_np(values):
    high = values.astype(np.float32).astype(jnp.bfloat16)
    low = (values - high.astype(np.float64)).astype(np.float32).astype(jnp.bfloat16)
    return high, low


def dft_matrices():
    ids = np.arange(INNER)
    angle = 2.0 * np.pi * (np.outer(ids, ids) % INNER) / INNER
    cosine, sine = np.cos(angle), np.sin(angle)
    left = np.block([[cosine, sine], [-sine, cosine]])
    return np.stack([*split_np(left), *split_np(left.T)])


def chirp_columns(length, shares):
    outer = length // INNER
    k = np.arange(outer)[:, None]
    m = np.arange(INNER)[None, :]
    twist = -2.0 * np.pi * ((k * m) % length) / length
    tables = [np.cos(twist), np.sin(twist)]
    p = k + outer * m
    freq = np.where(p < length // 2, p, p - length) / length
    for share in shares:
        angle = -share * diffraction * freq * freq
        tables += [np.cos(angle) / length, np.sin(angle) / length]
    return np.concatenate(tables, axis=0).astype(np.float32)


def row_table(length):
    cols = chirp_columns(length, ()).T
    return np.pad(cols, ((0, 0), (0, -cols.shape[1] % 128)))


def row_blocks(length, share):
    outer = length // INNER
    ids = np.arange(INNER)
    forward = np.exp(-2j * np.pi * (np.outer(ids, ids) % INNER) / INNER)
    blocks = []
    for k in range(outer):
        p = k + outer * ids
        freq = np.where(p < length // 2, p, p - length) / length
        block = forward.conj() @ (np.exp(-1j * share * diffraction * freq * freq)[:, None] / length * forward)
        blocks.append(np.stack(split_np(np.block([[block.real, -block.imag], [block.imag, block.real]]))))
    return np.stack(blocks)


def split(x):
    high = x.astype(BF16)
    return high, (x - high.astype(F32)).astype(BF16)


def times(a, b):
    return (a[0] * b[0] - a[1] * b[1], a[0] * b[1] + a[1] * b[0])


def small_fft(points, sign):
    count = len(points)
    if count == 1:
        return points
    even = small_fft(points[0::2], sign)
    odd = small_fft(points[1::2], sign)
    half = count // 2
    out = [None] * count
    for k in range(half):
        re, im = odd[k]
        if k == 0:
            turn = (re, im)
        elif 4 * k == count:
            turn = (-im, re) if sign > 0 else (im, -re)
        elif 8 * k == count:
            root = math.sqrt(0.5)
            turn = (root * (re - im), root * (im + re)) if sign > 0 else (root * (re + im), root * (im - re))
        elif 8 * k == 3 * count:
            root = math.sqrt(0.5)
            turn = (-root * (re + im), root * (re - im)) if sign > 0 else (root * (im - re), -root * (re + im))
        else:
            c = math.cos(2.0 * math.pi * k / count)
            s = sign * math.sin(2.0 * math.pi * k / count)
            turn = (c * re - s * im, s * re + c * im)
        out[k] = (even[k][0] + turn[0], even[k][1] + turn[1])
        out[k + half] = (even[k][0] - turn[0], even[k][1] - turn[1])
    return out


def cos_sin(x):
    turns = jnp.floor(x * (2.0 / math.pi) + 0.5)
    r = ((x - turns * 1.5703125) - turns * 4.837512969970703125e-4) - turns * 7.549789954891882e-8
    quad = turns.astype(jnp.int32)
    z = r * r
    s = r + r * z * (-1.6666654611e-1 + z * (8.3321608736e-3 - z * 1.9515295891e-4))
    c = 1.0 - 0.5 * z + z * z * (4.166664568298827e-2 + z * (-1.388731625493765e-3 + z * 2.443315711809948e-5))
    odd = (quad & 1) == 1
    sin_x = jnp.where(odd, c, s)
    cos_x = jnp.where(odd, s, c)
    sin_x = jnp.where((quad & 2) == 2, -sin_x, sin_x)
    cos_x = jnp.where(((quad + 1) & 2) == 2, -cos_x, cos_x)
    return cos_x, sin_x


def screened(value, screen):
    return times(value, cos_sin(screen))


def triple(a_high, a_low, b_high, b_low):
    dot = functools.partial(jnp.dot, preferred_element_type=F32)
    return dot(a_high, b_high) + dot(a_high, b_low) + dot(a_low, b_high)


def lower_ones(size):
    r = lax.broadcasted_iota(jnp.int32, (size, size), 0)
    c = lax.broadcasted_iota(jnp.int32, (size, size), 1)
    return jnp.where(r >= c, 1.0, 0.0).astype(BF16)


def chunks(count, body):
    def step(i, carry):
        body(pl.multiple_of(i * CHUNK, CHUNK))
        return carry

    lax.fori_loop(0, count // CHUNK, step, 0)


def along_rows(read, write, matrices, table, xh, z):
    outer = matrices.shape[0]
    width = z.shape[1] // outer
    lanes = lambda k: pl.ds(k * width, width)
    col = lambda part, off: table[pl.ds(off, CHUNK), part : part + 1]

    def first(off):
        for k, value in enumerate(small_fft([read(a, off) for a in range(outer)], -1)):
            if k:
                value = times(value, (col(k, off), col(outer + k, off)))
            for at, v in ((0, value[0]), (INNER, value[1])):
                high, low = split(v)
                xh[pl.ds(at + off, CHUNK), pl.ds(2 * k * width, width)] = high
                xh[pl.ds(at + off, CHUNK), pl.ds((2 * k + 1) * width, width)] = low

    def last(off):
        values = []
        for k in range(outer):
            value = (z[pl.ds(off, CHUNK), lanes(k)], z[pl.ds(INNER + off, CHUNK), lanes(k)])
            if k:
                value = times(value, (col(k, off), -col(outer + k, off)))
            values.append(value)
        for a, value in enumerate(small_fft(values, 1)):
            write(a, off, value)

    chunks(INNER, first)
    dot = functools.partial(jnp.dot, preferred_element_type=F32)
    for k in range(outer):
        both = dot(matrices[k, 0], xh[:, 2 * k * width : (2 * k + 2) * width])
        low = dot(matrices[k, 1], xh[:, 2 * k * width : (2 * k + 1) * width])
        z[:, k * width : (k + 1) * width] = both[:, :width] + both[:, width:] + low
    chunks(INNER, last)


def along_cols(main, read, writes, dft, table, xh, xl, y, z):
    outer = table.shape[0] // (2 * (1 + len(writes)))
    height = xh.shape[0] // outer

    def every(body):
        chunks(main, body)
        if height > main:
            body(main)

    row = lambda part: table[part : part + 1, :]

    def put(k, off, value):
        for at, v in ((0, value[0]), (INNER, value[1])):
            spot = (pl.ds(k * height + off, CHUNK), pl.ds(at, INNER))
            xh[spot], xl[spot] = split(v)

    def get(ref, k, off):
        return tuple(ref[pl.ds(k * height + off, CHUNK), pl.ds(at, INNER)] for at in (0, INNER))

    def first(off):
        for k, value in enumerate(small_fft([read(b, off) for b in range(outer)], -1)):
            if k:
                value = times(value, (row(k), row(outer + k)))
            put(k, off, value)

    every(first)
    y[...] = triple(xh[...], xl[...], dft[2], dft[3])
    for n, write in enumerate(writes):

        def middle(off, n=n):
            for k in range(outer):
                base = (2 + 2 * n) * outer + k
                put(k, off, times(get(y, k, off), (row(base), row(base + outer))))

        every(middle)
        z[...] = triple(xh[...], xl[...], dft[0], dft[1])

        def last(off, write=write):
            values = []
            for k in range(outer):
                value = get(z, k, off)
                if k:
                    value = times(value, (row(k), -row(outer + k)))
                values.append(value)
            for b, value in enumerate(small_fft(values, 1)):
                write(b, off, value)

        every(last)


class Plan:
    def __init__(self, rows_here, cols_here, wind, cross):
        self.wind, self.cross = wind, cross
        self.devices = wind * cross
        self.rows_here, self.cols_here = rows_here, cols_here
        self.height = rows_here // cross
        self.width = cols_here // wind
        self.rows, self.cols = rows_here * wind, cols_here * cross

    def local(self, w, c):
        return w + (c % 2) * (self.wind - 1 - 2 * w)

    def slot(self, block):
        c, i = block // self.wind, block % self.wind
        return self.local(i, c) * self.cross + c

    def home_a(self, ref, a, off):
        n = a * INNER
        src, at = n // self.rows_here, n % self.rows_here
        return tuple(ref[src, pl.ds(p * self.rows_here + at + off, CHUNK), :] for p in (0, 1))

    def spot_a(self, a, off):
        per = INNER // self.height
        return a * per + off // self.height, lax.rem(off, self.height)

    def flip_a(self, ref, a, off):
        s, at = self.spot_a(a, off)
        at = pl.multiple_of(at, CHUNK)
        return tuple(ref[s, pl.ds(p * self.height + at, CHUNK), :] for p in (0, 1))

    def send_a(self, ref, a, off, value):
        s, at = self.spot_a(a, off)
        at = pl.multiple_of(at, CHUNK)
        for p in (0, 1):
            ref[s, pl.ds(p * self.height + at, CHUNK), :] = value[p]

    def send_edges(self, ref):
        h = self.height
        for d in range(self.devices):
            for p in (0, 1):
                at = 2 * h + 4 * p
                before = ref[d - 1, p * h + h - 2 : p * h + h, :] if d else jnp.zeros((2, self.width), F32)
                after = ref[d + 1, p * h : p * h + 2, :] if d + 1 < self.devices else jnp.zeros((2, self.width), F32)
                ref[d, at : at + 2, :] = before
                ref[d, at + 2 : at + 4, :] = after

    def edges(self, value, left, right, at):
        turned = value.T
        left[:, at : at + INNER] = turned[0:8, :]
        right[:, at : at + INNER] = turned[self.width - 8 : self.width, :]

    def home_b(self, ref, b, off):
        per = self.cols_here // INNER
        return tuple(ref[b // per, pl.ds(p * self.height + off, CHUNK), pl.ds((b % per) * INNER, INNER)] for p in (0, 1))

    def wide_b(self, ref, b, off):
        if isinstance(off, int):
            extra = ref[self.slot(b), 2 * self.height : 2 * self.height + 8, :]
            turned = jnp.concatenate([extra[4:8], extra[0:4]], axis=0)
            return jnp.concatenate([extra, extra], axis=0), jnp.concatenate([turned, turned], axis=0)
        return self.flip_b(ref, b, off)

    def flip_b(self, ref, b, off):
        return tuple(ref[self.slot(b), pl.ds(p * self.height + off, CHUNK), :] for p in (0, 1))

    def send_b(self, ref, b, off, value):
        for p in (0, 1):
            ref[self.slot(b), pl.ds(p * self.height + off, CHUNK), :] = value[p]

    def back_b(self, ref, b, off, value):
        per = self.cols_here // INNER
        for p in (0, 1):
            ref[b // per, pl.ds(p * self.height + off, CHUNK), pl.ds((b % per) * INNER, INNER)] = value[p]

    @property
    def sent(self):
        return jax.ShapeDtypeStruct((self.devices, 2 * self.height, self.width), F32)

    def work_a(self):
        wide = (self.rows // INNER) * self.width
        return [
            pltpu.VMEM((2 * INNER, 2 * wide), BF16),
            pltpu.VMEM((2 * INNER, wide), F32),
        ]

    @property
    def sent_wide(self):
        return jax.ShapeDtypeStruct((self.devices, 2 * self.height + 8, self.width), F32)

    def work_b(self, extra=0):
        tall = (self.cols // INNER) * (self.height + extra)
        return [
            pltpu.VMEM((tall, 2 * INNER), BF16),
            pltpu.VMEM((tall, 2 * INNER), BF16),
            pltpu.VMEM((tall, 2 * INNER), F32),
            pltpu.VMEM((tall, 2 * INNER), F32),
        ]


def call(body, outs, scratch, near=(), near_outs=(), far=()):
    def run(*args):
        specs = [SCALAR if a.size <= 16 else WHOLE for a in args]
        spaces = [pltpu.VMEM if i in near else pltpu.HBM if i in far else None for i in range(len(args))]
        args = [pltpu.with_memory_space_constraint(a, space) if space else a for a, space in zip(args, spaces)]
        return pl.pallas_call(
            body,
            out_shape=[pltpu.VMEM(o.shape, o.dtype) if i in near_outs else o for i, o in enumerate(outs)],
            in_specs=specs,
            out_specs=[WHOLE] * len(outs),
            scratch_shapes=scratch,
            compiler_params=pltpu.CompilerParams(vmem_limit_bytes=24 * 1024 * 1024),
        )(*args)

    return run


def prepare_field(plan, field_real, field_imag, place):
    h = plan.height

    def body(real, imag, place, to_b, *to_a):
        for c in range(plan.cross):
            to_b[c, 0:h, :] = real[c * h : (c + 1) * h, :]
            to_b[c, h : 2 * h, :] = imag[c * h : (c + 1) * h, :]
        for t, out in enumerate(to_a):
            n = lax.rem(place[0] + t, plan.wind)
            lanes = pl.ds(pl.multiple_of(plan.local(n, place[1]) * plan.width, plan.width), plan.width)
            out[0 : plan.rows_here, :] = real[:, lanes]
            out[plan.rows_here : 2 * plan.rows_here, :] = imag[:, lanes]

    outs = [jax.ShapeDtypeStruct((plan.cross, 2 * h, plan.cols_here), F32)]
    outs += [jax.ShapeDtypeStruct((2 * plan.rows_here, plan.width), F32)] * plan.wind
    return call(body, outs, [], (), (), (0, 1))(field_real, field_imag, place)


def prepare(plan, zone_map, absorb_index, absorb_table, zone_conductivity, place):
    h = plan.height

    def picked(ids, count, level):
        value = jnp.zeros(ids.shape, F32)
        for n in range(count):
            value = jnp.where(ids == n, level(n), value)
        return value

    def body(zones, index, table, levels, place, *refs):
        to_b, to_a, alpha_a, kappa, alpha = refs[: plan.cross], refs[plan.cross : -3], refs[-3], refs[-2], refs[-1]
        w, c = place[0], place[1]

        def step(off):
            kappa[pl.ds(off, CHUNK), :] = picked(zones[pl.ds(off, CHUNK), :], levels.shape[0], lambda n: levels[n])

        chunks(plan.rows_here, step)
        alpha[...] = jnp.zeros_like(alpha)
        for layer in range(LAYERS):
            value = picked(index[layer : layer + 1, :], table.shape[1], lambda n: table[layer, n])
            alpha[layer : layer + 1, :] = value * (1.0 / plan.rows)
        alpha_a[...] = alpha[:, pl.ds(pl.multiple_of(plan.local(w, c) * plan.width, plan.width), plan.width)]
        for s, out in enumerate(to_b):
            out[0:h, :] = kappa[pl.ds(pl.multiple_of(lax.rem(c + s, plan.cross) * h, h), h), :]
            out[h:, :] = alpha[...]
        for t, out in enumerate(to_a):
            n = lax.rem(w + t, plan.wind)
            lanes = pl.ds(pl.multiple_of(plan.local(n, c) * plan.width, plan.width), plan.width)
            out[...] = kappa[:, lanes]

    outs = [jax.ShapeDtypeStruct((h + 8, plan.cols_here), F32)] * plan.cross
    outs += [jax.ShapeDtypeStruct((plan.rows_here, plan.width), F32)] * plan.wind
    outs.append(jax.ShapeDtypeStruct((8, plan.width), F32))
    scratch = [pltpu.VMEM(zone_map.shape, F32), pltpu.VMEM((8, plan.cols_here), F32)]
    return call(body, outs, scratch, (), (), (0,))(zone_map, absorb_index, absorb_table, zone_conductivity, place)


def home_rows(plan, parts, place):
    h = plan.height

    def body(*refs):
        place, kappa, alpha = refs[plan.cross :]
        for s, ref in enumerate(refs[: plan.cross]):
            c = lax.rem(place[1] + plan.cross - s, plan.cross)
            lanes = pl.ds(pl.multiple_of(c * plan.cols_here, plan.cols_here), plan.cols_here)
            kappa[:, lanes] = ref[0:h, :]
            alpha[:, lanes] = ref[h:, :]

    outs = [jax.ShapeDtypeStruct((h, plan.cols), F32), jax.ShapeDtypeStruct((8, plan.cols), F32)]
    return call(body, outs, [])(*parts, place)


def shifted(parts, axis):
    size = lax.axis_size(axis)
    return [parts[0]] + [lax.ppermute(parts[s], axis, [(i, (i + s) % size) for i in range(size)]) for s in range(1, size)]


def in_order(parts, place, which):
    size = len(parts)

    def body(*refs):
        place, out = refs[size], refs[-1]
        for s, ref in enumerate(refs[:size]):
            out[lax.rem(place[which] + size - s, size)] = ref[...]

    out = jax.ShapeDtypeStruct((size,) + parts[0].shape, F32)
    return call(body, [out], [], range(size))(*parts, place)[0]


def home_screen(plan, parts, place):
    h = plan.height

    def body(*refs):
        place, out = refs[plan.cross], refs[-1]
        for s, ref in enumerate(refs[: plan.cross]):
            c = lax.rem(place[1] + plan.cross - s, plan.cross)
            out[pl.ds(pl.multiple_of(c * h, h), h), :] = ref[...]

    out = jax.ShapeDtypeStruct((plan.rows_here, plan.cols_here), F32)
    return call(body, [out], [])(*parts, place)[0]


def rows_kappa(plan, parts, place):
    def body(*refs):
        place, out, left, right = refs[plan.wind :]
        for t, ref in enumerate(refs[: plan.wind]):
            w = lax.rem(place[0] + plan.wind - t, plan.wind)
            out[pl.ds(pl.multiple_of(w * plan.rows_here, plan.rows_here), plan.rows_here), :] = ref[...]
        for g in range(plan.rows // INNER):
            plan.edges(out[g * INNER : (g + 1) * INNER, :], left, right, g * INNER)

    edge = jax.ShapeDtypeStruct((8, plan.rows), F32)
    outs = [jax.ShapeDtypeStruct((plan.rows, plan.width), F32), edge, edge]
    return call(body, outs, [], range(plan.wind))(*parts, place)


def rows_field(plan, read_field, dft, table, field):
    def body(dft, table, field, out, *work):
        along_rows(functools.partial(read_field, field), functools.partial(plan.send_a, out), dft, table, *work)

    return call(body, [plan.sent], plan.work_a(), (0, 1, 2), (0,))(dft, table, field)[0]


def cols_send(plan, read_field, back, dft, table, field):
    out = jax.ShapeDtypeStruct((plan.cross, 2 * plan.height, plan.cols_here), F32) if back else plan.sent

    def body(dft, table, field, out, *work):
        put = plan.back_b if back else plan.send_b
        along_cols(plan.height, functools.partial(read_field, field), [functools.partial(put, out)], dft, table, *work)

    return call(body, [out], plan.work_b(), (0, 1, 2), () if back else (0,))(dft, table, field)[0]


def cols_heat(plan, layer, copies, dft, table, received, absorption):
    blocks = plan.cols // INNER
    h = plan.height

    def body(dft, table, received, absorption, part, beside, totals, xh, xl, y, z, dh, dl):
        def write(b, off, value):
            alpha = absorption[layer : layer + 1, pl.ds(b * INNER, INNER)]
            deposit = alpha * (value[0] * value[0] + value[1] * value[1])
            lanes = pl.ds(b * INNER, INNER)
            if isinstance(off, int):
                beside[:, lanes] = deposit[0:8]
                return
            spot = (pl.ds(off, CHUNK), lanes)
            dh[spot], dl[spot] = split(deposit)

        along_cols(h, functools.partial(plan.wide_b, received), [write], dft, table, xh, xl, y, z)
        ones = lower_ones(h)
        dot = functools.partial(jnp.dot, preferred_element_type=F32)
        part[...] = dot(ones, dh[...]) + dot(ones, dl[...])
        for b in range(blocks):
            total = part[h - 1 : h, b * INNER : (b + 1) * INNER]
            for d in range(copies):
                totals[d, b : b + 1, :] = total

    outs = [
        jax.ShapeDtypeStruct((h, plan.cols), F32),
        jax.ShapeDtypeStruct((8, plan.cols), F32),
        jax.ShapeDtypeStruct((copies, blocks, INNER), F32),
    ]
    scratch = plan.work_b(CHUNK) + [pltpu.VMEM((h, plan.cols), BF16), pltpu.VMEM((h, plan.cols), BF16)]
    return call(body, outs, scratch, (0, 1, 2), ())(dft, table, received, absorption)


def conducted(mid, up, down, left, right, k_mid, k_up, k_down, k_left, k_right):
    flux = (k_mid + k_up) * (up - mid) + (k_mid + k_down) * (down - mid)
    flux = flux + (k_mid + k_left) * (left - mid) + (k_mid + k_right) * (right - mid)
    return mid + (0.5 * conduct_rate) * flux


def cols_turn(plan, read_field, sets, dft, table, screen, field):
    def body(dft, table, screen, field, *refs):
        outs, work = refs[:sets], refs[sets:]

        def read(b, off):
            return screened(read_field(field, b, off), screen[pl.ds(off, CHUNK), pl.ds(b * INNER, INNER)])

        along_cols(plan.height, read, [functools.partial(plan.send_b, out) for out in outs], dft, table, *work)

    return call(body, [plan.sent] * sets, plan.work_b(), (0, 1, 2), range(sets))(
        dft, table, screen, field
    )


def cols_smooth(plan, keep, kappa, above, below, part, beside, *rest):
    blocks = plan.cols // INNER
    h = plan.height
    PAD = 16
    first, last = 0, plan.devices - 1

    def body(kappa, above, below, part, beside, *refs):
        count = plan.cross + 1 if keep else 1
        sums, me, outs, (h0, h1, kx, kept) = refs[: -5 - count], refs[-5 - count], refs[-4 - count : -4], refs[-4:]
        place = me[0] * plan.cross + me[1]
        zeros = jnp.zeros((PAD, plan.cols), F32)
        for ref in (h0, kx, h1):
            ref[0:PAD, :] = zeros
            ref[h + PAD : h + 2 * PAD, :] = zeros
        kx[PAD - 8 : PAD, :] = above[...]
        kx[PAD : PAD + h, :] = kappa[...]
        kx[PAD + h : PAD + h + 8, :] = below[...]
        upstream = jnp.zeros((blocks, INNER), F32)
        if len(sums) == 1:
            for d in range(plan.devices):
                upstream = upstream + jnp.where(d < place, sums[0][d], 0.0)
        else:
            for s in range(1, plan.cross):
                upstream = upstream + jnp.where(s <= me[1], sums[s - 1][...], 0.0)
            for t in range(1, plan.wind):
                upstream = upstream + jnp.where(t <= me[0], sums[plan.cross + t - 2][...], 0.0)
        has_next = jnp.where(place < last, 1.0, 0.0)
        for b in range(blocks):
            lanes = slice(b * INNER, (b + 1) * INNER)
            base = upstream[b : b + 1, :]
            h0[PAD : PAD + h, lanes] = part[:, lanes] + base
            h0[PAD - 1 : PAD, lanes] = base
            h0[PAD - 2 : PAD - 1, lanes] = base - beside[1:2, lanes]
            value = base + part[h - 1 : h, lanes] + beside[2:3, lanes]
            h0[PAD + h : PAD + h + 1, lanes] = value * has_next
            h0[PAD + h + 1 : PAD + h + 2, lanes] = (value + beside[3:4, lanes]) * has_next
        lane = lax.broadcasted_iota(jnp.int32, (8, plan.cols), 1)
        row = lax.broadcasted_iota(jnp.int32, (8, plan.cols), 0)

        def sides(x):
            left = jnp.where(lane == 0, 0.0, pltpu.roll(x, 1, 1))
            right = jnp.where(lane == plan.cols - 1, 0.0, pltpu.roll(x, plan.cols - 1, 1))
            return left, right

        def smooth(src, dst, low, count, masked):
            def step(i, carry):
                base = pl.multiple_of(low + i * 8, 8)
                value = src[pl.ds(base - 8, 24), :]
                kap = kx[pl.ds(base - 8, 24), :]
                mid, k_mid = value[8:16], kap[8:16]
                left, right = sides(mid)
                k_left, k_right = sides(k_mid)
                new = conducted(
                    mid, value[7:15], value[9:17], left, right, k_mid, kap[7:15], kap[9:17], k_left, k_right
                )
                if masked:
                    n = row + base
                    bad = ((n < PAD) & (place == first)) | ((n >= PAD + h) & (place == last))
                    new = jnp.where(bad, 0.0, new)
                if masked:
                    dst[pl.ds(base, 8), :] = new
                else:
                    at = pl.ds(base - PAD, 8)
                    if not keep:
                        outs[0][at, :] = -new
                        return carry
                    for b in range(blocks):
                        outs[0][plan.slot(b), at, :] = -new[:, b * INNER : (b + 1) * INNER]
                    kept[pl.ds(base - PAD, 8), :] = -new
                return carry

            lax.fori_loop(0, count, step, 0)

        refs = [h0, h1]
        for n in range(SMOOTH):
            if n < SMOOTH - 1:
                smooth(refs[n % 2], refs[(n + 1) % 2], PAD - 8, (h + 16) // 8, True)
            else:
                smooth(refs[n % 2], refs[(n + 1) % 2], PAD, h // 8, False)
        if keep:
            for s, out in enumerate(outs[1:]):
                c = lax.rem(me[1] + s, plan.cross)
                lanes = pl.ds(pl.multiple_of(c * plan.cols_here, plan.cols_here), plan.cols_here)
                out[...] = kept[:, lanes]

    tall = pltpu.VMEM((h + 2 * PAD, plan.cols), F32)
    flat = (h, plan.cols)
    if keep:
        outs = [jax.ShapeDtypeStruct((plan.devices, h, plan.width), F32)]
        outs += [jax.ShapeDtypeStruct((h, plan.cols_here), F32)] * plan.cross
    else:
        outs = [jax.ShapeDtypeStruct(flat, F32)]
    return call(body, outs, [tall] * 3 + [pltpu.VMEM(flat, F32)], (), () if keep else (0,))(
        kappa, above, below, part, beside, *rest
    )


def rows_heat(plan, dft, table, received, alpha):
    width = plan.width

    def body(dft, table, received, alpha, heat, edge_left, edge_right, xh, z, dep):
        def write(a, off, value):
            deposit = alpha[...] * (value[0] * value[0] + value[1] * value[1])
            rows = pl.ds(a * INNER + off, CHUNK)
            dep[rows, 0:width], dep[rows, width : 2 * width] = split(deposit)

        along_rows(functools.partial(plan.flip_a, received), write, dft, table, xh, z)
        tile = 2 * INNER
        ones = lower_ones(tile)
        carry = jnp.zeros((1, width), F32)
        for g in range(plan.rows // tile):
            both = jnp.dot(ones, dep[g * tile : (g + 1) * tile, :], preferred_element_type=F32)
            value = both[:, :width] + both[:, width:] + carry
            heat[g * tile : (g + 1) * tile, :] = value
            carry = value[tile - 1 : tile, :]
        for g in range(plan.rows // INNER):
            plan.edges(heat[g * INNER : (g + 1) * INNER, :], edge_left, edge_right, g * INNER)

    edge = jax.ShapeDtypeStruct((8, plan.rows), F32)
    outs = [jax.ShapeDtypeStruct((plan.rows, width), F32), edge, edge]
    scratch = plan.work_a() + [pltpu.VMEM((plan.rows, 2 * width), BF16)]
    return call(body, outs, scratch, (0, 1, 2), ())(dft, table, received, alpha)


def rows_turn(plan, read_field, wide, dft, table, screen, field):
    def body(dft, table, screen, field, out, *work):
        def read(a, off):
            return screened(read_field(field, a, off), screen[pl.ds(a * INNER + off, CHUNK), :])

        along_rows(read, functools.partial(plan.send_a, out), dft, table, *work)
        if wide:
            plan.send_edges(out)

    out = plan.sent_wide if wide else plan.sent
    return call(body, [out], plan.work_a(), (0, 1, 2), (0,))(dft, table, screen, field)[0]


def rows_smooth(plan, heat, from_left, from_right, kappa, kappa_left, kappa_right, me):
    width = plan.width
    PAD = 8
    step_rows = 32

    def body(heat, from_left, from_right, kappa, kappa_left, kappa_right, me, screen, h0, h1, kx):
        place = me[1] * plan.wind + plan.local(me[0], me[1])
        zeros = jnp.zeros((PAD, 2 * width), F32)
        for ref in (h0, h1, kx):
            ref[0:PAD, :] = zeros
            ref[plan.rows + PAD : plan.rows + 2 * PAD, :] = zeros
        for g in range(plan.rows // INNER):
            n = slice(g * INNER, (g + 1) * INNER)
            spot = slice(PAD + g * INNER, PAD + (g + 1) * INNER)
            for ref, value, left, right in ((h0, heat, from_left, from_right), (kx, kappa, kappa_left, kappa_right)):
                ref[spot, 0:width] = value[n, :]
                beside = [right[:, n], jnp.zeros((width - 16, INNER), F32), left[:, n]]
                ref[spot, width : 2 * width] = jnp.concatenate(beside, axis=0).T
        wide = lax.broadcasted_iota(jnp.int32, (step_rows, 2 * width), 1)
        bad = (wide >= width) & (wide < width + width // 2) & (place == plan.devices - 1)
        bad = bad | ((wide >= width + width // 2) & (place == 0))

        def smooth(src, dst):
            def one(base):
                value = src[pl.ds(base, step_rows + 16), :]
                kap = kx[pl.ds(base, step_rows + 16), :]
                mid, k_mid = value[8:-8], kap[8:-8]
                new = conducted(
                    mid, value[7:-9], value[9:-7], pltpu.roll(mid, 1, 1), pltpu.roll(mid, 2 * width - 1, 1),
                    k_mid, kap[7:-9], kap[9:-7], pltpu.roll(k_mid, 1, 1), pltpu.roll(k_mid, 2 * width - 1, 1),
                )
                dst(base, jnp.where(bad, 0.0, new))

            def step(i, carry):
                for n in range(4):
                    one(pl.multiple_of((4 * i + n) * step_rows, step_rows))
                return carry

            lax.fori_loop(0, plan.rows // (4 * step_rows), step, 0)

        def into(ref):
            def put(base, value):
                ref[pl.ds(base + PAD, step_rows), :] = value

            return put

        def into_screen(base, value):
            screen[pl.ds(base, step_rows), :] = -value[:, :width]

        refs = [h0, h1]
        for n in range(SMOOTH):
            smooth(refs[n % 2], into(refs[(n + 1) % 2]) if n < SMOOTH - 1 else into_screen)

    tall = pltpu.VMEM((plan.rows + 2 * PAD, 2 * width), F32)
    outs = [jax.ShapeDtypeStruct((plan.rows, width), F32)]
    return call(body, outs, [tall] * 3, (), (0,))(heat, from_left, from_right, kappa, kappa_left, kappa_right, me)[0]


def next_prev(value_up, value_down, axes, order):
    up = list(zip(order[:-1], order[1:]))
    down = [(j, i) for i, j in up]
    return lax.ppermute(value_up, axes, up), lax.ppermute(value_down, axes, down)


def extended(shard, sides, width):
    for axis, dim in sides:
        size, length = (lax.axis_size(axis), shard.shape[dim])
        up = [(i, (i + 1) % size) for i in range(size - 1)]
        down = [(j, i) for i, j in up]
        last = lax.slice_in_dim(shard, length - width, length, axis=dim)
        initial = lax.slice_in_dim(shard, 0, width, axis=dim)
        before = lax.ppermute(last, axis, up)
        after = lax.ppermute(initial, axis, down)
        shard = jnp.concatenate([before, shard, after], axis=dim)
    return shard


def carried_in(part, axis, combine, identity):
    place = lax.axis_index(axis)
    gathered = lax.all_gather(part, axis)
    state = jnp.zeros_like(part) + jnp.asarray(identity, part.dtype)

    def one(turn, state):
        return combine(state, lax.dynamic_index_in_dim(gathered, turn, 0, False))

    return lax.fori_loop(0, place, one, state)


def signed_freq(indices, length):
    shifted = jnp.where(indices < length // 2, indices, indices - length)
    return shifted.astype(jnp.float32) / length


def trig_table(first_ids, second_ids, length, sign_value):
    product = first_ids * second_ids % length
    phase_angle = product.astype(jnp.float32) * (sign_value * 2.0 * math.pi / length)
    return (jnp.cos(phase_angle), jnp.sin(phase_angle))


def complex_product(formula, real_part, imag_part, cosine, sine):
    highest = lax.Precision.HIGHEST
    out_real = jnp.einsum(formula, real_part, cosine, precision=highest) - jnp.einsum(
        formula, imag_part, sine, precision=highest
    )
    out_imag = jnp.einsum(formula, real_part, sine, precision=highest) + jnp.einsum(
        formula, imag_part, cosine, precision=highest
    )
    return (out_real, out_imag)


def transform(stacked, axis_dim, inverse):
    full_shape = stacked.shape
    length = full_shape[axis_dim]
    inner_len = math.gcd(length, 128)
    outer_len = length // inner_len
    leading = full_shape[1] if axis_dim == 2 else 1
    trailing = full_shape[2] if axis_dim == 1 else 1
    blocks = stacked.reshape(2, leading, outer_len, inner_len, trailing)
    sign_value = 1.0 if inverse else -1.0
    outer_ids = jnp.arange(outer_len, dtype=jnp.int32)
    inner_ids = jnp.arange(inner_len, dtype=jnp.int32)
    cos_outer, sin_outer = trig_table(outer_ids[:, None], outer_ids[None, :], outer_len, sign_value)
    first_real, first_imag = complex_product(
        "pabq,ak->pkbq", blocks[0], blocks[1], cos_outer, sin_outer
    )
    cos_twist, sin_twist = trig_table(outer_ids[:, None], inner_ids[None, :], length, sign_value)
    cos_twist = cos_twist[None, :, :, None]
    sin_twist = sin_twist[None, :, :, None]
    twist_real = first_real * cos_twist - first_imag * sin_twist
    twist_imag = first_real * sin_twist + first_imag * cos_twist
    cos_inner, sin_inner = trig_table(inner_ids[:, None], inner_ids[None, :], inner_len, sign_value)
    second_real, second_imag = complex_product(
        "pkbq,bm->pkmq", twist_real, twist_imag, cos_inner, sin_inner
    )
    result = jnp.stack([second_real, second_imag]).transpose(0, 1, 3, 2, 4).reshape(full_shape)
    if inverse:
        result = result * (1.0 / length)
    return result


def apply_phase(stacked, phase_angle):
    cosine = jnp.cos(phase_angle)
    sine = jnp.sin(phase_angle)
    return jnp.stack(
        [stacked[0] * cosine - stacked[1] * sine, stacked[0] * sine + stacked[1] * cosine]
    )


def along_joint(stacked, phase_rate, row_freq, col_freq):
    cross_count = lax.axis_size("cross")
    stacked = lax.all_to_all(stacked, ("wind", "cross"), split_axis=2, concat_axis=1, tiled=True)
    stacked = transform(stacked, 1, False)
    col_width = stacked.shape[2]
    joint_block = lax.axis_index("wind") * cross_count + lax.axis_index("cross")
    cols_held = lax.dynamic_slice_in_dim(col_freq, joint_block * col_width, col_width)
    phase_angle = -phase_rate * (
        row_freq[:, None] * row_freq[:, None] + cols_held[None, :] * cols_held[None, :]
    )
    stacked = apply_phase(stacked, phase_angle)
    stacked = transform(stacked, 1, True)
    return lax.all_to_all(stacked, ("wind", "cross"), split_axis=1, concat_axis=2, tiled=True)


def propagate_slab(slab_pair, share_step):
    rows_total = slab_pair.shape[1] * lax.axis_size("wind") * lax.axis_size("cross")
    cols_total = slab_pair.shape[2]
    phase_rate = share_step * diffraction
    row_freq = signed_freq(jnp.arange(rows_total, dtype=jnp.int32), rows_total)
    col_freq = signed_freq(jnp.arange(cols_total, dtype=jnp.int32), cols_total)
    stacked = transform(slab_pair, 2, False)
    stacked = along_joint(stacked, phase_rate, row_freq, col_freq)
    return transform(stacked, 2, True)


def conduct_core(padded, kappa_pad):
    height = padded.shape[0] - 2
    breadth = padded.shape[1] - 2
    center = padded[1:-1, 1:-1]
    kappa_mid = kappa_pad[1:-1, 1:-1]
    flux_sum = jnp.zeros_like(center)
    for offset_row, offset_col in ((0, 1), (2, 1), (1, 0), (1, 2)):
        neighbour = padded[offset_row : offset_row + height, offset_col : offset_col + breadth]
        kappa_side = kappa_pad[offset_row : offset_row + height, offset_col : offset_col + breadth]
        flux_sum = flux_sum + 0.5 * (kappa_mid + kappa_side) * (neighbour - center)
    return center + conduct_rate * flux_sum


def add_terms(earlier, later_term):
    return earlier + later_term


def layer_absorption(index_row, table_row, level_ids):
    one_hot = (index_row[:, None] == level_ids[None, :]).astype(jnp.float32)
    return jnp.sum(one_hot * table_row[None, :], axis=1)


def wide_device(field_real, field_imag, absorb_index, absorb_table, zone_map, zone_conductivity):
    rows_here, cols_here = field_real.shape
    conductivity = jnp.zeros((rows_here, cols_here), jnp.float32)
    for zone_no in range(zone_conductivity.shape[0]):
        conductivity = jnp.where(zone_map == zone_no, zone_conductivity[zone_no], conductivity)
    level_ids = jnp.arange(absorb_table.shape[1], dtype=jnp.int32)
    combined = lax.all_to_all(
        jnp.stack([field_real, field_imag, conductivity]),
        "cross",
        split_axis=1,
        concat_axis=2,
        tiled=True,
    )
    slab_pair = combined[:2]
    kappa_rows = extended(combined[2], ((("wind", "cross"), 0),), 1)
    kappa_pad = jnp.pad(kappa_rows, ((0, 0), (1, 1)))
    index_full = lax.all_gather(absorb_index, "cross", axis=1, tiled=True)
    slab_rows = slab_pair.shape[1]
    rows_total = slab_rows * lax.axis_size("wind") * lax.axis_size("cross")
    slab_ids = jnp.arange(slab_rows, dtype=jnp.int32)
    lower_slab = (slab_ids[:, None] >= slab_ids[None, :]).astype(jnp.float32)
    screen_phase = jnp.zeros((slab_rows, slab_pair.shape[2]), jnp.float32)
    for layer_no in range(LAYERS):
        absorption = layer_absorption(index_full[layer_no], absorb_table[layer_no], level_ids)
        screen_phase = jnp.zeros((slab_rows, slab_pair.shape[2]), jnp.float32)
        for _ in range(ITERS):
            middle = propagate_slab(apply_phase(slab_pair, screen_phase), 0.5)
            intensity = middle[0] * middle[0] + middle[1] * middle[1]
            deposit = absorption[None, :] * intensity * (1.0 / rows_total)
            partial_heat = jnp.dot(lower_slab, deposit, precision=lax.Precision.HIGHEST)
            totals = partial_heat[-1]
            upstream = carried_in(totals, ("wind", "cross"), add_terms, jnp.zeros_like(totals))
            heat_field = partial_heat + upstream[None, :]
            for _ in range(SMOOTH):
                padded = extended(heat_field, ((("wind", "cross"), 0),), 1)
                padded = jnp.pad(padded, ((0, 0), (1, 1)))
                heat_field = conduct_core(padded, kappa_pad)
            screen_phase = -heat_field
        slab_pair = propagate_slab(apply_phase(slab_pair, screen_phase), 1.0)
    returned = lax.all_to_all(
        jnp.stack([slab_pair[0], slab_pair[1], screen_phase]),
        "cross",
        split_axis=2,
        concat_axis=1,
        tiled=True,
    )
    return (returned[0], returned[1], returned[2])


def on_device(field_real, field_imag, absorb_index, absorb_table, zone_map, zone_conductivity):
    plan = Plan(*field_real.shape, lax.axis_size("wind"), lax.axis_size("cross"))
    fits = plan.width == INNER and INNER % plan.height == 0 and plan.height % CHUNK == 0
    if not fits or plan.rows_here % INNER or plan.rows % (2 * INNER):
        return wide_device(field_real, field_imag, absorb_index, absorb_table, zone_map, zone_conductivity)
    return tiled_device(plan, field_real, field_imag, absorb_index, absorb_table, zone_map, zone_conductivity)


def tiled_device(plan, field_real, field_imag, absorb_index, absorb_table, zone_map, zone_conductivity):
    cross = plan.cross
    w, c = lax.axis_index("wind"), lax.axis_index("cross")
    place = jnp.stack([w, c]).astype(jnp.int32)
    grid_axes = ("wind", "cross")
    columns_order = [plan.slot(i) for i in range(plan.devices)]

    def exchange(x, axes):
        return lax.all_to_all(x, axes, split_axis=0, concat_axis=0, tiled=True)

    def flip(x):
        return exchange(x, grid_axes)

    to_b, *field_blocks = prepare_field(plan, field_real, field_imag, place)
    home_b = exchange(to_b, "cross")
    field_blocks = shifted(field_blocks, "wind")
    *blocks, alpha_a = prepare(plan, zone_map, absorb_index, absorb_table, zone_conductivity, place)

    dft = jnp.asarray(dft_matrices())
    tab_a = lambda share: (jnp.asarray(row_blocks(plan.rows, share)), jnp.asarray(row_table(plan.rows)))
    tab_b = lambda *shares: jnp.asarray(chirp_columns(plan.cols, shares))

    def smooth_a(layer, share, received):
        heat, left, right = rows_heat(plan, *tab_a(share), received, alpha_a[layer : layer + 1])
        from_left, from_right = next_prev(right, left, grid_axes, columns_order)
        return rows_smooth(plan, heat, from_left, from_right, *kappas, place)

    def smooth_b(layer, keep, received):
        part, beside, totals = cols_heat(plan, layer, plan.devices, dft, tab_b(0.5), received, alpha_b)
        return cols_smooth(plan, keep, kappa_b, above, below, part, beside, flip(totals), place)

    home_b, across = lax.optimization_barrier((home_b, blocks[:cross]))
    sent = cols_send(plan, plan.home_b, False, dft, tab_b(0.5), home_b)
    kappa_b, alpha_b = home_rows(plan, shifted(across, "cross"), place)
    above, below = next_prev(kappa_b[-8:], kappa_b[:8], grid_axes, list(range(plan.devices)))
    received, along = lax.optimization_barrier((flip(sent), blocks[cross:]))
    along = shifted(along, "wind")
    kappa_a, left, right = rows_kappa(plan, along, place)
    kappas = (kappa_a, *next_prev(right, left, grid_axes, columns_order))
    home_a = in_order(field_blocks, place, 0)
    screen = smooth_a(0, 0.5, received)
    sent = rows_turn(plan, plan.home_a, True, *tab_a(0.5), screen, home_a)
    received, above, below = lax.optimization_barrier((flip(sent), above, below))
    (screen,) = smooth_b(0, False, received)
    sent_middle, sent_field = cols_turn(plan, plan.home_b, 2, dft, tab_b(1.5, 1.0), screen, home_b)
    middle = flip(sent_middle)
    field = flip(sent_field)
    screen = smooth_a(1, 1.5, middle)
    field, screen = lax.optimization_barrier((field, screen))
    field = rows_field(plan, plan.flip_a, *tab_a(1.0), field)
    sent = rows_turn(plan, plan.flip_a, True, *tab_a(0.5), screen, field)
    screen, *home_parts = smooth_b(1, True, flip(sent))
    screen, home_parts = lax.optimization_barrier((flip(screen), home_parts))
    screen = screen.reshape(plan.rows, plan.width)
    sent = rows_turn(plan, plan.flip_a, False, *tab_a(1.0), screen, field)
    back = cols_send(plan, plan.flip_b, True, dft, tab_b(1.0), flip(sent))
    screen = home_screen(plan, shifted(home_parts, "cross"), place)
    back = exchange(back, "cross")
    out_real = back[:, : plan.height].reshape(field_real.shape)
    out_imag = back[:, plan.height :].reshape(field_real.shape)
    return (out_real, out_imag, screen)


def solution(mesh):
    in_specs = (
        P(("beams", "wind"), "cross"),
        P(("beams", "wind"), "cross"),
        P(None, "cross"),
        P(),
        P("wind", "cross"),
        P(),
    )
    out_specs = (
        P(("beams", "wind"), "cross"),
        P(("beams", "wind"), "cross"),
        P(("beams", "wind"), "cross"),
    )
    return jax.shard_map(on_device, mesh=mesh, in_specs=in_specs, out_specs=out_specs, check_vma=False)
```

```python
import functools
import math

import jax
import jax.numpy as jnp
import numpy as np
from jax import lax
from jax.experimental import pallas as pl
from jax.experimental.pallas import tpu as pltpu
from jax.sharding import PartitionSpec as P


LAYERS = 2
ITERS = 2
SMOOTH = 2
INNER = 128
CHUNK = 16

diffraction = 2000.0
conduct_rate = 0.24

F32 = jnp.float32
BF16 = jnp.bfloat16
WHOLE = pl.BlockSpec(memory_space=pltpu.VMEM)
SCALAR = pl.BlockSpec(memory_space=pltpu.SMEM)


def split_np(values):
    high = values.astype(np.float32).astype(jnp.bfloat16)
    low = (values - high.astype(np.float64)).astype(np.float32).astype(jnp.bfloat16)
    return high, low


def dft_matrices():
    ids = np.arange(INNER)
    angle = 2.0 * np.pi * (np.outer(ids, ids) % INNER) / INNER
    cosine, sine = np.cos(angle), np.sin(angle)
    left = np.block([[cosine, sine], [-sine, cosine]])
    return np.stack([*split_np(left), *split_np(left.T)])


def chirp_columns(length, shares):
    outer = length // INNER
    k = np.arange(outer)[:, None]
    m = np.arange(INNER)[None, :]
    twist = -2.0 * np.pi * ((k * m) % length) / length
    tables = [np.cos(twist), np.sin(twist)]
    p = k + outer * m
    freq = np.where(p < length // 2, p, p - length) / length
    for share in shares:
        angle = -share * diffraction * freq * freq
        tables += [np.cos(angle) / length, np.sin(angle) / length]
    return np.concatenate(tables, axis=0).astype(np.float32)


def row_table(length):
    cols = chirp_columns(length, ()).T
    return np.pad(cols, ((0, 0), (0, -cols.shape[1] % 128)))


def row_blocks(length, share):
    outer = length // INNER
    ids = np.arange(INNER)
    forward = np.exp(-2j * np.pi * (np.outer(ids, ids) % INNER) / INNER)
    blocks = []
    for k in range(outer):
        p = k + outer * ids
        freq = np.where(p < length // 2, p, p - length) / length
        block = forward.conj() @ (np.exp(-1j * share * diffraction * freq * freq)[:, None] / length * forward)
        blocks.append(np.stack(split_np(np.block([[block.real, -block.imag], [block.imag, block.real]]))))
    return np.stack(blocks)


def split(x):
    high = x.astype(BF16)
    return high, (x - high.astype(F32)).astype(BF16)


def times(a, b):
    return (a[0] * b[0] - a[1] * b[1], a[0] * b[1] + a[1] * b[0])


def small_fft(points, sign):
    count = len(points)
    if count == 1:
        return points
    even = small_fft(points[0::2], sign)
    odd = small_fft(points[1::2], sign)
    half = count // 2
    out = [None] * count
    for k in range(half):
        re, im = odd[k]
        if k == 0:
            turn = (re, im)
        elif 4 * k == count:
            turn = (-im, re) if sign > 0 else (im, -re)
        elif 8 * k == count:
            root = math.sqrt(0.5)
            turn = (root * (re - im), root * (im + re)) if sign > 0 else (root * (re + im), root * (im - re))
        elif 8 * k == 3 * count:
            root = math.sqrt(0.5)
            turn = (-root * (re + im), root * (re - im)) if sign > 0 else (root * (im - re), -root * (re + im))
        else:
            c = math.cos(2.0 * math.pi * k / count)
            s = sign * math.sin(2.0 * math.pi * k / count)
            turn = (c * re - s * im, s * re + c * im)
        out[k] = (even[k][0] + turn[0], even[k][1] + turn[1])
        out[k + half] = (even[k][0] - turn[0], even[k][1] - turn[1])
    return out


def cos_sin(x):
    turns = jnp.floor(x * (2.0 / math.pi) + 0.5)
    r = ((x - turns * 1.5703125) - turns * 4.837512969970703125e-4) - turns * 7.549789954891882e-8
    quad = turns.astype(jnp.int32)
    z = r * r
    s = r + r * z * (-1.6666654611e-1 + z * (8.3321608736e-3 - z * 1.9515295891e-4))
    c = 1.0 - 0.5 * z + z * z * (4.166664568298827e-2 + z * (-1.388731625493765e-3 + z * 2.443315711809948e-5))
    odd = (quad & 1) == 1
    sin_x = jnp.where(odd, c, s)
    cos_x = jnp.where(odd, s, c)
    sin_x = jnp.where((quad & 2) == 2, -sin_x, sin_x)
    cos_x = jnp.where(((quad + 1) & 2) == 2, -cos_x, cos_x)
    return cos_x, sin_x


def screened(value, screen):
    return times(value, cos_sin(screen))


def triple(a_high, a_low, b_high, b_low):
    dot = functools.partial(jnp.dot, preferred_element_type=F32)
    return dot(a_high, b_high) + dot(a_high, b_low) + dot(a_low, b_high)


def lower_ones(size):
    r = lax.broadcasted_iota(jnp.int32, (size, size), 0)
    c = lax.broadcasted_iota(jnp.int32, (size, size), 1)
    return jnp.where(r >= c, 1.0, 0.0).astype(BF16)


def chunks(count, body):
    def step(i, carry):
        body(pl.multiple_of(i * CHUNK, CHUNK))
        return carry

    lax.fori_loop(0, count // CHUNK, step, 0)


def along_rows(read, write, matrices, table, xh, z):
    outer = matrices.shape[0]
    width = z.shape[1] // outer
    lanes = lambda k: pl.ds(k * width, width)
    col = lambda part, off: table[pl.ds(off, CHUNK), part : part + 1]

    def first(off):
        for k, value in enumerate(small_fft([read(a, off) for a in range(outer)], -1)):
            if k:
                value = times(value, (col(k, off), col(outer + k, off)))
            for at, v in ((0, value[0]), (INNER, value[1])):
                high, low = split(v)
                xh[pl.ds(at + off, CHUNK), pl.ds(2 * k * width, width)] = high
                xh[pl.ds(at + off, CHUNK), pl.ds((2 * k + 1) * width, width)] = low

    def last(off):
        values = []
        for k in range(outer):
            value = (z[pl.ds(off, CHUNK), lanes(k)], z[pl.ds(INNER + off, CHUNK), lanes(k)])
            if k:
                value = times(value, (col(k, off), -col(outer + k, off)))
            values.append(value)
        for a, value in enumerate(small_fft(values, 1)):
            write(a, off, value)

    chunks(INNER, first)
    dot = functools.partial(jnp.dot, preferred_element_type=F32)
    for k in range(outer):
        both = dot(matrices[k, 0], xh[:, 2 * k * width : (2 * k + 2) * width])
        low = dot(matrices[k, 1], xh[:, 2 * k * width : (2 * k + 1) * width])
        z[:, k * width : (k + 1) * width] = both[:, :width] + both[:, width:] + low
    chunks(INNER, last)


def along_cols(main, read, writes, dft, table, xh, xl, y, z):
    outer = table.shape[0] // (2 * (1 + len(writes)))
    height = xh.shape[0] // outer

    def every(body):
        chunks(main, body)
        if height > main:
            body(main)

    row = lambda part: table[part : part + 1, :]

    def put(k, off, value):
        for at, v in ((0, value[0]), (INNER, value[1])):
            spot = (pl.ds(k * height + off, CHUNK), pl.ds(at, INNER))
            xh[spot], xl[spot] = split(v)

    def get(ref, k, off):
        return tuple(ref[pl.ds(k * height + off, CHUNK), pl.ds(at, INNER)] for at in (0, INNER))

    def first(off):
        for k, value in enumerate(small_fft([read(b, off) for b in range(outer)], -1)):
            if k:
                value = times(value, (row(k), row(outer + k)))
            put(k, off, value)

    every(first)
    y[...] = triple(xh[...], xl[...], dft[2], dft[3])
    for n, write in enumerate(writes):

        def middle(off, n=n):
            for k in range(outer):
                base = (2 + 2 * n) * outer + k
                put(k, off, times(get(y, k, off), (row(base), row(base + outer))))

        every(middle)
        z[...] = triple(xh[...], xl[...], dft[0], dft[1])

        def last(off, write=write):
            values = []
            for k in range(outer):
                value = get(z, k, off)
                if k:
                    value = times(value, (row(k), -row(outer + k)))
                values.append(value)
            for b, value in enumerate(small_fft(values, 1)):
                write(b, off, value)

        every(last)


class Plan:
    def __init__(self, rows_here, cols_here, wind, cross):
        self.wind, self.cross = wind, cross
        self.devices = wind * cross
        self.rows_here, self.cols_here = rows_here, cols_here
        self.height = rows_here // cross
        self.width = cols_here // wind
        self.rows, self.cols = rows_here * wind, cols_here * cross

    def local(self, w, c):
        return w + (c % 2) * (self.wind - 1 - 2 * w)

    def slot(self, block):
        c, i = block // self.wind, block % self.wind
        return self.local(i, c) * self.cross + c

    def home_a(self, ref, a, off):
        n = a * INNER
        src, at = n // self.rows_here, n % self.rows_here
        return tuple(ref[src, pl.ds(p * self.rows_here + at + off, CHUNK), :] for p in (0, 1))

    def spot_a(self, a, off):
        per = INNER // self.height
        return a * per + off // self.height, lax.rem(off, self.height)

    def flip_a(self, ref, a, off):
        s, at = self.spot_a(a, off)
        at = pl.multiple_of(at, CHUNK)
        return tuple(ref[s, pl.ds(p * self.height + at, CHUNK), :] for p in (0, 1))

    def send_a(self, ref, a, off, value):
        s, at = self.spot_a(a, off)
        at = pl.multiple_of(at, CHUNK)
        for p in (0, 1):
            ref[s, pl.ds(p * self.height + at, CHUNK), :] = value[p]

    def send_edges(self, ref):
        h = self.height
        for d in range(self.devices):
            for p in (0, 1):
                at = 2 * h + 4 * p
                before = ref[d - 1, p * h + h - 2 : p * h + h, :] if d else jnp.zeros((2, self.width), F32)
                after = ref[d + 1, p * h : p * h + 2, :] if d + 1 < self.devices else jnp.zeros((2, self.width), F32)
                ref[d, at : at + 2, :] = before
                ref[d, at + 2 : at + 4, :] = after

    def edges(self, value, left, right, at):
        turned = value.T
        left[:, at : at + INNER] = turned[0:8, :]
        right[:, at : at + INNER] = turned[self.width - 8 : self.width, :]

    def home_b(self, ref, b, off):
        per = self.cols_here // INNER
        return tuple(ref[b // per, pl.ds(p * self.height + off, CHUNK), pl.ds((b % per) * INNER, INNER)] for p in (0, 1))

    def wide_b(self, ref, b, off):
        if isinstance(off, int):
            extra = ref[self.slot(b), 2 * self.height : 2 * self.height + 8, :]
            turned = jnp.concatenate([extra[4:8], extra[0:4]], axis=0)
            return jnp.concatenate([extra, extra], axis=0), jnp.concatenate([turned, turned], axis=0)
        return self.flip_b(ref, b, off)

    def flip_b(self, ref, b, off):
        return tuple(ref[self.slot(b), pl.ds(p * self.height + off, CHUNK), :] for p in (0, 1))

    def send_b(self, ref, b, off, value):
        for p in (0, 1):
            ref[self.slot(b), pl.ds(p * self.height + off, CHUNK), :] = value[p]

    def back_b(self, ref, b, off, value):
        per = self.cols_here // INNER
        for p in (0, 1):
            ref[b // per, pl.ds(p * self.height + off, CHUNK), pl.ds((b % per) * INNER, INNER)] = value[p]

    @property
    def sent(self):
        return jax.ShapeDtypeStruct((self.devices, 2 * self.height, self.width), F32)

    def work_a(self):
        wide = (self.rows // INNER) * self.width
        return [
            pltpu.VMEM((2 * INNER, 2 * wide), BF16),
            pltpu.VMEM((2 * INNER, wide), F32),
        ]

    @property
    def sent_wide(self):
        return jax.ShapeDtypeStruct((self.devices, 2 * self.height + 8, self.width), F32)

    def work_b(self, extra=0):
        tall = (self.cols // INNER) * (self.height + extra)
        return [
            pltpu.VMEM((tall, 2 * INNER), BF16),
            pltpu.VMEM((tall, 2 * INNER), BF16),
            pltpu.VMEM((tall, 2 * INNER), F32),
            pltpu.VMEM((tall, 2 * INNER), F32),
        ]


def call(body, outs, scratch, near=(), near_outs=(), far=()):
    def run(*args):
        specs = [SCALAR if a.size <= 16 else WHOLE for a in args]
        spaces = [pltpu.VMEM if i in near else pltpu.HBM if i in far else None for i in range(len(args))]
        args = [pltpu.with_memory_space_constraint(a, space) if space else a for a, space in zip(args, spaces)]
        return pl.pallas_call(
            body,
            out_shape=[pltpu.VMEM(o.shape, o.dtype) if i in near_outs else o for i, o in enumerate(outs)],
            in_specs=specs,
            out_specs=[WHOLE] * len(outs),
            scratch_shapes=scratch,
            compiler_params=pltpu.CompilerParams(vmem_limit_bytes=14 * 1024 * 1024),
        )(*args)

    return run


def prepare_field(plan, field_real, field_imag, place):
    h = plan.height

    def body(real, imag, place, to_b, *to_a):
        for c in range(plan.cross):
            to_b[c, 0:h, :] = real[c * h : (c + 1) * h, :]
            to_b[c, h : 2 * h, :] = imag[c * h : (c + 1) * h, :]
        for t, out in enumerate(to_a):
            n = lax.rem(place[0] + t, plan.wind)
            lanes = pl.ds(pl.multiple_of(plan.local(n, place[1]) * plan.width, plan.width), plan.width)
            out[0 : plan.rows_here, :] = real[:, lanes]
            out[plan.rows_here : 2 * plan.rows_here, :] = imag[:, lanes]

    outs = [jax.ShapeDtypeStruct((plan.cross, 2 * h, plan.cols_here), F32)]
    outs += [jax.ShapeDtypeStruct((2 * plan.rows_here, plan.width), F32)] * plan.wind
    return call(body, outs, [], (), (), (0, 1))(field_real, field_imag, place)


def prepare(plan, zone_map, absorb_index, absorb_table, zone_conductivity, place):
    h = plan.height

    def picked(ids, count, level):
        value = jnp.zeros(ids.shape, F32)
        for n in range(count):
            value = jnp.where(ids == n, level(n), value)
        return value

    def body(zones, index, table, levels, place, *refs):
        to_b, (kappa, left, right, alpha_a, alpha) = refs[: plan.cross], refs[plan.cross :]
        w, c = place[0], place[1]

        def step(off):
            kappa[pl.ds(off, CHUNK), :] = picked(zones[pl.ds(off, CHUNK), :], levels.shape[0], lambda n: levels[n])

        chunks(plan.rows_here, step)
        alpha[...] = jnp.zeros_like(alpha)
        for layer in range(LAYERS):
            value = picked(index[layer : layer + 1, :], table.shape[1], lambda n: table[layer, n])
            alpha[layer : layer + 1, :] = value * (1.0 / plan.rows)
        alpha_a[...] = alpha[:, pl.ds(pl.multiple_of(plan.local(w, c) * plan.width, plan.width), plan.width)]
        for s, out in enumerate(to_b):
            out[0:h, :] = kappa[pl.ds(pl.multiple_of(lax.rem(c + s, plan.cross) * h, h), h), :]
            out[h:, :] = alpha[...]
        for at in range(0, plan.rows_here, INNER):
            left[:, at : at + INNER] = kappa[at : at + INNER, 0 : plan.width].T[0:8, :]
            right[:, at : at + INNER] = kappa[at : at + INNER, plan.cols_here - plan.width :].T[plan.width - 8 :, :]

    edge = jax.ShapeDtypeStruct((8, plan.rows_here), F32)
    outs = [jax.ShapeDtypeStruct((h + 8, plan.cols_here), F32)] * plan.cross
    outs += [jax.ShapeDtypeStruct(zone_map.shape, F32), edge, edge, jax.ShapeDtypeStruct((8, plan.width), F32)]
    scratch = [pltpu.VMEM((8, plan.cols_here), F32)]
    return call(body, outs, scratch, (), (), (0,))(zone_map, absorb_index, absorb_table, zone_conductivity, place)


def home_kappa(plan, kappa, from_left, from_right, place):
    per = plan.rows_here // INNER

    def body(kappa, from_left, from_right, place, *refs):
        outs, edges = refs[: plan.wind], refs[-1]
        for at in range(per):
            n = slice(at * INNER, (at + 1) * INNER)
            edges[0, 8 * at : 8 * at + 8, :] = from_left[:, n]
            edges[plan.wind - 1, 8 * (per + at) : 8 * (per + at) + 8, :] = from_right[:, n]
            for i in range(plan.wind):
                turned = kappa[n, i * plan.width : (i + 1) * plan.width].T
                if i + 1 < plan.wind:
                    edges[i + 1, 8 * at : 8 * at + 8, :] = turned[plan.width - 8 :, :]
                if i:
                    edges[i - 1, 8 * (per + at) : 8 * (per + at) + 8, :] = turned[0:8, :]
        for t, out in enumerate(outs):
            i = plan.local(lax.rem(place[0] + t, plan.wind), place[1])
            out[0 : plan.rows_here, :] = kappa[:, pl.ds(pl.multiple_of(i * plan.width, plan.width), plan.width)]
            out[plan.rows_here :, :] = edges[i]

    outs = [jax.ShapeDtypeStruct((plan.rows_here + 16 * per, plan.width), F32)] * plan.wind
    scratch = [pltpu.VMEM((plan.wind, 16 * per, INNER), F32)]
    return call(body, outs, scratch)(kappa, from_left, from_right, place)


def home_rows(plan, parts, place):
    h = plan.height

    def body(*refs):
        place, kappa, alpha = refs[plan.cross :]
        for s, ref in enumerate(refs[: plan.cross]):
            c = lax.rem(place[1] + plan.cross - s, plan.cross)
            lanes = pl.ds(pl.multiple_of(c * plan.cols_here, plan.cols_here), plan.cols_here)
            kappa[:, lanes] = ref[0:h, :]
            alpha[:, lanes] = ref[h:, :]

    outs = [jax.ShapeDtypeStruct((h, plan.cols), F32), jax.ShapeDtypeStruct((8, plan.cols), F32)]
    return call(body, outs, [])(*parts, place)


def shifted(parts, axis):
    size = lax.axis_size(axis)
    return [parts[0]] + [lax.ppermute(parts[s], axis, [(i, (i + s) % size) for i in range(size)]) for s in range(1, size)]


def in_order(parts, place, which):
    size = len(parts)

    def body(*refs):
        place, out = refs[size], refs[-1]
        for s, ref in enumerate(refs[:size]):
            out[lax.rem(place[which] + size - s, size)] = ref[...]

    out = jax.ShapeDtypeStruct((size,) + parts[0].shape, F32)
    return call(body, [out], [], range(size))(*parts, place)[0]


def home_screen(plan, parts, place):
    h = plan.height

    def body(*refs):
        place, out = refs[plan.cross], refs[-1]
        for s, ref in enumerate(refs[: plan.cross]):
            c = lax.rem(place[1] + plan.cross - s, plan.cross)
            out[pl.ds(pl.multiple_of(c * h, h), h), :] = ref[...]

    out = jax.ShapeDtypeStruct((plan.rows_here, plan.cols_here), F32)
    return call(body, [out], [])(*parts, place)[0]


def rows_kappa(plan, parts, place):
    per = plan.rows_here // INNER

    def body(*refs):
        place, out, left, right = refs[plan.wind :]
        for t, ref in enumerate(refs[: plan.wind]):
            first = lax.rem(place[0] + plan.wind - t, plan.wind) * plan.rows_here
            out[pl.ds(pl.multiple_of(first, plan.rows_here), plan.rows_here), :] = ref[0 : plan.rows_here, :]
            for at in range(per):
                n = pl.ds(pl.multiple_of(first + at * INNER, INNER), INNER)
                line = plan.rows_here + 8 * at
                left[:, n] = ref[line : line + 8, :]
                right[:, n] = ref[line + 8 * per : line + 8 * per + 8, :]

    edge = jax.ShapeDtypeStruct((8, plan.rows), F32)
    outs = [jax.ShapeDtypeStruct((plan.rows, plan.width), F32), edge, edge]
    return call(body, outs, [], range(plan.wind))(*parts, place)


def rows_field(plan, read_field, dft, table, field):
    def body(dft, table, field, out, *work):
        along_rows(functools.partial(read_field, field), functools.partial(plan.send_a, out), dft, table, *work)

    return call(body, [plan.sent], plan.work_a(), (0, 1, 2), (0,))(dft, table, field)[0]


def cols_send(plan, read_field, back, dft, table, field):
    out = jax.ShapeDtypeStruct((plan.cross, 2 * plan.height, plan.cols_here), F32) if back else plan.sent

    def body(dft, table, field, out, *work):
        put = plan.back_b if back else plan.send_b
        along_cols(plan.height, functools.partial(read_field, field), [functools.partial(put, out)], dft, table, *work)

    return call(body, [out], plan.work_b(), (0, 1, 2), () if back else (0,))(dft, table, field)[0]


def cols_heat(plan, layer, copies, dft, table, received, absorption):
    blocks = plan.cols // INNER
    h = plan.height

    def body(dft, table, received, absorption, part, beside, totals, xh, xl, y, z, dh, dl):
        def write(b, off, value):
            alpha = absorption[layer : layer + 1, pl.ds(b * INNER, INNER)]
            deposit = alpha * (value[0] * value[0] + value[1] * value[1])
            lanes = pl.ds(b * INNER, INNER)
            if isinstance(off, int):
                beside[:, lanes] = deposit[0:8]
                return
            spot = (pl.ds(off, CHUNK), lanes)
            dh[spot], dl[spot] = split(deposit)

        along_cols(h, functools.partial(plan.wide_b, received), [write], dft, table, xh, xl, y, z)
        ones = lower_ones(h)
        dot = functools.partial(jnp.dot, preferred_element_type=F32)
        part[...] = dot(ones, dh[...]) + dot(ones, dl[...])
        for b in range(blocks):
            total = part[h - 1 : h, b * INNER : (b + 1) * INNER]
            for d in range(copies):
                totals[d, b : b + 1, :] = total

    outs = [
        jax.ShapeDtypeStruct((h, plan.cols), F32),
        jax.ShapeDtypeStruct((8, plan.cols), F32),
        jax.ShapeDtypeStruct((copies, blocks, INNER), F32),
    ]
    scratch = plan.work_b(CHUNK) + [pltpu.VMEM((h, plan.cols), BF16), pltpu.VMEM((h, plan.cols), BF16)]
    return call(body, outs, scratch, (0, 1, 2), ())(dft, table, received, absorption)


def conducted(mid, up, down, left, right, k_mid, k_up, k_down, k_left, k_right):
    flux = (k_mid + k_up) * (up - mid) + (k_mid + k_down) * (down - mid)
    flux = flux + (k_mid + k_left) * (left - mid) + (k_mid + k_right) * (right - mid)
    return mid + (0.5 * conduct_rate) * flux


def cols_turn(plan, read_field, sets, dft, table, screen, field):
    def body(dft, table, screen, field, *refs):
        outs, work = refs[:sets], refs[sets:]

        def read(b, off):
            return screened(read_field(field, b, off), screen[pl.ds(off, CHUNK), pl.ds(b * INNER, INNER)])

        along_cols(plan.height, read, [functools.partial(plan.send_b, out) for out in outs], dft, table, *work)

    return call(body, [plan.sent] * sets, plan.work_b(), (0, 1, 2), range(sets))(
        dft, table, screen, field
    )


def cols_smooth(plan, keep, kappa, above, below, part, beside, *rest):
    blocks = plan.cols // INNER
    h = plan.height
    PAD = 16
    first, last = 0, plan.devices - 1

    def body(kappa, above, below, part, beside, *refs):
        count = plan.cross + 1 if keep else 1
        sums, me, outs, (h0, h1, kx, kept) = refs[: -5 - count], refs[-5 - count], refs[-4 - count : -4], refs[-4:]
        place = me[0] * plan.cross + me[1]
        zeros = jnp.zeros((PAD, plan.cols), F32)
        for ref in (h0, kx, h1):
            ref[0:PAD, :] = zeros
            ref[h + PAD : h + 2 * PAD, :] = zeros
        kx[PAD - 8 : PAD, :] = above[...]
        kx[PAD : PAD + h, :] = kappa[...]
        kx[PAD + h : PAD + h + 8, :] = below[...]
        upstream = jnp.zeros((blocks, INNER), F32)
        if len(sums) == 1:
            for d in range(plan.devices):
                upstream = upstream + jnp.where(d < place, sums[0][d], 0.0)
        else:
            for s in range(1, plan.cross):
                upstream = upstream + jnp.where(s <= me[1], sums[s - 1][...], 0.0)
            for t in range(1, plan.wind):
                upstream = upstream + jnp.where(t <= me[0], sums[plan.cross + t - 2][...], 0.0)
        has_next = jnp.where(place < last, 1.0, 0.0)
        for b in range(blocks):
            lanes = slice(b * INNER, (b + 1) * INNER)
            base = upstream[b : b + 1, :]
            h0[PAD : PAD + h, lanes] = part[:, lanes] + base
            h0[PAD - 1 : PAD, lanes] = base
            h0[PAD - 2 : PAD - 1, lanes] = base - beside[1:2, lanes]
            value = base + part[h - 1 : h, lanes] + beside[2:3, lanes]
            h0[PAD + h : PAD + h + 1, lanes] = value * has_next
            h0[PAD + h + 1 : PAD + h + 2, lanes] = (value + beside[3:4, lanes]) * has_next
        lane = lax.broadcasted_iota(jnp.int32, (8, plan.cols), 1)
        row = lax.broadcasted_iota(jnp.int32, (8, plan.cols), 0)

        def sides(x):
            left = jnp.where(lane == 0, 0.0, pltpu.roll(x, 1, 1))
            right = jnp.where(lane == plan.cols - 1, 0.0, pltpu.roll(x, plan.cols - 1, 1))
            return left, right

        def smooth(src, dst, low, count, masked):
            def step(i, carry):
                base = pl.multiple_of(low + i * 8, 8)
                value = src[pl.ds(base - 8, 24), :]
                kap = kx[pl.ds(base - 8, 24), :]
                mid, k_mid = value[8:16], kap[8:16]
                left, right = sides(mid)
                k_left, k_right = sides(k_mid)
                new = conducted(
                    mid, value[7:15], value[9:17], left, right, k_mid, kap[7:15], kap[9:17], k_left, k_right
                )
                if masked:
                    n = row + base
                    bad = ((n < PAD) & (place == first)) | ((n >= PAD + h) & (place == last))
                    new = jnp.where(bad, 0.0, new)
                if masked:
                    dst[pl.ds(base, 8), :] = new
                else:
                    at = pl.ds(base - PAD, 8)
                    if not keep:
                        outs[0][at, :] = -new
                        return carry
                    for b in range(blocks):
                        outs[0][plan.slot(b), at, :] = -new[:, b * INNER : (b + 1) * INNER]
                    kept[pl.ds(base - PAD, 8), :] = -new
                return carry

            lax.fori_loop(0, count, step, 0)

        refs = [h0, h1]
        for n in range(SMOOTH):
            if n < SMOOTH - 1:
                smooth(refs[n % 2], refs[(n + 1) % 2], PAD - 8, (h + 16) // 8, True)
            else:
                smooth(refs[n % 2], refs[(n + 1) % 2], PAD, h // 8, False)
        if keep:
            for s, out in enumerate(outs[1:]):
                c = lax.rem(me[1] + s, plan.cross)
                lanes = pl.ds(pl.multiple_of(c * plan.cols_here, plan.cols_here), plan.cols_here)
                out[...] = kept[:, lanes]

    tall = pltpu.VMEM((h + 2 * PAD, plan.cols), F32)
    flat = (h, plan.cols)
    if keep:
        outs = [jax.ShapeDtypeStruct((plan.devices, h, plan.width), F32)]
        outs += [jax.ShapeDtypeStruct((h, plan.cols_here), F32)] * plan.cross
    else:
        outs = [jax.ShapeDtypeStruct(flat, F32)]
    return call(body, outs, [tall] * 3 + [pltpu.VMEM(flat, F32)], (), () if keep else (0,))(
        kappa, above, below, part, beside, *rest
    )


def rows_heat(plan, dft, table, received, alpha):
    width = plan.width

    def body(dft, table, received, alpha, heat, edge_left, edge_right, xh, z, dep):
        def write(a, off, value):
            deposit = alpha[...] * (value[0] * value[0] + value[1] * value[1])
            rows = pl.ds(a * INNER + off, CHUNK)
            dep[rows, 0:width], dep[rows, width : 2 * width] = split(deposit)

        along_rows(functools.partial(plan.flip_a, received), write, dft, table, xh, z)
        tile = 2 * INNER
        ones = lower_ones(tile)
        carry = jnp.zeros((1, width), F32)
        for g in range(plan.rows // tile):
            both = jnp.dot(ones, dep[g * tile : (g + 1) * tile, :], preferred_element_type=F32)
            value = both[:, :width] + both[:, width:] + carry
            heat[g * tile : (g + 1) * tile, :] = value
            carry = value[tile - 1 : tile, :]
        for g in range(plan.rows // INNER):
            plan.edges(heat[g * INNER : (g + 1) * INNER, :], edge_left, edge_right, g * INNER)

    edge = jax.ShapeDtypeStruct((8, plan.rows), F32)
    outs = [jax.ShapeDtypeStruct((plan.rows, width), F32), edge, edge]
    scratch = plan.work_a() + [pltpu.VMEM((plan.rows, 2 * width), BF16)]
    return call(body, outs, scratch, (0, 1, 2), ())(dft, table, received, alpha)


def rows_turn(plan, read_field, wide, dft, table, screen, field):
    def body(dft, table, screen, field, out, *work):
        def read(a, off):
            return screened(read_field(field, a, off), screen[pl.ds(a * INNER + off, CHUNK), :])

        along_rows(read, functools.partial(plan.send_a, out), dft, table, *work)
        if wide:
            plan.send_edges(out)

    out = plan.sent_wide if wide else plan.sent
    return call(body, [out], plan.work_a(), (0, 1, 2), (0,))(dft, table, screen, field)[0]


def rows_smooth(plan, heat, from_left, from_right, kappa, kappa_left, kappa_right, me):
    width = plan.width
    PAD = 8
    step_rows = 32

    def body(heat, from_left, from_right, kappa, kappa_left, kappa_right, me, screen, h0, h1, kx):
        place = me[1] * plan.wind + plan.local(me[0], me[1])
        zeros = jnp.zeros((PAD, 2 * width), F32)
        for ref in (h0, h1, kx):
            ref[0:PAD, :] = zeros
            ref[plan.rows + PAD : plan.rows + 2 * PAD, :] = zeros
        for g in range(plan.rows // INNER):
            n = slice(g * INNER, (g + 1) * INNER)
            spot = slice(PAD + g * INNER, PAD + (g + 1) * INNER)
            for ref, value, left, right in ((h0, heat, from_left, from_right), (kx, kappa, kappa_left, kappa_right)):
                ref[spot, 0:width] = value[n, :]
                beside = [right[:, n], jnp.zeros((width - 16, INNER), F32), left[:, n]]
                ref[spot, width : 2 * width] = jnp.concatenate(beside, axis=0).T
        wide = lax.broadcasted_iota(jnp.int32, (step_rows, 2 * width), 1)
        bad = (wide >= width) & (wide < width + width // 2) & (place == plan.devices - 1)
        bad = bad | ((wide >= width + width // 2) & (place == 0))

        def smooth(src, dst):
            def one(base):
                value = src[pl.ds(base, step_rows + 16), :]
                kap = kx[pl.ds(base, step_rows + 16), :]
                mid, k_mid = value[8:-8], kap[8:-8]
                new = conducted(
                    mid, value[7:-9], value[9:-7], pltpu.roll(mid, 1, 1), pltpu.roll(mid, 2 * width - 1, 1),
                    k_mid, kap[7:-9], kap[9:-7], pltpu.roll(k_mid, 1, 1), pltpu.roll(k_mid, 2 * width - 1, 1),
                )
                dst(base, jnp.where(bad, 0.0, new))

            def step(i, carry):
                for n in range(4):
                    one(pl.multiple_of((4 * i + n) * step_rows, step_rows))
                return carry

            lax.fori_loop(0, plan.rows // (4 * step_rows), step, 0)

        def into(ref):
            def put(base, value):
                ref[pl.ds(base + PAD, step_rows), :] = value

            return put

        def into_screen(base, value):
            screen[pl.ds(base, step_rows), :] = -value[:, :width]

        refs = [h0, h1]
        for n in range(SMOOTH):
            smooth(refs[n % 2], into(refs[(n + 1) % 2]) if n < SMOOTH - 1 else into_screen)

    tall = pltpu.VMEM((plan.rows + 2 * PAD, 2 * width), F32)
    outs = [jax.ShapeDtypeStruct((plan.rows, width), F32)]
    return call(body, outs, [tall] * 3, (), (0,))(heat, from_left, from_right, kappa, kappa_left, kappa_right, me)[0]


def next_prev(value_up, value_down, axes, order):
    up = list(zip(order[:-1], order[1:]))
    down = [(j, i) for i, j in up]
    return lax.ppermute(value_up, axes, up), lax.ppermute(value_down, axes, down)


def extended(shard, sides, width):
    for axis, dim in sides:
        size, length = (lax.axis_size(axis), shard.shape[dim])
        up = [(i, (i + 1) % size) for i in range(size - 1)]
        down = [(j, i) for i, j in up]
        last = lax.slice_in_dim(shard, length - width, length, axis=dim)
        initial = lax.slice_in_dim(shard, 0, width, axis=dim)
        before = lax.ppermute(last, axis, up)
        after = lax.ppermute(initial, axis, down)
        shard = jnp.concatenate([before, shard, after], axis=dim)
    return shard


def carried_in(part, axis, combine, identity):
    place = lax.axis_index(axis)
    gathered = lax.all_gather(part, axis)
    state = jnp.zeros_like(part) + jnp.asarray(identity, part.dtype)

    def one(turn, state):
        return combine(state, lax.dynamic_index_in_dim(gathered, turn, 0, False))

    return lax.fori_loop(0, place, one, state)


def signed_freq(indices, length):
    shifted = jnp.where(indices < length // 2, indices, indices - length)
    return shifted.astype(jnp.float32) / length


def trig_table(first_ids, second_ids, length, sign_value):
    product = first_ids * second_ids % length
    phase_angle = product.astype(jnp.float32) * (sign_value * 2.0 * math.pi / length)
    return (jnp.cos(phase_angle), jnp.sin(phase_angle))


def complex_product(formula, real_part, imag_part, cosine, sine):
    highest = lax.Precision.HIGHEST
    out_real = jnp.einsum(formula, real_part, cosine, precision=highest) - jnp.einsum(
        formula, imag_part, sine, precision=highest
    )
    out_imag = jnp.einsum(formula, real_part, sine, precision=highest) + jnp.einsum(
        formula, imag_part, cosine, precision=highest
    )
    return (out_real, out_imag)


def transform(stacked, axis_dim, inverse):
    full_shape = stacked.shape
    length = full_shape[axis_dim]
    inner_len = math.gcd(length, 128)
    outer_len = length // inner_len
    leading = full_shape[1] if axis_dim == 2 else 1
    trailing = full_shape[2] if axis_dim == 1 else 1
    blocks = stacked.reshape(2, leading, outer_len, inner_len, trailing)
    sign_value = 1.0 if inverse else -1.0
    outer_ids = jnp.arange(outer_len, dtype=jnp.int32)
    inner_ids = jnp.arange(inner_len, dtype=jnp.int32)
    cos_outer, sin_outer = trig_table(outer_ids[:, None], outer_ids[None, :], outer_len, sign_value)
    first_real, first_imag = complex_product(
        "pabq,ak->pkbq", blocks[0], blocks[1], cos_outer, sin_outer
    )
    cos_twist, sin_twist = trig_table(outer_ids[:, None], inner_ids[None, :], length, sign_value)
    cos_twist = cos_twist[None, :, :, None]
    sin_twist = sin_twist[None, :, :, None]
    twist_real = first_real * cos_twist - first_imag * sin_twist
    twist_imag = first_real * sin_twist + first_imag * cos_twist
    cos_inner, sin_inner = trig_table(inner_ids[:, None], inner_ids[None, :], inner_len, sign_value)
    second_real, second_imag = complex_product(
        "pkbq,bm->pkmq", twist_real, twist_imag, cos_inner, sin_inner
    )
    result = jnp.stack([second_real, second_imag]).transpose(0, 1, 3, 2, 4).reshape(full_shape)
    if inverse:
        result = result * (1.0 / length)
    return result


def apply_phase(stacked, phase_angle):
    cosine = jnp.cos(phase_angle)
    sine = jnp.sin(phase_angle)
    return jnp.stack(
        [stacked[0] * cosine - stacked[1] * sine, stacked[0] * sine + stacked[1] * cosine]
    )


def along_joint(stacked, phase_rate, row_freq, col_freq):
    cross_count = lax.axis_size("cross")
    stacked = lax.all_to_all(stacked, ("wind", "cross"), split_axis=2, concat_axis=1, tiled=True)
    stacked = transform(stacked, 1, False)
    col_width = stacked.shape[2]
    joint_block = lax.axis_index("wind") * cross_count + lax.axis_index("cross")
    cols_held = lax.dynamic_slice_in_dim(col_freq, joint_block * col_width, col_width)
    phase_angle = -phase_rate * (
        row_freq[:, None] * row_freq[:, None] + cols_held[None, :] * cols_held[None, :]
    )
    stacked = apply_phase(stacked, phase_angle)
    stacked = transform(stacked, 1, True)
    return lax.all_to_all(stacked, ("wind", "cross"), split_axis=1, concat_axis=2, tiled=True)


def propagate_slab(slab_pair, share_step):
    rows_total = slab_pair.shape[1] * lax.axis_size("wind") * lax.axis_size("cross")
    cols_total = slab_pair.shape[2]
    phase_rate = share_step * diffraction
    row_freq = signed_freq(jnp.arange(rows_total, dtype=jnp.int32), rows_total)
    col_freq = signed_freq(jnp.arange(cols_total, dtype=jnp.int32), cols_total)
    stacked = transform(slab_pair, 2, False)
    stacked = along_joint(stacked, phase_rate, row_freq, col_freq)
    return transform(stacked, 2, True)


def conduct_core(padded, kappa_pad):
    height = padded.shape[0] - 2
    breadth = padded.shape[1] - 2
    center = padded[1:-1, 1:-1]
    kappa_mid = kappa_pad[1:-1, 1:-1]
    flux_sum = jnp.zeros_like(center)
    for offset_row, offset_col in ((0, 1), (2, 1), (1, 0), (1, 2)):
        neighbour = padded[offset_row : offset_row + height, offset_col : offset_col + breadth]
        kappa_side = kappa_pad[offset_row : offset_row + height, offset_col : offset_col + breadth]
        flux_sum = flux_sum + 0.5 * (kappa_mid + kappa_side) * (neighbour - center)
    return center + conduct_rate * flux_sum


def add_terms(earlier, later_term):
    return earlier + later_term


def layer_absorption(index_row, table_row, level_ids):
    one_hot = (index_row[:, None] == level_ids[None, :]).astype(jnp.float32)
    return jnp.sum(one_hot * table_row[None, :], axis=1)


def wide_device(field_real, field_imag, absorb_index, absorb_table, zone_map, zone_conductivity):
    rows_here, cols_here = field_real.shape
    conductivity = jnp.zeros((rows_here, cols_here), jnp.float32)
    for zone_no in range(zone_conductivity.shape[0]):
        conductivity = jnp.where(zone_map == zone_no, zone_conductivity[zone_no], conductivity)
    level_ids = jnp.arange(absorb_table.shape[1], dtype=jnp.int32)
    combined = lax.all_to_all(
        jnp.stack([field_real, field_imag, conductivity]),
        "cross",
        split_axis=1,
        concat_axis=2,
        tiled=True,
    )
    slab_pair = combined[:2]
    kappa_rows = extended(combined[2], ((("wind", "cross"), 0),), 1)
    kappa_pad = jnp.pad(kappa_rows, ((0, 0), (1, 1)))
    index_full = lax.all_gather(absorb_index, "cross", axis=1, tiled=True)
    slab_rows = slab_pair.shape[1]
    rows_total = slab_rows * lax.axis_size("wind") * lax.axis_size("cross")
    slab_ids = jnp.arange(slab_rows, dtype=jnp.int32)
    lower_slab = (slab_ids[:, None] >= slab_ids[None, :]).astype(jnp.float32)
    screen_phase = jnp.zeros((slab_rows, slab_pair.shape[2]), jnp.float32)
    for layer_no in range(LAYERS):
        absorption = layer_absorption(index_full[layer_no], absorb_table[layer_no], level_ids)
        screen_phase = jnp.zeros((slab_rows, slab_pair.shape[2]), jnp.float32)
        for _ in range(ITERS):
            middle = propagate_slab(apply_phase(slab_pair, screen_phase), 0.5)
            intensity = middle[0] * middle[0] + middle[1] * middle[1]
            deposit = absorption[None, :] * intensity * (1.0 / rows_total)
            partial_heat = jnp.dot(lower_slab, deposit, precision=lax.Precision.HIGHEST)
            totals = partial_heat[-1]
            upstream = carried_in(totals, ("wind", "cross"), add_terms, jnp.zeros_like(totals))
            heat_field = partial_heat + upstream[None, :]
            for _ in range(SMOOTH):
                padded = extended(heat_field, ((("wind", "cross"), 0),), 1)
                padded = jnp.pad(padded, ((0, 0), (1, 1)))
                heat_field = conduct_core(padded, kappa_pad)
            screen_phase = -heat_field
        slab_pair = propagate_slab(apply_phase(slab_pair, screen_phase), 1.0)
    returned = lax.all_to_all(
        jnp.stack([slab_pair[0], slab_pair[1], screen_phase]),
        "cross",
        split_axis=2,
        concat_axis=1,
        tiled=True,
    )
    return (returned[0], returned[1], returned[2])


def on_device(field_real, field_imag, absorb_index, absorb_table, zone_map, zone_conductivity):
    plan = Plan(*field_real.shape, lax.axis_size("wind"), lax.axis_size("cross"))
    fits = plan.width == INNER and INNER % plan.height == 0 and plan.height % CHUNK == 0
    if not fits or plan.rows_here % INNER or plan.rows % (2 * INNER):
        return wide_device(field_real, field_imag, absorb_index, absorb_table, zone_map, zone_conductivity)
    return tiled_device(plan, field_real, field_imag, absorb_index, absorb_table, zone_map, zone_conductivity)


def tiled_device(plan, field_real, field_imag, absorb_index, absorb_table, zone_map, zone_conductivity):
    cross = plan.cross
    w, c = lax.axis_index("wind"), lax.axis_index("cross")
    place = jnp.stack([w, c]).astype(jnp.int32)
    grid_axes = ("wind", "cross")
    columns_order = [plan.slot(i) for i in range(plan.devices)]

    def exchange(x, axes):
        return lax.all_to_all(x, axes, split_axis=0, concat_axis=0, tiled=True)

    def flip(x):
        return exchange(x, grid_axes)

    to_b, *field_blocks = prepare_field(plan, field_real, field_imag, place)
    home_b = exchange(to_b, "cross")
    field_blocks = shifted(field_blocks, "wind")
    *across, kappa, left, right, alpha_a = prepare(plan, zone_map, absorb_index, absorb_table, zone_conductivity, place)
    along = home_kappa(plan, kappa, *next_prev(right, left, "cross", list(range(cross))), place)

    dft = jnp.asarray(dft_matrices())
    tab_a = lambda share: (jnp.asarray(row_blocks(plan.rows, share)), jnp.asarray(row_table(plan.rows)))
    tab_b = lambda *shares: jnp.asarray(chirp_columns(plan.cols, shares))

    def smooth_a(layer, share, received):
        heat, left, right = rows_heat(plan, *tab_a(share), received, alpha_a[layer : layer + 1])
        from_left, from_right = next_prev(right, left, grid_axes, columns_order)
        return rows_smooth(plan, heat, from_left, from_right, *kappas, place)

    def smooth_b(layer, keep, received):
        part, beside, totals = cols_heat(plan, layer, plan.devices, dft, tab_b(0.5), received, alpha_b)
        return cols_smooth(plan, keep, kappa_b, above, below, part, beside, flip(totals), place)

    home_b, across = lax.optimization_barrier((home_b, across))
    sent = cols_send(plan, plan.home_b, False, dft, tab_b(0.5), home_b)
    kappa_b, alpha_b = home_rows(plan, shifted(across, "cross"), place)
    above, below = next_prev(kappa_b[-8:], kappa_b[:8], grid_axes, list(range(plan.devices)))
    received, along = lax.optimization_barrier((flip(sent), along))
    along = shifted(along, "wind")
    kappas = rows_kappa(plan, along, place)
    home_a = in_order(field_blocks, place, 0)
    screen = smooth_a(0, 0.5, received)
    sent = rows_turn(plan, plan.home_a, True, *tab_a(0.5), screen, home_a)
    received, above, below = lax.optimization_barrier((flip(sent), above, below))
    (screen,) = smooth_b(0, False, received)
    sent_middle, sent_field = cols_turn(plan, plan.home_b, 2, dft, tab_b(1.5, 1.0), screen, home_b)
    middle = flip(sent_middle)
    field = flip(sent_field)
    screen = smooth_a(1, 1.5, middle)
    field, screen = lax.optimization_barrier((field, screen))
    field = rows_field(plan, plan.flip_a, *tab_a(1.0), field)
    sent = rows_turn(plan, plan.flip_a, True, *tab_a(0.5), screen, field)
    screen, *home_parts = smooth_b(1, True, flip(sent))
    home_parts = shifted(home_parts, "cross")
    screen = flip(screen).reshape(plan.rows, plan.width)
    sent = rows_turn(plan, plan.flip_a, False, *tab_a(1.0), screen, field)
    back = cols_send(plan, plan.flip_b, True, dft, tab_b(1.0), flip(sent))
    screen = home_screen(plan, home_parts, place)
    back = exchange(back, "cross")
    out_real = back[:, : plan.height].reshape(field_real.shape)
    out_imag = back[:, plan.height :].reshape(field_real.shape)
    return (out_real, out_imag, screen)


def solution(mesh):
    in_specs = (
        P(("beams", "wind"), "cross"),
        P(("beams", "wind"), "cross"),
        P(None, "cross"),
        P(),
        P("wind", "cross"),
        P(),
    )
    out_specs = (
        P(("beams", "wind"), "cross"),
        P(("beams", "wind"), "cross"),
        P(("beams", "wind"), "cross"),
    )
    return jax.shard_map(on_device, mesh=mesh, in_specs=in_specs, out_specs=out_specs, check_vma=False)
```

```python
import functools
import math

import jax
import jax.numpy as jnp
import numpy as np
from jax import lax
from jax.experimental import pallas as pl
from jax.experimental.pallas import tpu as pltpu
from jax.sharding import PartitionSpec as P


LAYERS = 2
ITERS = 2
SMOOTH = 2
INNER = 128
CHUNK = 16

diffraction = 2000.0
conduct_rate = 0.24

F32 = jnp.float32
BF16 = jnp.bfloat16
WHOLE = pl.BlockSpec(memory_space=pltpu.VMEM)
SCALAR = pl.BlockSpec(memory_space=pltpu.SMEM)


def split_np(values):
    high = values.astype(np.float32).astype(jnp.bfloat16)
    low = (values - high.astype(np.float64)).astype(np.float32).astype(jnp.bfloat16)
    return high, low


def dft_matrices():
    ids = np.arange(INNER)
    angle = 2.0 * np.pi * (np.outer(ids, ids) % INNER) / INNER
    cosine, sine = np.cos(angle), np.sin(angle)
    left = np.block([[cosine, sine], [-sine, cosine]])
    return np.stack([*split_np(left), *split_np(left.T)])


def chirp_columns(length, shares):
    outer = length // INNER
    k = np.arange(outer)[:, None]
    m = np.arange(INNER)[None, :]
    twist = -2.0 * np.pi * ((k * m) % length) / length
    tables = [np.cos(twist), np.sin(twist)]
    p = k + outer * m
    freq = np.where(p < length // 2, p, p - length) / length
    for share in shares:
        angle = -share * diffraction * freq * freq
        tables += [np.cos(angle) / length, np.sin(angle) / length]
    return np.concatenate(tables, axis=0).astype(np.float32)


def row_table(length):
    cols = chirp_columns(length, ()).T
    return np.pad(cols, ((0, 0), (0, -cols.shape[1] % 128)))


def row_blocks(length, share):
    outer = length // INNER
    ids = np.arange(INNER)
    forward = np.exp(-2j * np.pi * (np.outer(ids, ids) % INNER) / INNER)
    blocks = []
    for k in range(outer):
        p = k + outer * ids
        freq = np.where(p < length // 2, p, p - length) / length
        block = forward.conj() @ (np.exp(-1j * share * diffraction * freq * freq)[:, None] / length * forward)
        blocks.append(np.stack(split_np(np.block([[block.real, -block.imag], [block.imag, block.real]]))))
    return np.stack(blocks)


def split(x):
    high = x.astype(BF16)
    return high, (x - high.astype(F32)).astype(BF16)


def times(a, b):
    return (a[0] * b[0] - a[1] * b[1], a[0] * b[1] + a[1] * b[0])


def small_fft(points, sign):
    count = len(points)
    if count == 1:
        return points
    even = small_fft(points[0::2], sign)
    odd = small_fft(points[1::2], sign)
    half = count // 2
    out = [None] * count
    for k in range(half):
        re, im = odd[k]
        if k == 0:
            turn = (re, im)
        elif 4 * k == count:
            turn = (-im, re) if sign > 0 else (im, -re)
        elif 8 * k == count:
            root = math.sqrt(0.5)
            turn = (root * (re - im), root * (im + re)) if sign > 0 else (root * (re + im), root * (im - re))
        elif 8 * k == 3 * count:
            root = math.sqrt(0.5)
            turn = (-root * (re + im), root * (re - im)) if sign > 0 else (root * (im - re), -root * (re + im))
        else:
            c = math.cos(2.0 * math.pi * k / count)
            s = sign * math.sin(2.0 * math.pi * k / count)
            turn = (c * re - s * im, s * re + c * im)
        out[k] = (even[k][0] + turn[0], even[k][1] + turn[1])
        out[k + half] = (even[k][0] - turn[0], even[k][1] - turn[1])
    return out


def cos_sin(x):
    turns = jnp.floor(x * (2.0 / math.pi) + 0.5)
    r = ((x - turns * 1.5703125) - turns * 4.837512969970703125e-4) - turns * 7.549789954891882e-8
    quad = turns.astype(jnp.int32)
    z = r * r
    s = r + r * z * (-1.6666654611e-1 + z * (8.3321608736e-3 - z * 1.9515295891e-4))
    c = 1.0 - 0.5 * z + z * z * (4.166664568298827e-2 + z * (-1.388731625493765e-3 + z * 2.443315711809948e-5))
    odd = (quad & 1) == 1
    sin_x = jnp.where(odd, c, s)
    cos_x = jnp.where(odd, s, c)
    sin_x = jnp.where((quad & 2) == 2, -sin_x, sin_x)
    cos_x = jnp.where(((quad + 1) & 2) == 2, -cos_x, cos_x)
    return cos_x, sin_x


def screened(value, screen):
    return times(value, cos_sin(screen))


def triple(a_high, a_low, b_high, b_low):
    dot = functools.partial(jnp.dot, preferred_element_type=F32)
    return dot(a_high, b_high) + dot(a_high, b_low) + dot(a_low, b_high)


def lower_ones(size):
    r = lax.broadcasted_iota(jnp.int32, (size, size), 0)
    c = lax.broadcasted_iota(jnp.int32, (size, size), 1)
    return jnp.where(r >= c, 1.0, 0.0).astype(BF16)


def chunks(count, body):
    def step(i, carry):
        for n in range(side):
            body(pl.multiple_of((side * i + n) * CHUNK, CHUNK))
        return carry

    side = 2 if count % (2 * CHUNK) == 0 else 1
    lax.fori_loop(0, count // (side * CHUNK), step, 0)


def along_rows(read, write, matrices, table, xh, z):
    outer = matrices.shape[0]
    width = z.shape[1] // outer
    lanes = lambda k: pl.ds(k * width, width)
    col = lambda part, off: table[pl.ds(off, CHUNK), part : part + 1]

    def first(off):
        for k, value in enumerate(small_fft([read(a, off) for a in range(outer)], -1)):
            if k:
                value = times(value, (col(k, off), col(outer + k, off)))
            for at, v in ((0, value[0]), (INNER, value[1])):
                high, low = split(v)
                xh[pl.ds(at + off, CHUNK), pl.ds(2 * k * width, width)] = high
                xh[pl.ds(at + off, CHUNK), pl.ds((2 * k + 1) * width, width)] = low

    def last(off):
        values = []
        for k in range(outer):
            value = (z[pl.ds(off, CHUNK), lanes(k)], z[pl.ds(INNER + off, CHUNK), lanes(k)])
            if k:
                value = times(value, (col(k, off), -col(outer + k, off)))
            values.append(value)
        for a, value in enumerate(small_fft(values, 1)):
            write(a, off, value)

    chunks(INNER, first)
    dot = functools.partial(jnp.dot, preferred_element_type=F32)
    for k in range(outer):
        both = dot(matrices[k, 0], xh[:, 2 * k * width : (2 * k + 2) * width])
        low = dot(matrices[k, 1], xh[:, 2 * k * width : (2 * k + 1) * width])
        z[:, k * width : (k + 1) * width] = both[:, :width] + both[:, width:] + low
    chunks(INNER, last)


def along_cols(main, read, writes, dft, table, xh, xl, y, z):
    outer = table.shape[0] // (2 * (1 + len(writes)))
    height = xh.shape[0] // outer

    def every(body):
        chunks(main, body)
        if height > main:
            body(main)

    row = lambda part: table[part : part + 1, :]

    def put(k, off, value):
        for at, v in ((0, value[0]), (INNER, value[1])):
            spot = (pl.ds(k * height + off, CHUNK), pl.ds(at, INNER))
            xh[spot], xl[spot] = split(v)

    def get(ref, k, off):
        return tuple(ref[pl.ds(k * height + off, CHUNK), pl.ds(at, INNER)] for at in (0, INNER))

    def first(off):
        for k, value in enumerate(small_fft([read(b, off) for b in range(outer)], -1)):
            if k:
                value = times(value, (row(k), row(outer + k)))
            put(k, off, value)

    every(first)
    y[...] = triple(xh[...], xl[...], dft[2], dft[3])
    for n, write in enumerate(writes):

        def middle(off, n=n):
            for k in range(outer):
                base = (2 + 2 * n) * outer + k
                put(k, off, times(get(y, k, off), (row(base), row(base + outer))))

        every(middle)
        z[...] = triple(xh[...], xl[...], dft[0], dft[1])

        def last(off, write=write):
            values = []
            for k in range(outer):
                value = get(z, k, off)
                if k:
                    value = times(value, (row(k), -row(outer + k)))
                values.append(value)
            for b, value in enumerate(small_fft(values, 1)):
                write(b, off, value)

        every(last)


class Plan:
    def __init__(self, rows_here, cols_here, wind, cross):
        self.wind, self.cross = wind, cross
        self.devices = wind * cross
        self.rows_here, self.cols_here = rows_here, cols_here
        self.height = rows_here // cross
        self.width = cols_here // wind
        self.rows, self.cols = rows_here * wind, cols_here * cross

    def local(self, w, c):
        return w + (c % 2) * (self.wind - 1 - 2 * w)

    def slot(self, block):
        c, i = block // self.wind, block % self.wind
        return self.local(i, c) * self.cross + c

    def home_a(self, ref, a, off):
        n = a * INNER
        src, at = n // self.rows_here, n % self.rows_here
        return tuple(ref[src, pl.ds(p * self.rows_here + at + off, CHUNK), :] for p in (0, 1))

    def spot_a(self, a, off):
        per = INNER // self.height
        return a * per + off // self.height, lax.rem(off, self.height)

    def flip_a(self, ref, a, off):
        s, at = self.spot_a(a, off)
        at = pl.multiple_of(at, CHUNK)
        return tuple(ref[s, pl.ds(p * self.height + at, CHUNK), :] for p in (0, 1))

    def send_a(self, ref, a, off, value):
        s, at = self.spot_a(a, off)
        at = pl.multiple_of(at, CHUNK)
        for p in (0, 1):
            ref[s, pl.ds(p * self.height + at, CHUNK), :] = value[p]

    def send_edges(self, ref):
        h = self.height
        for d in range(self.devices):
            for p in (0, 1):
                at = 2 * h + 4 * p
                before = ref[d - 1, p * h + h - 2 : p * h + h, :] if d else jnp.zeros((2, self.width), F32)
                after = ref[d + 1, p * h : p * h + 2, :] if d + 1 < self.devices else jnp.zeros((2, self.width), F32)
                ref[d, at : at + 2, :] = before
                ref[d, at + 2 : at + 4, :] = after

    def edges(self, value, left, right, at):
        turned = value.T
        left[:, at : at + INNER] = turned[0:8, :]
        right[:, at : at + INNER] = turned[self.width - 8 : self.width, :]

    def send_sides(self, ref):
        h, w = self.height, self.width
        last = self.devices - 1
        for b in range(self.devices):
            turned = ref[self.slot(b), 0 : 2 * h, :].T
            if b < last:
                ref[self.slot(b + 1), 2 * h : 2 * h + 2, :] = turned[w - 2 : w, :]
            if b:
                ref[self.slot(b - 1), 2 * h + 2 : 2 * h + 4, :] = turned[0:2, :]
        none = jnp.zeros((2, w), F32)
        ref[self.slot(0), 2 * h : 2 * h + 2, :] = none
        ref[self.slot(last), 2 * h + 2 : 2 * h + 4, :] = none

    def home_b(self, ref, b, off):
        per = self.cols_here // INNER
        return tuple(ref[b // per, pl.ds(p * self.height + off, CHUNK), pl.ds((b % per) * INNER, INNER)] for p in (0, 1))

    def wide_b(self, ref, b, off):
        if isinstance(off, int):
            extra = ref[self.slot(b), 2 * self.height : 2 * self.height + 8, :]
            turned = jnp.concatenate([extra[4:8], extra[0:4]], axis=0)
            return jnp.concatenate([extra, extra], axis=0), jnp.concatenate([turned, turned], axis=0)
        return self.flip_b(ref, b, off)

    def flip_b(self, ref, b, off):
        return tuple(ref[self.slot(b), pl.ds(p * self.height + off, CHUNK), :] for p in (0, 1))

    def send_b(self, ref, b, off, value):
        for p in (0, 1):
            ref[self.slot(b), pl.ds(p * self.height + off, CHUNK), :] = value[p]

    def back_b(self, ref, b, off, value):
        per = self.cols_here // INNER
        for p in (0, 1):
            ref[b // per, pl.ds(p * self.height + off, CHUNK), pl.ds((b % per) * INNER, INNER)] = value[p]

    @property
    def sent(self):
        return jax.ShapeDtypeStruct((self.devices, 2 * self.height, self.width), F32)

    def work_a(self):
        wide = (self.rows // INNER) * self.width
        return [
            pltpu.VMEM((2 * INNER, 2 * wide), BF16),
            pltpu.VMEM((2 * INNER, wide), F32),
        ]

    @property
    def sent_wide(self):
        return jax.ShapeDtypeStruct((self.devices, 2 * self.height + 8, self.width), F32)

    def work_b(self, extra=0):
        tall = (self.cols // INNER) * (self.height + extra)
        return [
            pltpu.VMEM((tall, 2 * INNER), BF16),
            pltpu.VMEM((tall, 2 * INNER), BF16),
            pltpu.VMEM((tall, 2 * INNER), F32),
            pltpu.VMEM((tall, 2 * INNER), F32),
        ]


def call(body, outs, scratch, near=(), near_outs=(), far=()):
    def run(*args):
        specs = [SCALAR if a.size <= 16 else WHOLE for a in args]
        spaces = [pltpu.VMEM if i in near else pltpu.HBM if i in far else None for i in range(len(args))]
        args = [pltpu.with_memory_space_constraint(a, space) if space else a for a, space in zip(args, spaces)]
        return pl.pallas_call(
            body,
            out_shape=[pltpu.VMEM(o.shape, o.dtype) if i in near_outs else o for i, o in enumerate(outs)],
            in_specs=specs,
            out_specs=[WHOLE] * len(outs),
            scratch_shapes=scratch,
            compiler_params=pltpu.CompilerParams(vmem_limit_bytes=14 * 1024 * 1024),
        )(*args)

    return run


def prepare_field(plan, field_real, field_imag, place):
    h = plan.height

    def body(real, imag, place, to_b, *to_a):
        for c in range(plan.cross):
            to_b[c, 0:h, :] = real[c * h : (c + 1) * h, :]
            to_b[c, h : 2 * h, :] = imag[c * h : (c + 1) * h, :]
        for t, out in enumerate(to_a):
            n = lax.rem(place[0] + t, plan.wind)
            lanes = pl.ds(pl.multiple_of(plan.local(n, place[1]) * plan.width, plan.width), plan.width)
            out[0 : plan.rows_here, :] = real[:, lanes]
            out[plan.rows_here : 2 * plan.rows_here, :] = imag[:, lanes]

    outs = [jax.ShapeDtypeStruct((plan.cross, 2 * h, plan.cols_here), F32)]
    outs += [jax.ShapeDtypeStruct((2 * plan.rows_here, plan.width), F32)] * plan.wind
    return call(body, outs, [], (), (), (0, 1))(field_real, field_imag, place)


def prepare(plan, zone_map, absorb_index, absorb_table, zone_conductivity, place):
    h = plan.height

    def picked(ids, count, level):
        value = jnp.zeros(ids.shape, F32)
        for n in range(count):
            value = jnp.where(ids == n, level(n), value)
        return value

    def body(zones, index, table, levels, place, *refs):
        to_b, (kappa, left, right, alpha_a, alpha) = refs[: plan.cross], refs[plan.cross :]
        w, c = place[0], place[1]

        def step(off):
            kappa[pl.ds(off, CHUNK), :] = picked(zones[pl.ds(off, CHUNK), :], levels.shape[0], lambda n: levels[n])

        chunks(plan.rows_here, step)
        alpha[...] = jnp.zeros_like(alpha)
        for layer in range(LAYERS):
            value = picked(index[layer : layer + 1, :], table.shape[1], lambda n: table[layer, n])
            alpha[layer : layer + 1, :] = value * (1.0 / plan.rows)
        alpha_a[...] = alpha[:, pl.ds(pl.multiple_of(plan.local(w, c) * plan.width, plan.width), plan.width)]
        for s, out in enumerate(to_b):
            out[0:h, :] = kappa[pl.ds(pl.multiple_of(lax.rem(c + s, plan.cross) * h, h), h), :]
            out[h:, :] = alpha[...]
        for at in range(0, plan.rows_here, INNER):
            left[0:8, at : at + INNER] = kappa[at : at + INNER, 0 : plan.width].T[0:8, :]
            right[0:8, at : at + INNER] = kappa[at : at + INNER, plan.cols_here - plan.width :].T[plan.width - 8 :, :]
        left[8:16, :] = jnp.zeros((8, plan.rows_here), F32)
        right[8:16, :] = jnp.zeros((8, plan.rows_here), F32)
        left[8:16, 0:INNER] = alpha[:, 0 : plan.width]
        right[8:16, 0:INNER] = alpha[:, plan.cols_here - plan.width :]

    edge = jax.ShapeDtypeStruct((16, plan.rows_here), F32)
    outs = [jax.ShapeDtypeStruct((h + 8, plan.cols_here), F32)] * plan.cross
    outs += [jax.ShapeDtypeStruct(zone_map.shape, F32), edge, edge, jax.ShapeDtypeStruct((8, plan.width), F32)]
    outs.append(jax.ShapeDtypeStruct((8, plan.cols_here), F32))
    return call(body, outs, [], (), (), (0,))(
        zone_map, absorb_index, absorb_table, zone_conductivity, place
    )


def home_kappa(plan, kappa, from_left, from_right, alpha, place):
    per = plan.rows_here // INNER

    def body(kappa, from_left, from_right, alpha, place, side_alpha, *refs):
        outs, edges = refs[: plan.wind], refs[-1]
        mine = plan.local(place[0], place[1])
        side_alpha[...] = jnp.zeros_like(side_alpha)
        for i in range(plan.wind):

            @pl.when(mine == i)
            def _():
                for layer in range(LAYERS):
                    line = slice(layer, layer + 1)
                    before = alpha[line, (i - 1) * plan.width : i * plan.width] if i else from_left[8 + layer : 9 + layer, 0:INNER]
                    last = i + 1 == plan.wind
                    after = from_right[8 + layer : 9 + layer, 0:INNER] if last else alpha[line, (i + 1) * plan.width : (i + 2) * plan.width]
                    for n, value in enumerate((before[:, -2:-1], before[:, -1:], after[:, 0:1], after[:, 1:2])):
                        side_alpha[layer, n : n + 1, :] = jnp.broadcast_to(value, (1, INNER))

        for at in range(per):
            n = slice(at * INNER, (at + 1) * INNER)
            edges[0, 8 * at : 8 * at + 8, :] = from_left[0:8, n]
            edges[plan.wind - 1, 8 * (per + at) : 8 * (per + at) + 8, :] = from_right[0:8, n]
            for i in range(plan.wind):
                turned = kappa[n, i * plan.width : (i + 1) * plan.width].T
                if i + 1 < plan.wind:
                    edges[i + 1, 8 * at : 8 * at + 8, :] = turned[plan.width - 8 :, :]
                if i:
                    edges[i - 1, 8 * (per + at) : 8 * (per + at) + 8, :] = turned[0:8, :]
        for t, out in enumerate(outs):
            i = plan.local(lax.rem(place[0] + t, plan.wind), place[1])
            out[0 : plan.rows_here, :] = kappa[:, pl.ds(pl.multiple_of(i * plan.width, plan.width), plan.width)]
            out[plan.rows_here :, :] = edges[i]

    outs = [jax.ShapeDtypeStruct((LAYERS, 8, INNER), F32)]
    outs += [jax.ShapeDtypeStruct((plan.rows_here + 16 * per, plan.width), F32)] * plan.wind
    scratch = [pltpu.VMEM((plan.wind, 16 * per, INNER), F32)]
    return call(body, outs, scratch)(
        kappa, from_left, from_right, alpha, place
    )


def home_rows(plan, parts, place):
    h = plan.height

    def body(*refs):
        place, kappa, alpha = refs[plan.cross :]
        for s, ref in enumerate(refs[: plan.cross]):
            c = lax.rem(place[1] + plan.cross - s, plan.cross)
            lanes = pl.ds(pl.multiple_of(c * plan.cols_here, plan.cols_here), plan.cols_here)
            kappa[:, lanes] = ref[0:h, :]
            alpha[:, lanes] = ref[h:, :]

    outs = [jax.ShapeDtypeStruct((h, plan.cols), F32), jax.ShapeDtypeStruct((8, plan.cols), F32)]
    return call(body, outs, [])(*parts, place)


def shifted(parts, axis):
    size = lax.axis_size(axis)
    return [parts[0]] + [lax.ppermute(parts[s], axis, [(i, (i + s) % size) for i in range(size)]) for s in range(1, size)]


def in_order(parts, place, which):
    size = len(parts)

    def body(*refs):
        place, out = refs[size], refs[-1]
        for s, ref in enumerate(refs[:size]):
            out[lax.rem(place[which] + size - s, size)] = ref[...]

    out = jax.ShapeDtypeStruct((size,) + parts[0].shape, F32)
    return call(body, [out], [], range(size))(*parts, place)[0]


def home_screen(plan, parts, place):
    h = plan.height

    def body(*refs):
        place, out = refs[plan.cross], refs[-1]
        for s, ref in enumerate(refs[: plan.cross]):
            c = lax.rem(place[1] + plan.cross - s, plan.cross)
            out[pl.ds(pl.multiple_of(c * h, h), h), :] = ref[...]

    out = jax.ShapeDtypeStruct((plan.rows_here, plan.cols_here), F32)
    return call(body, [out], [])(*parts, place)[0]


def rows_kappa(plan, parts, place):
    per = plan.rows_here // INNER

    def body(*refs):
        place, out, left, right = refs[plan.wind :]
        for t, ref in enumerate(refs[: plan.wind]):
            first = lax.rem(place[0] + plan.wind - t, plan.wind) * plan.rows_here
            out[pl.ds(pl.multiple_of(first, plan.rows_here), plan.rows_here), :] = ref[0 : plan.rows_here, :]
            for at in range(per):
                n = pl.ds(pl.multiple_of(first + at * INNER, INNER), INNER)
                line = plan.rows_here + 8 * at
                left[:, n] = ref[line : line + 8, :]
                right[:, n] = ref[line + 8 * per : line + 8 * per + 8, :]

    edge = jax.ShapeDtypeStruct((8, plan.rows), F32)
    outs = [jax.ShapeDtypeStruct((plan.rows, plan.width), F32), edge, edge]
    return call(body, outs, [], range(plan.wind))(*parts, place)


def rows_field(plan, read_field, dft, table, field):
    def body(dft, table, field, out, *work):
        along_rows(functools.partial(read_field, field), functools.partial(plan.send_a, out), dft, table, *work)

    return call(body, [plan.sent], plan.work_a(), (0, 1, 2), (0,))(dft, table, field)[0]


def cols_send(plan, read_field, back, dft, table, field, sides=False):
    out = plan.sent_wide if sides else plan.sent
    if back:
        out = jax.ShapeDtypeStruct((plan.cross, 2 * plan.height, plan.cols_here), F32)

    def body(dft, table, field, out, *work):
        put = plan.back_b if back else plan.send_b
        along_cols(plan.height, functools.partial(read_field, field), [functools.partial(put, out)], dft, table, *work)
        if sides:
            plan.send_sides(out)

    return call(body, [out], plan.work_b(), (0, 1, 2), () if back else (0,))(dft, table, field)[0]


def cols_heat(plan, layer, copies, dft, table, received, absorption):
    blocks = plan.cols // INNER
    h = plan.height

    def body(dft, table, received, absorption, part, beside, totals, xh, xl, y, z, dh, dl):
        def write(b, off, value):
            alpha = absorption[layer : layer + 1, pl.ds(b * INNER, INNER)]
            deposit = alpha * (value[0] * value[0] + value[1] * value[1])
            lanes = pl.ds(b * INNER, INNER)
            if isinstance(off, int):
                beside[:, lanes] = deposit[0:8]
                return
            spot = (pl.ds(off, CHUNK), lanes)
            dh[spot], dl[spot] = split(deposit)

        along_cols(h, functools.partial(plan.wide_b, received), [write], dft, table, xh, xl, y, z)
        ones = lower_ones(h)
        dot = functools.partial(jnp.dot, preferred_element_type=F32)
        part[...] = dot(ones, dh[...]) + dot(ones, dl[...])
        for b in range(blocks):
            total = part[h - 1 : h, b * INNER : (b + 1) * INNER]
            for d in range(copies):
                totals[d, b : b + 1, :] = total

    outs = [
        jax.ShapeDtypeStruct((h, plan.cols), F32),
        jax.ShapeDtypeStruct((8, plan.cols), F32),
        jax.ShapeDtypeStruct((copies, blocks, INNER), F32),
    ]
    scratch = plan.work_b(CHUNK) + [pltpu.VMEM((h, plan.cols), BF16), pltpu.VMEM((h, plan.cols), BF16)]
    return call(body, outs, scratch, (0, 1, 2), ())(dft, table, received, absorption)


def conducted(mid, up, down, left, right, k_mid, k_up, k_down, k_left, k_right):
    flux = (k_mid + k_up) * (up - mid) + (k_mid + k_down) * (down - mid)
    flux = flux + (k_mid + k_left) * (left - mid) + (k_mid + k_right) * (right - mid)
    return mid + (0.5 * conduct_rate) * flux


def cols_turn(plan, read_field, sets, dft, table, screen, field):
    def body(dft, table, screen, field, *refs):
        outs, work = refs[:sets], refs[sets:]

        def read(b, off):
            return screened(read_field(field, b, off), screen[pl.ds(off, CHUNK), pl.ds(b * INNER, INNER)])

        along_cols(plan.height, read, [functools.partial(plan.send_b, out) for out in outs], dft, table, *work)
        if sets > 1:
            plan.send_sides(outs[0])

    return call(body, [plan.sent_wide if sets > 1 and n == 0 else plan.sent for n in range(sets)], plan.work_b(), (0, 1, 2), range(sets))(
        dft, table, screen, field
    )


def cols_smooth(plan, keep, kappa, above, below, part, beside, *rest):
    blocks = plan.cols // INNER
    h = plan.height
    PAD = 16
    first, last = 0, plan.devices - 1

    def body(kappa, above, below, part, beside, *refs):
        count = plan.cross + 1 if keep else 1
        sums, me, outs, (h0, h1, kx, kept) = refs[: -5 - count], refs[-5 - count], refs[-4 - count : -4], refs[-4:]
        place = me[0] * plan.cross + me[1]
        zeros = jnp.zeros((PAD, plan.cols), F32)
        for ref in (h0, kx, h1):
            ref[0:PAD, :] = zeros
            ref[h + PAD : h + 2 * PAD, :] = zeros
        kx[PAD - 8 : PAD, :] = above[...]
        kx[PAD : PAD + h, :] = kappa[...]
        kx[PAD + h : PAD + h + 8, :] = below[...]
        upstream = jnp.zeros((blocks, INNER), F32)
        if len(sums) == 1:
            for d in range(plan.devices):
                upstream = upstream + jnp.where(d < place, sums[0][d], 0.0)
        else:
            for s in range(1, plan.cross):
                upstream = upstream + jnp.where(s <= me[1], sums[s - 1][...], 0.0)
            for t in range(1, plan.wind):
                upstream = upstream + jnp.where(t <= me[0], sums[plan.cross + t - 2][...], 0.0)
        has_next = jnp.where(place < last, 1.0, 0.0)
        for b in range(blocks):
            lanes = slice(b * INNER, (b + 1) * INNER)
            base = upstream[b : b + 1, :]
            h0[PAD : PAD + h, lanes] = part[:, lanes] + base
            h0[PAD - 1 : PAD, lanes] = base
            h0[PAD - 2 : PAD - 1, lanes] = base - beside[1:2, lanes]
            value = base + part[h - 1 : h, lanes] + beside[2:3, lanes]
            h0[PAD + h : PAD + h + 1, lanes] = value * has_next
            h0[PAD + h + 1 : PAD + h + 2, lanes] = (value + beside[3:4, lanes]) * has_next
        lane = lax.broadcasted_iota(jnp.int32, (8, plan.cols), 1)
        row = lax.broadcasted_iota(jnp.int32, (8, plan.cols), 0)

        def sides(x):
            left = jnp.where(lane == 0, 0.0, pltpu.roll(x, 1, 1))
            right = jnp.where(lane == plan.cols - 1, 0.0, pltpu.roll(x, plan.cols - 1, 1))
            return left, right

        def smooth(src, dst, low, count, masked):
            def step(i, carry):
                base = pl.multiple_of(low + i * 8, 8)
                value = src[pl.ds(base - 8, 24), :]
                kap = kx[pl.ds(base - 8, 24), :]
                mid, k_mid = value[8:16], kap[8:16]
                left, right = sides(mid)
                k_left, k_right = sides(k_mid)
                new = conducted(
                    mid, value[7:15], value[9:17], left, right, k_mid, kap[7:15], kap[9:17], k_left, k_right
                )
                if masked:
                    n = row + base
                    bad = ((n < PAD) & (place == first)) | ((n >= PAD + h) & (place == last))
                    new = jnp.where(bad, 0.0, new)
                if masked:
                    dst[pl.ds(base, 8), :] = new
                else:
                    at = pl.ds(base - PAD, 8)
                    if not keep:
                        outs[0][at, :] = -new
                        return carry
                    for b in range(blocks):
                        outs[0][plan.slot(b), at, :] = -new[:, b * INNER : (b + 1) * INNER]
                    kept[pl.ds(base - PAD, 8), :] = -new
                return carry

            lax.fori_loop(0, count, step, 0)

        refs = [h0, h1]
        for n in range(SMOOTH):
            if n < SMOOTH - 1:
                smooth(refs[n % 2], refs[(n + 1) % 2], PAD - 8, (h + 16) // 8, True)
            else:
                smooth(refs[n % 2], refs[(n + 1) % 2], PAD, h // 8, False)
        if keep:
            for s, out in enumerate(outs[1:]):
                c = lax.rem(me[1] + s, plan.cross)
                lanes = pl.ds(pl.multiple_of(c * plan.cols_here, plan.cols_here), plan.cols_here)
                out[...] = kept[:, lanes]

    tall = pltpu.VMEM((h + 2 * PAD, plan.cols), F32)
    flat = (h, plan.cols)
    if keep:
        outs = [jax.ShapeDtypeStruct((plan.devices, h, plan.width), F32)]
        outs += [jax.ShapeDtypeStruct((h, plan.cols_here), F32)] * plan.cross
    else:
        outs = [jax.ShapeDtypeStruct(flat, F32)]
    return call(body, outs, [tall] * 3 + [pltpu.VMEM(flat, F32)], (), () if keep else (0,))(
        kappa, above, below, part, beside, *rest
    )


def rows_heat(plan, matrices, table, received, alpha, side_table, side_alpha):
    width = plan.width
    outer = plan.rows // INNER
    per = INNER // plan.height
    two_rows = lambda a, b: lax.dot_general(a, b, (((1,), (1,)), ((), ())), preferred_element_type=F32)

    def sides(matrices, received, side_table, side_alpha, from_left, from_right):
        h = plan.height
        lane = lax.broadcasted_iota(jnp.int32, (8, INNER), 1)
        row = lambda part: side_table[part : part + 1, :]
        points = []
        for a in range(outer):
            re = jnp.zeros((8, INNER), F32)
            im = re
            for j in range(per):
                part = received[a * per + j, 2 * h : 2 * h + 8, :]
                here = (lane >= j * h) & (lane < (j + 1) * h)
                re = jnp.where(here, pltpu.roll(part, j * h, 1) if j else part, re)
                im = jnp.where(here, pltpu.roll(part, (j * h + INNER - h) % INNER, 1), im)
            points.append((re, im))
        values = []
        for k, value in enumerate(small_fft(points, -1)):
            if k:
                value = times(value, (row(k), row(outer + k)))
            high, low = split(jnp.concatenate(value, axis=1))
            both = two_rows(jnp.concatenate([high, low], axis=0), matrices[k, 0])
            value = both[0:8] + both[8:16] + two_rows(jnp.concatenate([high, high], axis=0), matrices[k, 1])[0:8]
            value = (value[:, :INNER], value[:, INNER:])
            if k:
                value = times(value, (row(k), -row(outer + k)))
            values.append(value)
        deposits = [side_alpha[...] * (re * re + im * im) for re, im in small_fft(values, 1)]
        high, low = split(jnp.concatenate(deposits, axis=0))
        ones = lower_ones(INNER)
        sums = two_rows(high, ones) + two_rows(low, ones)
        carry = jnp.zeros((8, 1), F32)
        none = jnp.zeros((6, INNER), F32)
        for a in range(outer):
            part = sums[8 * a : 8 * a + 8] + carry
            carry = part[:, INNER - 1 : INNER]
            n = slice(a * INNER, (a + 1) * INNER)
            from_left[:, n] = jnp.concatenate([none, part[0:2]], axis=0)
            from_right[:, n] = jnp.concatenate([part[2:4], none], axis=0)

    def body(matrices, table, received, alpha, side_table, side_alpha, heat, from_left, from_right, xh, z, dep):
        def write(a, off, value):
            deposit = alpha[...] * (value[0] * value[0] + value[1] * value[1])
            rows = pl.ds(a * INNER + off, CHUNK)
            dep[rows, 0:width], dep[rows, width : 2 * width] = split(deposit)

        sides(matrices, received, side_table, side_alpha, from_left, from_right)
        along_rows(functools.partial(plan.flip_a, received), write, matrices, table, xh, z)
        tile = 2 * INNER
        ones = lower_ones(tile)
        carry = jnp.zeros((1, width), F32)
        for g in range(plan.rows // tile):
            both = jnp.dot(ones, dep[g * tile : (g + 1) * tile, :], preferred_element_type=F32)
            value = both[:, :width] + both[:, width:] + carry
            heat[g * tile : (g + 1) * tile, :] = value
            carry = value[tile - 1 : tile, :]

    edge = jax.ShapeDtypeStruct((8, plan.rows), F32)
    outs = [jax.ShapeDtypeStruct((plan.rows, width), F32), edge, edge]
    scratch = plan.work_a() + [pltpu.VMEM((plan.rows, 2 * width), BF16)]
    return call(body, outs, scratch, (0, 1, 2), ())(matrices, table, received, alpha, side_table, side_alpha)


def rows_turn(plan, read_field, wide, dft, table, screen, field):
    def body(dft, table, screen, field, out, *work):
        def read(a, off):
            return screened(read_field(field, a, off), screen[pl.ds(a * INNER + off, CHUNK), :])

        along_rows(read, functools.partial(plan.send_a, out), dft, table, *work)
        if wide:
            plan.send_edges(out)

    out = plan.sent_wide if wide else plan.sent
    return call(body, [out], plan.work_a(), (0, 1, 2), (0,))(dft, table, screen, field)[0]


def rows_smooth(plan, heat, from_left, from_right, kappa, kappa_left, kappa_right, me):
    width = plan.width
    PAD = 8
    step_rows = 32

    def body(heat, from_left, from_right, kappa, kappa_left, kappa_right, me, screen, h0, h1, kx):
        place = me[1] * plan.wind + plan.local(me[0], me[1])
        zeros = jnp.zeros((PAD, 2 * width), F32)
        for ref in (h0, h1, kx):
            ref[0:PAD, :] = zeros
            ref[plan.rows + PAD : plan.rows + 2 * PAD, :] = zeros
        for g in range(plan.rows // INNER):
            n = slice(g * INNER, (g + 1) * INNER)
            spot = slice(PAD + g * INNER, PAD + (g + 1) * INNER)
            for ref, value, left, right in ((h0, heat, from_left, from_right), (kx, kappa, kappa_left, kappa_right)):
                ref[spot, 0:width] = value[n, :]
                beside = [right[:, n], jnp.zeros((width - 16, INNER), F32), left[:, n]]
                ref[spot, width : 2 * width] = jnp.concatenate(beside, axis=0).T
        wide = lax.broadcasted_iota(jnp.int32, (step_rows, 2 * width), 1)
        bad = (wide >= width) & (wide < width + width // 2) & (place == plan.devices - 1)
        bad = bad | ((wide >= width + width // 2) & (place == 0))

        def smooth(src, dst):
            def one(base):
                value = src[pl.ds(base, step_rows + 16), :]
                kap = kx[pl.ds(base, step_rows + 16), :]
                mid, k_mid = value[8:-8], kap[8:-8]
                new = conducted(
                    mid, value[7:-9], value[9:-7], pltpu.roll(mid, 1, 1), pltpu.roll(mid, 2 * width - 1, 1),
                    k_mid, kap[7:-9], kap[9:-7], pltpu.roll(k_mid, 1, 1), pltpu.roll(k_mid, 2 * width - 1, 1),
                )
                dst(base, jnp.where(bad, 0.0, new))

            def step(i, carry):
                for n in range(4):
                    one(pl.multiple_of((4 * i + n) * step_rows, step_rows))
                return carry

            lax.fori_loop(0, plan.rows // (4 * step_rows), step, 0)

        def into(ref):
            def put(base, value):
                ref[pl.ds(base + PAD, step_rows), :] = value

            return put

        def into_screen(base, value):
            screen[pl.ds(base, step_rows), :] = -value[:, :width]

        refs = [h0, h1]
        for n in range(SMOOTH):
            smooth(refs[n % 2], into(refs[(n + 1) % 2]) if n < SMOOTH - 1 else into_screen)

    tall = pltpu.VMEM((plan.rows + 2 * PAD, 2 * width), F32)
    outs = [jax.ShapeDtypeStruct((plan.rows, width), F32)]
    return call(body, outs, [tall] * 3, (), (0,))(heat, from_left, from_right, kappa, kappa_left, kappa_right, me)[0]


def next_prev(value_up, value_down, axes, order):
    up = list(zip(order[:-1], order[1:]))
    down = [(j, i) for i, j in up]
    return lax.ppermute(value_up, axes, up), lax.ppermute(value_down, axes, down)


def extended(shard, sides, width):
    for axis, dim in sides:
        size, length = (lax.axis_size(axis), shard.shape[dim])
        up = [(i, (i + 1) % size) for i in range(size - 1)]
        down = [(j, i) for i, j in up]
        last = lax.slice_in_dim(shard, length - width, length, axis=dim)
        initial = lax.slice_in_dim(shard, 0, width, axis=dim)
        before = lax.ppermute(last, axis, up)
        after = lax.ppermute(initial, axis, down)
        shard = jnp.concatenate([before, shard, after], axis=dim)
    return shard


def carried_in(part, axis, combine, identity):
    place = lax.axis_index(axis)
    gathered = lax.all_gather(part, axis)
    state = jnp.zeros_like(part) + jnp.asarray(identity, part.dtype)

    def one(turn, state):
        return combine(state, lax.dynamic_index_in_dim(gathered, turn, 0, False))

    return lax.fori_loop(0, place, one, state)


def signed_freq(indices, length):
    shifted = jnp.where(indices < length // 2, indices, indices - length)
    return shifted.astype(jnp.float32) / length


def trig_table(first_ids, second_ids, length, sign_value):
    product = first_ids * second_ids % length
    phase_angle = product.astype(jnp.float32) * (sign_value * 2.0 * math.pi / length)
    return (jnp.cos(phase_angle), jnp.sin(phase_angle))


def complex_product(formula, real_part, imag_part, cosine, sine):
    highest = lax.Precision.HIGHEST
    out_real = jnp.einsum(formula, real_part, cosine, precision=highest) - jnp.einsum(
        formula, imag_part, sine, precision=highest
    )
    out_imag = jnp.einsum(formula, real_part, sine, precision=highest) + jnp.einsum(
        formula, imag_part, cosine, precision=highest
    )
    return (out_real, out_imag)


def transform(stacked, axis_dim, inverse):
    full_shape = stacked.shape
    length = full_shape[axis_dim]
    inner_len = math.gcd(length, 128)
    outer_len = length // inner_len
    leading = full_shape[1] if axis_dim == 2 else 1
    trailing = full_shape[2] if axis_dim == 1 else 1
    blocks = stacked.reshape(2, leading, outer_len, inner_len, trailing)
    sign_value = 1.0 if inverse else -1.0
    outer_ids = jnp.arange(outer_len, dtype=jnp.int32)
    inner_ids = jnp.arange(inner_len, dtype=jnp.int32)
    cos_outer, sin_outer = trig_table(outer_ids[:, None], outer_ids[None, :], outer_len, sign_value)
    first_real, first_imag = complex_product(
        "pabq,ak->pkbq", blocks[0], blocks[1], cos_outer, sin_outer
    )
    cos_twist, sin_twist = trig_table(outer_ids[:, None], inner_ids[None, :], length, sign_value)
    cos_twist = cos_twist[None, :, :, None]
    sin_twist = sin_twist[None, :, :, None]
    twist_real = first_real * cos_twist - first_imag * sin_twist
    twist_imag = first_real * sin_twist + first_imag * cos_twist
    cos_inner, sin_inner = trig_table(inner_ids[:, None], inner_ids[None, :], inner_len, sign_value)
    second_real, second_imag = complex_product(
        "pkbq,bm->pkmq", twist_real, twist_imag, cos_inner, sin_inner
    )
    result = jnp.stack([second_real, second_imag]).transpose(0, 1, 3, 2, 4).reshape(full_shape)
    if inverse:
        result = result * (1.0 / length)
    return result


def apply_phase(stacked, phase_angle):
    cosine = jnp.cos(phase_angle)
    sine = jnp.sin(phase_angle)
    return jnp.stack(
        [stacked[0] * cosine - stacked[1] * sine, stacked[0] * sine + stacked[1] * cosine]
    )


def along_joint(stacked, phase_rate, row_freq, col_freq):
    cross_count = lax.axis_size("cross")
    stacked = lax.all_to_all(stacked, ("wind", "cross"), split_axis=2, concat_axis=1, tiled=True)
    stacked = transform(stacked, 1, False)
    col_width = stacked.shape[2]
    joint_block = lax.axis_index("wind") * cross_count + lax.axis_index("cross")
    cols_held = lax.dynamic_slice_in_dim(col_freq, joint_block * col_width, col_width)
    phase_angle = -phase_rate * (
        row_freq[:, None] * row_freq[:, None] + cols_held[None, :] * cols_held[None, :]
    )
    stacked = apply_phase(stacked, phase_angle)
    stacked = transform(stacked, 1, True)
    return lax.all_to_all(stacked, ("wind", "cross"), split_axis=1, concat_axis=2, tiled=True)


def propagate_slab(slab_pair, share_step):
    rows_total = slab_pair.shape[1] * lax.axis_size("wind") * lax.axis_size("cross")
    cols_total = slab_pair.shape[2]
    phase_rate = share_step * diffraction
    row_freq = signed_freq(jnp.arange(rows_total, dtype=jnp.int32), rows_total)
    col_freq = signed_freq(jnp.arange(cols_total, dtype=jnp.int32), cols_total)
    stacked = transform(slab_pair, 2, False)
    stacked = along_joint(stacked, phase_rate, row_freq, col_freq)
    return transform(stacked, 2, True)


def conduct_core(padded, kappa_pad):
    height = padded.shape[0] - 2
    breadth = padded.shape[1] - 2
    center = padded[1:-1, 1:-1]
    kappa_mid = kappa_pad[1:-1, 1:-1]
    flux_sum = jnp.zeros_like(center)
    for offset_row, offset_col in ((0, 1), (2, 1), (1, 0), (1, 2)):
        neighbour = padded[offset_row : offset_row + height, offset_col : offset_col + breadth]
        kappa_side = kappa_pad[offset_row : offset_row + height, offset_col : offset_col + breadth]
        flux_sum = flux_sum + 0.5 * (kappa_mid + kappa_side) * (neighbour - center)
    return center + conduct_rate * flux_sum


def add_terms(earlier, later_term):
    return earlier + later_term


def layer_absorption(index_row, table_row, level_ids):
    one_hot = (index_row[:, None] == level_ids[None, :]).astype(jnp.float32)
    return jnp.sum(one_hot * table_row[None, :], axis=1)


def wide_device(field_real, field_imag, absorb_index, absorb_table, zone_map, zone_conductivity):
    rows_here, cols_here = field_real.shape
    conductivity = jnp.zeros((rows_here, cols_here), jnp.float32)
    for zone_no in range(zone_conductivity.shape[0]):
        conductivity = jnp.where(zone_map == zone_no, zone_conductivity[zone_no], conductivity)
    level_ids = jnp.arange(absorb_table.shape[1], dtype=jnp.int32)
    combined = lax.all_to_all(
        jnp.stack([field_real, field_imag, conductivity]),
        "cross",
        split_axis=1,
        concat_axis=2,
        tiled=True,
    )
    slab_pair = combined[:2]
    kappa_rows = extended(combined[2], ((("wind", "cross"), 0),), 1)
    kappa_pad = jnp.pad(kappa_rows, ((0, 0), (1, 1)))
    index_full = lax.all_gather(absorb_index, "cross", axis=1, tiled=True)
    slab_rows = slab_pair.shape[1]
    rows_total = slab_rows * lax.axis_size("wind") * lax.axis_size("cross")
    slab_ids = jnp.arange(slab_rows, dtype=jnp.int32)
    lower_slab = (slab_ids[:, None] >= slab_ids[None, :]).astype(jnp.float32)
    screen_phase = jnp.zeros((slab_rows, slab_pair.shape[2]), jnp.float32)
    for layer_no in range(LAYERS):
        absorption = layer_absorption(index_full[layer_no], absorb_table[layer_no], level_ids)
        screen_phase = jnp.zeros((slab_rows, slab_pair.shape[2]), jnp.float32)
        for _ in range(ITERS):
            middle = propagate_slab(apply_phase(slab_pair, screen_phase), 0.5)
            intensity = middle[0] * middle[0] + middle[1] * middle[1]
            deposit = absorption[None, :] * intensity * (1.0 / rows_total)
            partial_heat = jnp.dot(lower_slab, deposit, precision=lax.Precision.HIGHEST)
            totals = partial_heat[-1]
            upstream = carried_in(totals, ("wind", "cross"), add_terms, jnp.zeros_like(totals))
            heat_field = partial_heat + upstream[None, :]
            for _ in range(SMOOTH):
                padded = extended(heat_field, ((("wind", "cross"), 0),), 1)
                padded = jnp.pad(padded, ((0, 0), (1, 1)))
                heat_field = conduct_core(padded, kappa_pad)
            screen_phase = -heat_field
        slab_pair = propagate_slab(apply_phase(slab_pair, screen_phase), 1.0)
    returned = lax.all_to_all(
        jnp.stack([slab_pair[0], slab_pair[1], screen_phase]),
        "cross",
        split_axis=2,
        concat_axis=1,
        tiled=True,
    )
    return (returned[0], returned[1], returned[2])


def on_device(field_real, field_imag, absorb_index, absorb_table, zone_map, zone_conductivity):
    plan = Plan(*field_real.shape, lax.axis_size("wind"), lax.axis_size("cross"))
    fits = plan.width == INNER and INNER % plan.height == 0 and plan.height % CHUNK == 0
    if not fits or plan.rows_here % INNER or plan.rows % (2 * INNER):
        return wide_device(field_real, field_imag, absorb_index, absorb_table, zone_map, zone_conductivity)
    return tiled_device(plan, field_real, field_imag, absorb_index, absorb_table, zone_map, zone_conductivity)


def tiled_device(plan, field_real, field_imag, absorb_index, absorb_table, zone_map, zone_conductivity):
    cross = plan.cross
    w, c = lax.axis_index("wind"), lax.axis_index("cross")
    place = jnp.stack([w, c]).astype(jnp.int32)
    grid_axes = ("wind", "cross")

    def exchange(x, axes):
        return lax.all_to_all(x, axes, split_axis=0, concat_axis=0, tiled=True)

    def flip(x):
        return exchange(x, grid_axes)

    to_b, *field_blocks = prepare_field(plan, field_real, field_imag, place)
    home_b = exchange(to_b, "cross")
    field_blocks = shifted(field_blocks, "wind")
    *across, kappa, left, right, alpha_a, alpha = prepare(
        plan, zone_map, absorb_index, absorb_table, zone_conductivity, place
    )
    side_alpha, *along = home_kappa(plan, kappa, *next_prev(right, left, "cross", list(range(cross))), alpha, place)

    dft = jnp.asarray(dft_matrices())
    tab_a = lambda share: (jnp.asarray(row_blocks(plan.rows, share)), jnp.asarray(row_table(plan.rows)))
    tab_b_of = lambda length: jnp.asarray(chirp_columns(length, ()))
    tab_b = lambda *shares: jnp.asarray(chirp_columns(plan.cols, shares))

    def smooth_a(layer, share, received):
        heat, from_left, from_right = rows_heat(
            plan, *tab_a(share), received, alpha_a[layer : layer + 1], tab_b_of(plan.rows), side_alpha[layer]
        )
        return rows_smooth(plan, heat, from_left, from_right, *kappas, place)

    def smooth_b(layer, keep, received):
        part, beside, totals = cols_heat(plan, layer, plan.devices, dft, tab_b(0.5), received, alpha_b)
        return cols_smooth(plan, keep, kappa_b, above, below, part, beside, flip(totals), place)

    home_b, across = lax.optimization_barrier((home_b, across))
    sent = cols_send(plan, plan.home_b, False, dft, tab_b(0.5), home_b, True)
    kappa_b, alpha_b = home_rows(plan, shifted(across, "cross"), place)
    above, below = next_prev(kappa_b[-8:], kappa_b[:8], grid_axes, list(range(plan.devices)))
    received, along = lax.optimization_barrier((flip(sent), along))
    along = shifted(along, "wind")
    kappas = rows_kappa(plan, along, place)
    home_a = in_order(field_blocks, place, 0)
    screen = smooth_a(0, 0.5, received)
    sent = rows_turn(plan, plan.home_a, True, *tab_a(0.5), screen, home_a)
    received, above, below = lax.optimization_barrier((flip(sent), above, below))
    (screen,) = smooth_b(0, False, received)
    sent_middle, sent_field = cols_turn(plan, plan.home_b, 2, dft, tab_b(1.5, 1.0), screen, home_b)
    middle = flip(sent_middle)
    field = flip(sent_field)
    screen = smooth_a(1, 1.5, middle)
    field, screen = lax.optimization_barrier((field, screen))
    field = rows_field(plan, plan.flip_a, *tab_a(1.0), field)
    sent = rows_turn(plan, plan.flip_a, True, *tab_a(0.5), screen, field)
    screen, *home_parts = smooth_b(1, True, flip(sent))
    home_parts = shifted(home_parts, "cross")
    screen = flip(screen).reshape(plan.rows, plan.width)
    sent = rows_turn(plan, plan.flip_a, False, *tab_a(1.0), screen, field)
    back = cols_send(plan, plan.flip_b, True, dft, tab_b(1.0), flip(sent))
    screen = home_screen(plan, home_parts, place)
    back = exchange(back, "cross")
    out_real = back[:, : plan.height].reshape(field_real.shape)
    out_imag = back[:, plan.height :].reshape(field_real.shape)
    return (out_real, out_imag, screen)


def solution(mesh):
    in_specs = (
        P(("beams", "wind"), "cross"),
        P(("beams", "wind"), "cross"),
        P(None, "cross"),
        P(),
        P("wind", "cross"),
        P(),
    )
    out_specs = (
        P(("beams", "wind"), "cross"),
        P(("beams", "wind"), "cross"),
        P(("beams", "wind"), "cross"),
    )
    return jax.shard_map(on_device, mesh=mesh, in_specs=in_specs, out_specs=out_specs, check_vma=False)
```

```python
import functools
import math

import jax
import jax.numpy as jnp
import numpy as np
from jax import lax
from jax.experimental import pallas as pl
from jax.experimental.pallas import tpu as pltpu
from jax.sharding import PartitionSpec as P


LAYERS = 2
ITERS = 2
SMOOTH = 2
INNER = 128
CHUNK = 16

diffraction = 2000.0
conduct_rate = 0.24

F32 = jnp.float32
BF16 = jnp.bfloat16
WHOLE = pl.BlockSpec(memory_space=pltpu.VMEM)
SCALAR = pl.BlockSpec(memory_space=pltpu.SMEM)


def split_np(values):
    high = values.astype(np.float32).astype(jnp.bfloat16)
    low = (values - high.astype(np.float64)).astype(np.float32).astype(jnp.bfloat16)
    return high, low


def dft_matrices():
    ids = np.arange(INNER)
    angle = 2.0 * np.pi * (np.outer(ids, ids) % INNER) / INNER
    cosine, sine = np.cos(angle), np.sin(angle)
    left = np.block([[cosine, sine], [-sine, cosine]])
    return np.stack([*split_np(left), *split_np(left.T)])


def chirp_columns(length, shares):
    outer = length // INNER
    k = np.arange(outer)[:, None]
    m = np.arange(INNER)[None, :]
    twist = -2.0 * np.pi * ((k * m) % length) / length
    tables = [np.cos(twist), np.sin(twist)]
    p = k + outer * m
    freq = np.where(p < length // 2, p, p - length) / length
    for share in shares:
        angle = -share * diffraction * freq * freq
        tables += [np.cos(angle) / length, np.sin(angle) / length]
    return np.concatenate(tables, axis=0).astype(np.float32)


def row_table(length):
    cols = chirp_columns(length, ()).T
    return np.pad(cols, ((0, 0), (0, -cols.shape[1] % 128)))


def row_blocks(length, share):
    outer = length // INNER
    ids = np.arange(INNER)
    forward = np.exp(-2j * np.pi * (np.outer(ids, ids) % INNER) / INNER)
    blocks = []
    for k in range(outer):
        p = k + outer * ids
        freq = np.where(p < length // 2, p, p - length) / length
        block = forward.conj() @ (np.exp(-1j * share * diffraction * freq * freq)[:, None] / length * forward)
        blocks.append(np.stack(split_np(np.block([[block.real, -block.imag], [block.imag, block.real]]))))
    return np.stack(blocks)


def split(x):
    high = x.astype(BF16)
    return high, (x - high.astype(F32)).astype(BF16)


def times(a, b):
    return (a[0] * b[0] - a[1] * b[1], a[0] * b[1] + a[1] * b[0])


def small_fft(points, sign):
    count = len(points)
    if count == 1:
        return points
    even = small_fft(points[0::2], sign)
    odd = small_fft(points[1::2], sign)
    half = count // 2
    out = [None] * count
    for k in range(half):
        re, im = odd[k]
        if k == 0:
            turn = (re, im)
        elif 4 * k == count:
            turn = (-im, re) if sign > 0 else (im, -re)
        elif 8 * k == count:
            root = math.sqrt(0.5)
            turn = (root * (re - im), root * (im + re)) if sign > 0 else (root * (re + im), root * (im - re))
        elif 8 * k == 3 * count:
            root = math.sqrt(0.5)
            turn = (-root * (re + im), root * (re - im)) if sign > 0 else (root * (im - re), -root * (re + im))
        else:
            c = math.cos(2.0 * math.pi * k / count)
            s = sign * math.sin(2.0 * math.pi * k / count)
            turn = (c * re - s * im, s * re + c * im)
        out[k] = (even[k][0] + turn[0], even[k][1] + turn[1])
        out[k + half] = (even[k][0] - turn[0], even[k][1] - turn[1])
    return out


def cos_sin(x):
    turns = jnp.floor(x * (2.0 / math.pi) + 0.5)
    r = ((x - turns * 1.5703125) - turns * 4.837512969970703125e-4) - turns * 7.549789954891882e-8
    quad = turns.astype(jnp.int32)
    z = r * r
    s = r + r * z * (-1.6666654611e-1 + z * (8.3321608736e-3 - z * 1.9515295891e-4))
    c = 1.0 - 0.5 * z + z * z * (4.166664568298827e-2 + z * (-1.388731625493765e-3 + z * 2.443315711809948e-5))
    odd = (quad & 1) == 1
    sin_x = jnp.where(odd, c, s)
    cos_x = jnp.where(odd, s, c)
    sin_x = jnp.where((quad & 2) == 2, -sin_x, sin_x)
    cos_x = jnp.where(((quad + 1) & 2) == 2, -cos_x, cos_x)
    return cos_x, sin_x


def screened(value, screen):
    return times(value, cos_sin(screen))


def triple(a_high, a_low, b_high, b_low):
    dot = functools.partial(jnp.dot, preferred_element_type=F32)
    return dot(a_high, b_high) + dot(a_high, b_low) + dot(a_low, b_high)


def lower_ones(size):
    r = lax.broadcasted_iota(jnp.int32, (size, size), 0)
    c = lax.broadcasted_iota(jnp.int32, (size, size), 1)
    return jnp.where(r >= c, 1.0, 0.0).astype(BF16)


def chunks(count, body):
    def step(i, carry):
        for n in range(side):
            body(pl.multiple_of((side * i + n) * CHUNK, CHUNK))
        return carry

    side = 2 if count % (2 * CHUNK) == 0 else 1
    lax.fori_loop(0, count // (side * CHUNK), step, 0)


def along_rows(read, write, matrices, table, xh, z):
    outer = matrices.shape[0]
    width = z.shape[1] // outer
    lanes = lambda k: pl.ds(k * width, width)
    col = lambda part, off: table[pl.ds(off, CHUNK), part : part + 1]

    def first(off):
        for k, value in enumerate(small_fft([read(a, off) for a in range(outer)], -1)):
            if k:
                value = times(value, (col(k, off), col(outer + k, off)))
            for at, v in ((0, value[0]), (INNER, value[1])):
                high, low = split(v)
                xh[pl.ds(at + off, CHUNK), pl.ds(2 * k * width, width)] = high
                xh[pl.ds(at + off, CHUNK), pl.ds((2 * k + 1) * width, width)] = low

    def last(off):
        values = []
        for k in range(outer):
            value = (z[pl.ds(off, CHUNK), lanes(k)], z[pl.ds(INNER + off, CHUNK), lanes(k)])
            if k:
                value = times(value, (col(k, off), -col(outer + k, off)))
            values.append(value)
        for a, value in enumerate(small_fft(values, 1)):
            write(a, off, value)

    chunks(INNER, first)
    dot = functools.partial(jnp.dot, preferred_element_type=F32)
    for k in range(outer):
        both = dot(matrices[k, 0], xh[:, 2 * k * width : (2 * k + 2) * width])
        low = dot(matrices[k, 1], xh[:, 2 * k * width : (2 * k + 1) * width])
        z[:, k * width : (k + 1) * width] = both[:, :width] + both[:, width:] + low
    chunks(INNER, last)


def along_cols(main, read, writes, dft, table, xh, xl, y, z):
    outer = table.shape[0] // (2 * (1 + len(writes)))
    height = xh.shape[0] // outer

    def every(body):
        chunks(main, body)
        if height > main:
            body(main)

    row = lambda part: table[part : part + 1, :]

    def put(k, off, value):
        for at, v in ((0, value[0]), (INNER, value[1])):
            spot = (pl.ds(k * height + off, CHUNK), pl.ds(at, INNER))
            xh[spot], xl[spot] = split(v)

    def get(ref, k, off):
        return tuple(ref[pl.ds(k * height + off, CHUNK), pl.ds(at, INNER)] for at in (0, INNER))

    def first(off):
        for k, value in enumerate(small_fft([read(b, off) for b in range(outer)], -1)):
            if k:
                value = times(value, (row(k), row(outer + k)))
            put(k, off, value)

    every(first)
    y[...] = triple(xh[...], xl[...], dft[2], dft[3])
    for n, write in enumerate(writes):

        def middle(off, n=n):
            for k in range(outer):
                base = (2 + 2 * n) * outer + k
                put(k, off, times(get(y, k, off), (row(base), row(base + outer))))

        every(middle)
        z[...] = triple(xh[...], xl[...], dft[0], dft[1])

        def last(off, write=write):
            values = []
            for k in range(outer):
                value = get(z, k, off)
                if k:
                    value = times(value, (row(k), -row(outer + k)))
                values.append(value)
            for b, value in enumerate(small_fft(values, 1)):
                write(b, off, value)

        every(last)


class Plan:
    def __init__(self, rows_here, cols_here, wind, cross):
        self.wind, self.cross = wind, cross
        self.devices = wind * cross
        self.rows_here, self.cols_here = rows_here, cols_here
        self.height = rows_here // cross
        self.width = cols_here // wind
        self.rows, self.cols = rows_here * wind, cols_here * cross

    def local(self, w, c):
        return w + (c % 2) * (self.wind - 1 - 2 * w)

    def slot(self, block):
        c, i = block // self.wind, block % self.wind
        return self.local(i, c) * self.cross + c

    def home_a(self, ref, a, off):
        n = a * INNER
        src, at = n // self.rows_here, n % self.rows_here
        return tuple(ref[src, pl.ds(p * self.rows_here + at + off, CHUNK), :] for p in (0, 1))

    def spot_a(self, a, off):
        per = INNER // self.height
        return a * per + off // self.height, lax.rem(off, self.height)

    def flip_a(self, ref, a, off):
        s, at = self.spot_a(a, off)
        at = pl.multiple_of(at, CHUNK)
        return tuple(ref[s, pl.ds(p * self.height + at, CHUNK), :] for p in (0, 1))

    def send_a(self, ref, a, off, value):
        s, at = self.spot_a(a, off)
        at = pl.multiple_of(at, CHUNK)
        for p in (0, 1):
            ref[s, pl.ds(p * self.height + at, CHUNK), :] = value[p]

    def send_edges(self, ref):
        h = self.height
        for d in range(self.devices):
            for p in (0, 1):
                at = 2 * h + 4 * p
                before = ref[d - 1, p * h + h - 2 : p * h + h, :] if d else jnp.zeros((2, self.width), F32)
                after = ref[d + 1, p * h : p * h + 2, :] if d + 1 < self.devices else jnp.zeros((2, self.width), F32)
                ref[d, at : at + 2, :] = before
                ref[d, at + 2 : at + 4, :] = after

    def edges(self, value, left, right, at):
        turned = value.T
        left[:, at : at + INNER] = turned[0:8, :]
        right[:, at : at + INNER] = turned[self.width - 8 : self.width, :]

    def send_sides(self, ref):
        h, w = self.height, self.width
        last = self.devices - 1
        for b in range(self.devices):
            turned = ref[self.slot(b), 0 : 2 * h, :].T
            if b < last:
                ref[self.slot(b + 1), 2 * h : 2 * h + 2, :] = turned[w - 2 : w, :]
            if b:
                ref[self.slot(b - 1), 2 * h + 2 : 2 * h + 4, :] = turned[0:2, :]
        none = jnp.zeros((2, w), F32)
        ref[self.slot(0), 2 * h : 2 * h + 2, :] = none
        ref[self.slot(last), 2 * h + 2 : 2 * h + 4, :] = none

    def home_b(self, ref, b, off):
        per = self.cols_here // INNER
        return tuple(ref[b // per, pl.ds(p * self.height + off, CHUNK), pl.ds((b % per) * INNER, INNER)] for p in (0, 1))

    def wide_b(self, ref, b, off):
        if isinstance(off, int):
            extra = ref[self.slot(b), 2 * self.height : 2 * self.height + 8, :]
            turned = jnp.concatenate([extra[4:8], extra[0:4]], axis=0)
            return jnp.concatenate([extra, extra], axis=0), jnp.concatenate([turned, turned], axis=0)
        return self.flip_b(ref, b, off)

    def flip_b(self, ref, b, off):
        return tuple(ref[self.slot(b), pl.ds(p * self.height + off, CHUNK), :] for p in (0, 1))

    def send_b(self, ref, b, off, value):
        for p in (0, 1):
            ref[self.slot(b), pl.ds(p * self.height + off, CHUNK), :] = value[p]

    def back_b(self, ref, b, off, value):
        per = self.cols_here // INNER
        for p in (0, 1):
            ref[b // per, pl.ds(p * self.height + off, CHUNK), pl.ds((b % per) * INNER, INNER)] = value[p]

    @property
    def sent(self):
        return jax.ShapeDtypeStruct((self.devices, 2 * self.height, self.width), F32)

    def work_a(self):
        wide = (self.rows // INNER) * self.width
        return [
            pltpu.VMEM((2 * INNER, 2 * wide), BF16),
            pltpu.VMEM((2 * INNER, wide), F32),
        ]

    @property
    def sent_wide(self):
        return jax.ShapeDtypeStruct((self.devices, 2 * self.height + 8, self.width), F32)

    def work_b(self, extra=0):
        tall = (self.cols // INNER) * (self.height + extra)
        return [
            pltpu.VMEM((tall, 2 * INNER), BF16),
            pltpu.VMEM((tall, 2 * INNER), BF16),
            pltpu.VMEM((tall, 2 * INNER), F32),
            pltpu.VMEM((tall, 2 * INNER), F32),
        ]


def call(body, outs, scratch, near=(), near_outs=(), far=(), far_outs=()):
    def run(*args):
        specs = [SCALAR if a.size <= 16 else WHOLE for a in args]
        spaces = [pltpu.VMEM if i in near else pltpu.HBM if i in far else None for i in range(len(args))]
        args = [pltpu.with_memory_space_constraint(a, space) if space else a for a, space in zip(args, spaces)]
        return pl.pallas_call(
            body,
            out_shape=[
                pltpu.VMEM(o.shape, o.dtype) if i in near_outs else pltpu.HBM(o.shape, o.dtype) if i in far_outs else o
                for i, o in enumerate(outs)
            ],
            in_specs=specs,
            out_specs=[WHOLE] * len(outs),
            scratch_shapes=scratch,
            compiler_params=pltpu.CompilerParams(vmem_limit_bytes=14 * 1024 * 1024),
        )(*args)

    return run


def prepare_field(plan, field_real, field_imag, place):
    h = plan.height

    def body(real, imag, place, to_b, *to_a):
        for c in range(plan.cross):
            to_b[c, 0:h, :] = real[c * h : (c + 1) * h, :]
            to_b[c, h : 2 * h, :] = imag[c * h : (c + 1) * h, :]
        for t, out in enumerate(to_a):
            n = lax.rem(place[0] + t, plan.wind)
            lanes = pl.ds(pl.multiple_of(plan.local(n, place[1]) * plan.width, plan.width), plan.width)
            out[0 : plan.rows_here, :] = real[:, lanes]
            out[plan.rows_here : 2 * plan.rows_here, :] = imag[:, lanes]

    outs = [jax.ShapeDtypeStruct((plan.cross, 2 * h, plan.cols_here), F32)]
    outs += [jax.ShapeDtypeStruct((2 * plan.rows_here, plan.width), F32)] * plan.wind
    return call(body, outs, [], (), (), (0, 1))(field_real, field_imag, place)


def prepare(plan, zone_map, absorb_index, absorb_table, zone_conductivity, place):
    h = plan.height

    def picked(ids, count, level):
        value = jnp.zeros(ids.shape, F32)
        for n in range(count):
            value = jnp.where(ids == n, level(n), value)
        return value

    def body(zones, index, table, levels, place, *refs):
        to_b, (kappa, left, right, alpha_a, alpha) = refs[: plan.cross], refs[plan.cross :]
        w, c = place[0], place[1]

        def step(off):
            kappa[pl.ds(off, CHUNK), :] = picked(zones[pl.ds(off, CHUNK), :], levels.shape[0], lambda n: levels[n])

        chunks(plan.rows_here, step)
        alpha[...] = jnp.zeros_like(alpha)
        for layer in range(LAYERS):
            value = picked(index[layer : layer + 1, :], table.shape[1], lambda n: table[layer, n])
            alpha[layer : layer + 1, :] = value * (1.0 / plan.rows)
        alpha_a[...] = alpha[:, pl.ds(pl.multiple_of(plan.local(w, c) * plan.width, plan.width), plan.width)]
        for s, out in enumerate(to_b):
            out[0:h, :] = kappa[pl.ds(pl.multiple_of(lax.rem(c + s, plan.cross) * h, h), h), :]
            out[h:, :] = alpha[...]
        for at in range(0, plan.rows_here, INNER):
            left[0:8, at : at + INNER] = kappa[at : at + INNER, 0 : plan.width].T[0:8, :]
            right[0:8, at : at + INNER] = kappa[at : at + INNER, plan.cols_here - plan.width :].T[plan.width - 8 :, :]
        left[8:16, :] = jnp.zeros((8, plan.rows_here), F32)
        right[8:16, :] = jnp.zeros((8, plan.rows_here), F32)
        left[8:16, 0:INNER] = alpha[:, 0 : plan.width]
        right[8:16, 0:INNER] = alpha[:, plan.cols_here - plan.width :]

    edge = jax.ShapeDtypeStruct((16, plan.rows_here), F32)
    outs = [jax.ShapeDtypeStruct((h + 8, plan.cols_here), F32)] * plan.cross
    outs += [jax.ShapeDtypeStruct(zone_map.shape, F32), edge, edge, jax.ShapeDtypeStruct((8, plan.width), F32)]
    outs.append(jax.ShapeDtypeStruct((8, plan.cols_here), F32))
    return call(body, outs, [], (), (), (0,))(
        zone_map, absorb_index, absorb_table, zone_conductivity, place
    )


def home_kappa(plan, kappa, from_left, from_right, alpha, place):
    per = plan.rows_here // INNER

    def body(kappa, from_left, from_right, alpha, place, side_alpha, *refs):
        outs, edges = refs[: plan.wind], refs[-1]
        mine = plan.local(place[0], place[1])
        side_alpha[...] = jnp.zeros_like(side_alpha)
        for i in range(plan.wind):

            @pl.when(mine == i)
            def _():
                for layer in range(LAYERS):
                    line = slice(layer, layer + 1)
                    before = alpha[line, (i - 1) * plan.width : i * plan.width] if i else from_left[8 + layer : 9 + layer, 0:INNER]
                    last = i + 1 == plan.wind
                    after = from_right[8 + layer : 9 + layer, 0:INNER] if last else alpha[line, (i + 1) * plan.width : (i + 2) * plan.width]
                    for n, value in enumerate((before[:, -2:-1], before[:, -1:], after[:, 0:1], after[:, 1:2])):
                        side_alpha[layer, n : n + 1, :] = jnp.broadcast_to(value, (1, INNER))

        for at in range(per):
            n = slice(at * INNER, (at + 1) * INNER)
            edges[0, 8 * at : 8 * at + 8, :] = from_left[0:8, n]
            edges[plan.wind - 1, 8 * (per + at) : 8 * (per + at) + 8, :] = from_right[0:8, n]
            for i in range(plan.wind):
                turned = kappa[n, i * plan.width : (i + 1) * plan.width].T
                if i + 1 < plan.wind:
                    edges[i + 1, 8 * at : 8 * at + 8, :] = turned[plan.width - 8 :, :]
                if i:
                    edges[i - 1, 8 * (per + at) : 8 * (per + at) + 8, :] = turned[0:8, :]
        for t, out in enumerate(outs):
            i = plan.local(lax.rem(place[0] + t, plan.wind), place[1])
            out[0 : plan.rows_here, :] = kappa[:, pl.ds(pl.multiple_of(i * plan.width, plan.width), plan.width)]
            out[plan.rows_here :, :] = edges[i]

    outs = [jax.ShapeDtypeStruct((LAYERS, 8, INNER), F32)]
    outs += [jax.ShapeDtypeStruct((plan.rows_here + 16 * per, plan.width), F32)] * plan.wind
    scratch = [pltpu.VMEM((plan.wind, 16 * per, INNER), F32)]
    return call(body, outs, scratch)(
        kappa, from_left, from_right, alpha, place
    )


def home_rows(plan, parts, place):
    h = plan.height

    def body(*refs):
        place, kappa, alpha = refs[plan.cross :]
        for s, ref in enumerate(refs[: plan.cross]):
            c = lax.rem(place[1] + plan.cross - s, plan.cross)
            lanes = pl.ds(pl.multiple_of(c * plan.cols_here, plan.cols_here), plan.cols_here)
            kappa[:, lanes] = ref[0:h, :]
            alpha[:, lanes] = ref[h:, :]

    outs = [jax.ShapeDtypeStruct((h, plan.cols), F32), jax.ShapeDtypeStruct((8, plan.cols), F32)]
    return call(body, outs, [])(*parts, place)


def shifted(parts, axis):
    size = lax.axis_size(axis)
    return [parts[0]] + [lax.ppermute(parts[s], axis, [(i, (i + s) % size) for i in range(size)]) for s in range(1, size)]


def in_order(parts, place, which):
    size = len(parts)

    def body(*refs):
        place, out = refs[size], refs[-1]
        for s, ref in enumerate(refs[:size]):
            out[lax.rem(place[which] + size - s, size)] = ref[...]

    out = jax.ShapeDtypeStruct((size,) + parts[0].shape, F32)
    return call(body, [out], [], range(size))(*parts, place)[0]


def home_screen(plan, parts, place):
    h = plan.height

    def body(*refs):
        place, out = refs[plan.cross], refs[-1]
        for s, ref in enumerate(refs[: plan.cross]):
            c = lax.rem(place[1] + plan.cross - s, plan.cross)
            out[pl.ds(pl.multiple_of(c * h, h), h), :] = ref[...]

    out = jax.ShapeDtypeStruct((plan.rows_here, plan.cols_here), F32)
    return call(body, [out], [])(*parts, place)[0]


def rows_kappa(plan, parts, place):
    per = plan.rows_here // INNER

    def body(*refs):
        place, out, left, right = refs[plan.wind :]
        for t, ref in enumerate(refs[: plan.wind]):
            first = lax.rem(place[0] + plan.wind - t, plan.wind) * plan.rows_here
            out[pl.ds(pl.multiple_of(first, plan.rows_here), plan.rows_here), :] = ref[0 : plan.rows_here, :]
            for at in range(per):
                n = pl.ds(pl.multiple_of(first + at * INNER, INNER), INNER)
                line = plan.rows_here + 8 * at
                left[:, n] = ref[line : line + 8, :]
                right[:, n] = ref[line + 8 * per : line + 8 * per + 8, :]

    edge = jax.ShapeDtypeStruct((8, plan.rows), F32)
    outs = [jax.ShapeDtypeStruct((plan.rows, plan.width), F32), edge, edge]
    return call(body, outs, [], range(plan.wind))(*parts, place)


def rows_field(plan, read_field, dft, table, field):
    def body(dft, table, field, out, *work):
        along_rows(functools.partial(read_field, field), functools.partial(plan.send_a, out), dft, table, *work)

    return call(body, [plan.sent], plan.work_a(), (0, 1, 2), (0,))(dft, table, field)[0]


def cols_send(plan, read_field, back, dft, table, field, sides=False):
    out = plan.sent_wide if sides else plan.sent
    if back:
        out = jax.ShapeDtypeStruct((plan.cross, 2 * plan.height, plan.cols_here), F32)

    def body(dft, table, field, out, *work):
        put = plan.back_b if back else plan.send_b
        along_cols(plan.height, functools.partial(read_field, field), [functools.partial(put, out)], dft, table, *work)
        if sides:
            plan.send_sides(out)

    return call(body, [out], plan.work_b(), (0, 1, 2), () if back else (0,))(dft, table, field)[0]


def cols_heat(plan, layer, copies, dft, table, received, absorption):
    blocks = plan.cols // INNER
    h = plan.height

    def body(dft, table, received, absorption, part, beside, totals, xh, xl, y, z, dh, dl):
        def write(b, off, value):
            alpha = absorption[layer : layer + 1, pl.ds(b * INNER, INNER)]
            deposit = alpha * (value[0] * value[0] + value[1] * value[1])
            lanes = pl.ds(b * INNER, INNER)
            if isinstance(off, int):
                beside[:, lanes] = deposit[0:8]
                return
            spot = (pl.ds(off, CHUNK), lanes)
            dh[spot], dl[spot] = split(deposit)

        along_cols(h, functools.partial(plan.wide_b, received), [write], dft, table, xh, xl, y, z)
        ones = lower_ones(h)
        dot = functools.partial(jnp.dot, preferred_element_type=F32)
        part[...] = dot(ones, dh[...]) + dot(ones, dl[...])
        for b in range(blocks):
            total = part[h - 1 : h, b * INNER : (b + 1) * INNER]
            for d in range(copies):
                totals[d, b : b + 1, :] = total

    outs = [
        jax.ShapeDtypeStruct((h, plan.cols), F32),
        jax.ShapeDtypeStruct((8, plan.cols), F32),
        jax.ShapeDtypeStruct((copies, blocks, INNER), F32),
    ]
    scratch = plan.work_b(CHUNK) + [pltpu.VMEM((h, plan.cols), BF16), pltpu.VMEM((h, plan.cols), BF16)]
    return call(body, outs, scratch, (0, 1, 2), ())(dft, table, received, absorption)


def conducted(mid, up, down, left, right, k_mid, k_up, k_down, k_left, k_right):
    flux = (k_mid + k_up) * (up - mid) + (k_mid + k_down) * (down - mid)
    flux = flux + (k_mid + k_left) * (left - mid) + (k_mid + k_right) * (right - mid)
    return mid + (0.5 * conduct_rate) * flux


def cols_turn(plan, read_field, sets, dft, table, screen, field):
    def body(dft, table, screen, field, *refs):
        outs, work = refs[:sets], refs[sets:]

        def read(b, off):
            return screened(read_field(field, b, off), screen[pl.ds(off, CHUNK), pl.ds(b * INNER, INNER)])

        along_cols(plan.height, read, [functools.partial(plan.send_b, out) for out in outs], dft, table, *work)
        if sets > 1:
            plan.send_sides(outs[0])

    return call(body, [plan.sent_wide if sets > 1 and n == 0 else plan.sent for n in range(sets)], plan.work_b(), (0, 1, 2), range(sets))(
        dft, table, screen, field
    )


def cols_smooth(plan, keep, kappa, above, below, part, beside, *rest):
    blocks = plan.cols // INNER
    h = plan.height
    PAD = 16
    first, last = 0, plan.devices - 1

    def body(kappa, above, below, part, beside, *refs):
        count = plan.cross + 1 if keep else 1
        sums, me, outs, (h0, h1, kx, kept) = refs[: -5 - count], refs[-5 - count], refs[-4 - count : -4], refs[-4:]
        place = me[0] * plan.cross + me[1]
        zeros = jnp.zeros((PAD, plan.cols), F32)
        for ref in (h0, kx, h1):
            ref[0:PAD, :] = zeros
            ref[h + PAD : h + 2 * PAD, :] = zeros
        kx[PAD - 8 : PAD, :] = above[...]
        kx[PAD : PAD + h, :] = kappa[...]
        kx[PAD + h : PAD + h + 8, :] = below[...]
        upstream = jnp.zeros((blocks, INNER), F32)
        if len(sums) == 1:
            for d in range(plan.devices):
                upstream = upstream + jnp.where(d < place, sums[0][d], 0.0)
        else:
            for s in range(1, plan.cross):
                upstream = upstream + jnp.where(s <= me[1], sums[s - 1][...], 0.0)
            for t in range(1, plan.wind):
                upstream = upstream + jnp.where(t <= me[0], sums[plan.cross + t - 2][...], 0.0)
        has_next = jnp.where(place < last, 1.0, 0.0)
        for b in range(blocks):
            lanes = slice(b * INNER, (b + 1) * INNER)
            base = upstream[b : b + 1, :]
            h0[PAD : PAD + h, lanes] = part[:, lanes] + base
            h0[PAD - 1 : PAD, lanes] = base
            h0[PAD - 2 : PAD - 1, lanes] = base - beside[1:2, lanes]
            value = base + part[h - 1 : h, lanes] + beside[2:3, lanes]
            h0[PAD + h : PAD + h + 1, lanes] = value * has_next
            h0[PAD + h + 1 : PAD + h + 2, lanes] = (value + beside[3:4, lanes]) * has_next
        lane = lax.broadcasted_iota(jnp.int32, (8, plan.cols), 1)
        row = lax.broadcasted_iota(jnp.int32, (8, plan.cols), 0)

        def sides(x):
            left = jnp.where(lane == 0, 0.0, pltpu.roll(x, 1, 1))
            right = jnp.where(lane == plan.cols - 1, 0.0, pltpu.roll(x, plan.cols - 1, 1))
            return left, right

        def smooth(src, dst, low, count, masked):
            def step(i, carry):
                base = pl.multiple_of(low + i * 8, 8)
                value = src[pl.ds(base - 8, 24), :]
                kap = kx[pl.ds(base - 8, 24), :]
                mid, k_mid = value[8:16], kap[8:16]
                left, right = sides(mid)
                k_left, k_right = sides(k_mid)
                new = conducted(
                    mid, value[7:15], value[9:17], left, right, k_mid, kap[7:15], kap[9:17], k_left, k_right
                )
                if masked:
                    n = row + base
                    bad = ((n < PAD) & (place == first)) | ((n >= PAD + h) & (place == last))
                    new = jnp.where(bad, 0.0, new)
                if masked:
                    dst[pl.ds(base, 8), :] = new
                else:
                    at = pl.ds(base - PAD, 8)
                    if not keep:
                        outs[0][at, :] = -new
                        return carry
                    for b in range(blocks):
                        outs[0][plan.slot(b), at, :] = -new[:, b * INNER : (b + 1) * INNER]
                    kept[pl.ds(base - PAD, 8), :] = -new
                return carry

            lax.fori_loop(0, count, step, 0)

        refs = [h0, h1]
        for n in range(SMOOTH):
            if n < SMOOTH - 1:
                smooth(refs[n % 2], refs[(n + 1) % 2], PAD - 8, (h + 16) // 8, True)
            else:
                smooth(refs[n % 2], refs[(n + 1) % 2], PAD, h // 8, False)
        if keep:
            for s, out in enumerate(outs[1:]):
                c = lax.rem(me[1] + s, plan.cross)
                lanes = pl.ds(pl.multiple_of(c * plan.cols_here, plan.cols_here), plan.cols_here)
                out[...] = kept[:, lanes]

    tall = pltpu.VMEM((h + 2 * PAD, plan.cols), F32)
    flat = (h, plan.cols)
    if keep:
        outs = [jax.ShapeDtypeStruct((plan.devices, h, plan.width), F32)]
        outs += [jax.ShapeDtypeStruct((h, plan.cols_here), F32)] * plan.cross
    else:
        outs = [jax.ShapeDtypeStruct(flat, F32)]
    return call(body, outs, [tall] * 3 + [pltpu.VMEM(flat, F32)], (), () if keep else (0,), (), range(len(outs)) if keep else ())(
        kappa, above, below, part, beside, *rest
    )


def rows_heat(plan, matrices, table, received, alpha, side_table, side_alpha):
    width = plan.width
    outer = plan.rows // INNER
    per = INNER // plan.height
    two_rows = lambda a, b: lax.dot_general(a, b, (((1,), (1,)), ((), ())), preferred_element_type=F32)

    def sides(matrices, received, side_table, side_alpha, from_left, from_right):
        h = plan.height
        lane = lax.broadcasted_iota(jnp.int32, (8, INNER), 1)
        row = lambda part: side_table[part : part + 1, :]
        points = []
        for a in range(outer):
            re = jnp.zeros((8, INNER), F32)
            im = re
            for j in range(per):
                part = received[a * per + j, 2 * h : 2 * h + 8, :]
                here = (lane >= j * h) & (lane < (j + 1) * h)
                re = jnp.where(here, pltpu.roll(part, j * h, 1) if j else part, re)
                im = jnp.where(here, pltpu.roll(part, (j * h + INNER - h) % INNER, 1), im)
            points.append((re, im))
        values = []
        for k, value in enumerate(small_fft(points, -1)):
            if k:
                value = times(value, (row(k), row(outer + k)))
            high, low = split(jnp.concatenate(value, axis=1))
            both = two_rows(jnp.concatenate([high, low], axis=0), matrices[k, 0])
            value = both[0:8] + both[8:16] + two_rows(jnp.concatenate([high, high], axis=0), matrices[k, 1])[0:8]
            value = (value[:, :INNER], value[:, INNER:])
            if k:
                value = times(value, (row(k), -row(outer + k)))
            values.append(value)
        deposits = [side_alpha[...] * (re * re + im * im) for re, im in small_fft(values, 1)]
        high, low = split(jnp.concatenate(deposits, axis=0))
        ones = lower_ones(INNER)
        sums = two_rows(high, ones) + two_rows(low, ones)
        carry = jnp.zeros((8, 1), F32)
        none = jnp.zeros((6, INNER), F32)
        for a in range(outer):
            part = sums[8 * a : 8 * a + 8] + carry
            carry = part[:, INNER - 1 : INNER]
            n = slice(a * INNER, (a + 1) * INNER)
            from_left[:, n] = jnp.concatenate([none, part[0:2]], axis=0)
            from_right[:, n] = jnp.concatenate([part[2:4], none], axis=0)

    def body(matrices, table, received, alpha, side_table, side_alpha, heat, from_left, from_right, xh, z, dep):
        def write(a, off, value):
            deposit = alpha[...] * (value[0] * value[0] + value[1] * value[1])
            rows = pl.ds(a * INNER + off, CHUNK)
            dep[rows, 0:width], dep[rows, width : 2 * width] = split(deposit)

        sides(matrices, received, side_table, side_alpha, from_left, from_right)
        along_rows(functools.partial(plan.flip_a, received), write, matrices, table, xh, z)
        tile = 2 * INNER
        ones = lower_ones(tile)
        carry = jnp.zeros((1, width), F32)
        for g in range(plan.rows // tile):
            both = jnp.dot(ones, dep[g * tile : (g + 1) * tile, :], preferred_element_type=F32)
            value = both[:, :width] + both[:, width:] + carry
            heat[g * tile : (g + 1) * tile, :] = value
            carry = value[tile - 1 : tile, :]

    edge = jax.ShapeDtypeStruct((8, plan.rows), F32)
    outs = [jax.ShapeDtypeStruct((plan.rows, width), F32), edge, edge]
    scratch = plan.work_a() + [pltpu.VMEM((plan.rows, 2 * width), BF16)]
    return call(body, outs, scratch, (0, 1, 2), ())(matrices, table, received, alpha, side_table, side_alpha)


def rows_turn(plan, read_field, wide, dft, table, screen, field):
    def body(dft, table, screen, field, out, *work):
        def read(a, off):
            return screened(read_field(field, a, off), screen[pl.ds(a * INNER + off, CHUNK), :])

        along_rows(read, functools.partial(plan.send_a, out), dft, table, *work)
        if wide:
            plan.send_edges(out)

    out = plan.sent_wide if wide else plan.sent
    return call(body, [out], plan.work_a(), (0, 1, 2), (0,))(dft, table, screen, field)[0]


def rows_smooth(plan, heat, from_left, from_right, kappa, kappa_left, kappa_right, me, *ahead):
    width = plan.width
    PAD = 8
    step_rows = 32

    def body(heat, from_left, from_right, kappa, kappa_left, kappa_right, me, *refs):
        screen, h0, h1, kx = refs[-4:]

        place = me[1] * plan.wind + plan.local(me[0], me[1])
        zeros = jnp.zeros((PAD, 2 * width), F32)
        for ref in (h0, h1, kx):
            ref[0:PAD, :] = zeros
            ref[plan.rows + PAD : plan.rows + 2 * PAD, :] = zeros
        for g in range(plan.rows // INNER):
            n = slice(g * INNER, (g + 1) * INNER)
            spot = slice(PAD + g * INNER, PAD + (g + 1) * INNER)
            for ref, value, left, right in ((h0, heat, from_left, from_right), (kx, kappa, kappa_left, kappa_right)):
                ref[spot, 0:width] = value[n, :]
                beside = [right[:, n], jnp.zeros((width - 16, INNER), F32), left[:, n]]
                ref[spot, width : 2 * width] = jnp.concatenate(beside, axis=0).T
        wide = lax.broadcasted_iota(jnp.int32, (step_rows, 2 * width), 1)
        bad = (wide >= width) & (wide < width + width // 2) & (place == plan.devices - 1)
        bad = bad | ((wide >= width + width // 2) & (place == 0))

        def smooth(src, dst):
            def one(base):
                value = src[pl.ds(base, step_rows + 16), :]
                kap = kx[pl.ds(base, step_rows + 16), :]
                mid, k_mid = value[8:-8], kap[8:-8]
                new = conducted(
                    mid, value[7:-9], value[9:-7], pltpu.roll(mid, 1, 1), pltpu.roll(mid, 2 * width - 1, 1),
                    k_mid, kap[7:-9], kap[9:-7], pltpu.roll(k_mid, 1, 1), pltpu.roll(k_mid, 2 * width - 1, 1),
                )
                dst(base, jnp.where(bad, 0.0, new))

            def step(i, carry):
                for n in range(4):
                    one(pl.multiple_of((4 * i + n) * step_rows, step_rows))
                return carry

            lax.fori_loop(0, plan.rows // (4 * step_rows), step, 0)

        def into(ref):
            def put(base, value):
                ref[pl.ds(base + PAD, step_rows), :] = value

            return put

        def into_screen(base, value):
            screen[pl.ds(base, step_rows), :] = -value[:, :width]

        refs = [h0, h1]
        for n in range(SMOOTH):
            smooth(refs[n % 2], into(refs[(n + 1) % 2]) if n < SMOOTH - 1 else into_screen)

    tall = pltpu.VMEM((plan.rows + 2 * PAD, 2 * width), F32)
    outs = [jax.ShapeDtypeStruct((plan.rows, width), F32)]
    return call(body, outs, [tall] * 3, range(7, 7 + len(ahead)), (0,))(
        heat, from_left, from_right, kappa, kappa_left, kappa_right, me, *ahead
    )[0]


def next_prev(value_up, value_down, axes, order):
    up = list(zip(order[:-1], order[1:]))
    down = [(j, i) for i, j in up]
    return lax.ppermute(value_up, axes, up), lax.ppermute(value_down, axes, down)


def extended(shard, sides, width):
    for axis, dim in sides:
        size, length = (lax.axis_size(axis), shard.shape[dim])
        up = [(i, (i + 1) % size) for i in range(size - 1)]
        down = [(j, i) for i, j in up]
        last = lax.slice_in_dim(shard, length - width, length, axis=dim)
        initial = lax.slice_in_dim(shard, 0, width, axis=dim)
        before = lax.ppermute(last, axis, up)
        after = lax.ppermute(initial, axis, down)
        shard = jnp.concatenate([before, shard, after], axis=dim)
    return shard


def carried_in(part, axis, combine, identity):
    place = lax.axis_index(axis)
    gathered = lax.all_gather(part, axis)
    state = jnp.zeros_like(part) + jnp.asarray(identity, part.dtype)

    def one(turn, state):
        return combine(state, lax.dynamic_index_in_dim(gathered, turn, 0, False))

    return lax.fori_loop(0, place, one, state)


def signed_freq(indices, length):
    shifted = jnp.where(indices < length // 2, indices, indices - length)
    return shifted.astype(jnp.float32) / length


def trig_table(first_ids, second_ids, length, sign_value):
    product = first_ids * second_ids % length
    phase_angle = product.astype(jnp.float32) * (sign_value * 2.0 * math.pi / length)
    return (jnp.cos(phase_angle), jnp.sin(phase_angle))


def complex_product(formula, real_part, imag_part, cosine, sine):
    highest = lax.Precision.HIGHEST
    out_real = jnp.einsum(formula, real_part, cosine, precision=highest) - jnp.einsum(
        formula, imag_part, sine, precision=highest
    )
    out_imag = jnp.einsum(formula, real_part, sine, precision=highest) + jnp.einsum(
        formula, imag_part, cosine, precision=highest
    )
    return (out_real, out_imag)


def transform(stacked, axis_dim, inverse):
    full_shape = stacked.shape
    length = full_shape[axis_dim]
    inner_len = math.gcd(length, 128)
    outer_len = length // inner_len
    leading = full_shape[1] if axis_dim == 2 else 1
    trailing = full_shape[2] if axis_dim == 1 else 1
    blocks = stacked.reshape(2, leading, outer_len, inner_len, trailing)
    sign_value = 1.0 if inverse else -1.0
    outer_ids = jnp.arange(outer_len, dtype=jnp.int32)
    inner_ids = jnp.arange(inner_len, dtype=jnp.int32)
    cos_outer, sin_outer = trig_table(outer_ids[:, None], outer_ids[None, :], outer_len, sign_value)
    first_real, first_imag = complex_product(
        "pabq,ak->pkbq", blocks[0], blocks[1], cos_outer, sin_outer
    )
    cos_twist, sin_twist = trig_table(outer_ids[:, None], inner_ids[None, :], length, sign_value)
    cos_twist = cos_twist[None, :, :, None]
    sin_twist = sin_twist[None, :, :, None]
    twist_real = first_real * cos_twist - first_imag * sin_twist
    twist_imag = first_real * sin_twist + first_imag * cos_twist
    cos_inner, sin_inner = trig_table(inner_ids[:, None], inner_ids[None, :], inner_len, sign_value)
    second_real, second_imag = complex_product(
        "pkbq,bm->pkmq", twist_real, twist_imag, cos_inner, sin_inner
    )
    result = jnp.stack([second_real, second_imag]).transpose(0, 1, 3, 2, 4).reshape(full_shape)
    if inverse:
        result = result * (1.0 / length)
    return result


def apply_phase(stacked, phase_angle):
    cosine = jnp.cos(phase_angle)
    sine = jnp.sin(phase_angle)
    return jnp.stack(
        [stacked[0] * cosine - stacked[1] * sine, stacked[0] * sine + stacked[1] * cosine]
    )


def along_joint(stacked, phase_rate, row_freq, col_freq):
    cross_count = lax.axis_size("cross")
    stacked = lax.all_to_all(stacked, ("wind", "cross"), split_axis=2, concat_axis=1, tiled=True)
    stacked = transform(stacked, 1, False)
    col_width = stacked.shape[2]
    joint_block = lax.axis_index("wind") * cross_count + lax.axis_index("cross")
    cols_held = lax.dynamic_slice_in_dim(col_freq, joint_block * col_width, col_width)
    phase_angle = -phase_rate * (
        row_freq[:, None] * row_freq[:, None] + cols_held[None, :] * cols_held[None, :]
    )
    stacked = apply_phase(stacked, phase_angle)
    stacked = transform(stacked, 1, True)
    return lax.all_to_all(stacked, ("wind", "cross"), split_axis=1, concat_axis=2, tiled=True)


def propagate_slab(slab_pair, share_step):
    rows_total = slab_pair.shape[1] * lax.axis_size("wind") * lax.axis_size("cross")
    cols_total = slab_pair.shape[2]
    phase_rate = share_step * diffraction
    row_freq = signed_freq(jnp.arange(rows_total, dtype=jnp.int32), rows_total)
    col_freq = signed_freq(jnp.arange(cols_total, dtype=jnp.int32), cols_total)
    stacked = transform(slab_pair, 2, False)
    stacked = along_joint(stacked, phase_rate, row_freq, col_freq)
    return transform(stacked, 2, True)


def conduct_core(padded, kappa_pad):
    height = padded.shape[0] - 2
    breadth = padded.shape[1] - 2
    center = padded[1:-1, 1:-1]
    kappa_mid = kappa_pad[1:-1, 1:-1]
    flux_sum = jnp.zeros_like(center)
    for offset_row, offset_col in ((0, 1), (2, 1), (1, 0), (1, 2)):
        neighbour = padded[offset_row : offset_row + height, offset_col : offset_col + breadth]
        kappa_side = kappa_pad[offset_row : offset_row + height, offset_col : offset_col + breadth]
        flux_sum = flux_sum + 0.5 * (kappa_mid + kappa_side) * (neighbour - center)
    return center + conduct_rate * flux_sum


def add_terms(earlier, later_term):
    return earlier + later_term


def layer_absorption(index_row, table_row, level_ids):
    one_hot = (index_row[:, None] == level_ids[None, :]).astype(jnp.float32)
    return jnp.sum(one_hot * table_row[None, :], axis=1)


def wide_device(field_real, field_imag, absorb_index, absorb_table, zone_map, zone_conductivity):
    rows_here, cols_here = field_real.shape
    conductivity = jnp.zeros((rows_here, cols_here), jnp.float32)
    for zone_no in range(zone_conductivity.shape[0]):
        conductivity = jnp.where(zone_map == zone_no, zone_conductivity[zone_no], conductivity)
    level_ids = jnp.arange(absorb_table.shape[1], dtype=jnp.int32)
    combined = lax.all_to_all(
        jnp.stack([field_real, field_imag, conductivity]),
        "cross",
        split_axis=1,
        concat_axis=2,
        tiled=True,
    )
    slab_pair = combined[:2]
    kappa_rows = extended(combined[2], ((("wind", "cross"), 0),), 1)
    kappa_pad = jnp.pad(kappa_rows, ((0, 0), (1, 1)))
    index_full = lax.all_gather(absorb_index, "cross", axis=1, tiled=True)
    slab_rows = slab_pair.shape[1]
    rows_total = slab_rows * lax.axis_size("wind") * lax.axis_size("cross")
    slab_ids = jnp.arange(slab_rows, dtype=jnp.int32)
    lower_slab = (slab_ids[:, None] >= slab_ids[None, :]).astype(jnp.float32)
    screen_phase = jnp.zeros((slab_rows, slab_pair.shape[2]), jnp.float32)
    for layer_no in range(LAYERS):
        absorption = layer_absorption(index_full[layer_no], absorb_table[layer_no], level_ids)
        screen_phase = jnp.zeros((slab_rows, slab_pair.shape[2]), jnp.float32)
        for _ in range(ITERS):
            middle = propagate_slab(apply_phase(slab_pair, screen_phase), 0.5)
            intensity = middle[0] * middle[0] + middle[1] * middle[1]
            deposit = absorption[None, :] * intensity * (1.0 / rows_total)
            partial_heat = jnp.dot(lower_slab, deposit, precision=lax.Precision.HIGHEST)
            totals = partial_heat[-1]
            upstream = carried_in(totals, ("wind", "cross"), add_terms, jnp.zeros_like(totals))
            heat_field = partial_heat + upstream[None, :]
            for _ in range(SMOOTH):
                padded = extended(heat_field, ((("wind", "cross"), 0),), 1)
                padded = jnp.pad(padded, ((0, 0), (1, 1)))
                heat_field = conduct_core(padded, kappa_pad)
            screen_phase = -heat_field
        slab_pair = propagate_slab(apply_phase(slab_pair, screen_phase), 1.0)
    returned = lax.all_to_all(
        jnp.stack([slab_pair[0], slab_pair[1], screen_phase]),
        "cross",
        split_axis=2,
        concat_axis=1,
        tiled=True,
    )
    return (returned[0], returned[1], returned[2])


def on_device(field_real, field_imag, absorb_index, absorb_table, zone_map, zone_conductivity):
    plan = Plan(*field_real.shape, lax.axis_size("wind"), lax.axis_size("cross"))
    fits = plan.width == INNER and INNER % plan.height == 0 and plan.height % CHUNK == 0
    if not fits or plan.rows_here % INNER or plan.rows % (2 * INNER):
        return wide_device(field_real, field_imag, absorb_index, absorb_table, zone_map, zone_conductivity)
    return tiled_device(plan, field_real, field_imag, absorb_index, absorb_table, zone_map, zone_conductivity)


def tiled_device(plan, field_real, field_imag, absorb_index, absorb_table, zone_map, zone_conductivity):
    cross = plan.cross
    w, c = lax.axis_index("wind"), lax.axis_index("cross")
    place = jnp.stack([w, c]).astype(jnp.int32)
    grid_axes = ("wind", "cross")

    def exchange(x, axes):
        return lax.all_to_all(x, axes, split_axis=0, concat_axis=0, tiled=True)

    def flip(x):
        return exchange(x, grid_axes)

    to_b, *field_blocks = prepare_field(plan, field_real, field_imag, place)
    home_b = exchange(to_b, "cross")
    field_blocks = shifted(field_blocks, "wind")
    *across, kappa, left, right, alpha_a, alpha = prepare(
        plan, zone_map, absorb_index, absorb_table, zone_conductivity, place
    )
    side_alpha, *along = home_kappa(plan, kappa, *next_prev(right, left, "cross", list(range(cross))), alpha, place)

    dft = jnp.asarray(dft_matrices())
    tab_a = lambda share: (jnp.asarray(row_blocks(plan.rows, share)), jnp.asarray(row_table(plan.rows)))
    tab_b_of = lambda length: jnp.asarray(chirp_columns(length, ()))
    tab_b = lambda *shares: jnp.asarray(chirp_columns(plan.cols, shares))

    def smooth_a(layer, share, received, *ahead):
        heat, from_left, from_right = rows_heat(
            plan, *tab_a(share), received, alpha_a[layer : layer + 1], tab_b_of(plan.rows), side_alpha[layer]
        )
        return rows_smooth(plan, heat, from_left, from_right, *kappas, place, *ahead)

    def smooth_b(layer, keep, received):
        part, beside, totals = cols_heat(plan, layer, plan.devices, dft, tab_b(0.5), received, alpha_b)
        return cols_smooth(plan, keep, kappa_b, above, below, part, beside, flip(totals), place)

    home_b, across = lax.optimization_barrier((home_b, across))
    sent = cols_send(plan, plan.home_b, False, dft, tab_b(0.5), home_b, True)
    kappa_b, alpha_b = home_rows(plan, shifted(across, "cross"), place)
    above, below = next_prev(kappa_b[-8:], kappa_b[:8], grid_axes, list(range(plan.devices)))
    received, along = lax.optimization_barrier((flip(sent), along))
    along = shifted(along, "wind")
    kappas = rows_kappa(plan, along, place)
    home_a = in_order(field_blocks, place, 0)
    screen = smooth_a(0, 0.5, received)
    sent = rows_turn(plan, plan.home_a, True, *tab_a(0.5), screen, home_a)
    received, above, below = lax.optimization_barrier((flip(sent), above, below))
    (screen,) = smooth_b(0, False, received)
    sent_middle, sent_field = cols_turn(plan, plan.home_b, 2, dft, tab_b(1.5, 1.0), screen, home_b)
    middle = flip(sent_middle)
    field = flip(sent_field)
    whole_share = tab_a(1.0)
    screen = smooth_a(1, 1.5, middle, whole_share[0])
    field, screen = lax.optimization_barrier((field, screen))
    field = rows_field(plan, plan.flip_a, *whole_share, field)
    sent = rows_turn(plan, plan.flip_a, True, *tab_a(0.5), screen, field)
    screen, *home_parts = smooth_b(1, True, flip(sent))
    home_parts = shifted(home_parts, "cross")
    screen = flip(screen).reshape(plan.rows, plan.width)
    sent = rows_turn(plan, plan.flip_a, False, *whole_share, screen, field)
    back = cols_send(plan, plan.flip_b, True, dft, tab_b(1.0), flip(sent))
    screen = home_screen(plan, home_parts, place)
    back = exchange(back, "cross")
    out_real = back[:, : plan.height].reshape(field_real.shape)
    out_imag = back[:, plan.height :].reshape(field_real.shape)
    return (out_real, out_imag, screen)


def solution(mesh):
    in_specs = (
        P(("beams", "wind"), "cross"),
        P(("beams", "wind"), "cross"),
        P(None, "cross"),
        P(),
        P("wind", "cross"),
        P(),
    )
    out_specs = (
        P(("beams", "wind"), "cross"),
        P(("beams", "wind"), "cross"),
        P(("beams", "wind"), "cross"),
    )
    return jax.shard_map(on_device, mesh=mesh, in_specs=in_specs, out_specs=out_specs, check_vma=False)
```

```python
import functools
import math

import jax
import jax.numpy as jnp
import numpy as np
from jax import lax
from jax.experimental import pallas as pl
from jax.experimental.pallas import tpu as pltpu
from jax.sharding import PartitionSpec as P


LAYERS = 2
ITERS = 2
SMOOTH = 2
INNER = 128
CHUNK = 16

diffraction = 2000.0
conduct_rate = 0.24

F32 = jnp.float32
BF16 = jnp.bfloat16
WHOLE = pl.BlockSpec(memory_space=pltpu.VMEM)
SCALAR = pl.BlockSpec(memory_space=pltpu.SMEM)


def split_np(values):
    high = values.astype(np.float32).astype(jnp.bfloat16)
    low = (values - high.astype(np.float64)).astype(np.float32).astype(jnp.bfloat16)
    return high, low


def dft_matrices():
    ids = np.arange(INNER)
    angle = 2.0 * np.pi * (np.outer(ids, ids) % INNER) / INNER
    cosine, sine = np.cos(angle), np.sin(angle)
    left = np.block([[cosine, sine], [-sine, cosine]])
    return np.stack([*split_np(left), *split_np(left.T)])


def chirp_columns(length, shares):
    outer = length // INNER
    k = np.arange(outer)[:, None]
    m = np.arange(INNER)[None, :]
    twist = -2.0 * np.pi * ((k * m) % length) / length
    tables = [np.cos(twist), np.sin(twist)]
    p = k + outer * m
    freq = np.where(p < length // 2, p, p - length) / length
    for share in shares:
        angle = -share * diffraction * freq * freq
        tables += [np.cos(angle) / length, np.sin(angle) / length]
    return np.concatenate(tables, axis=0).astype(np.float32)


def row_table(length):
    cols = chirp_columns(length, ()).T
    return np.pad(cols, ((0, 0), (0, -cols.shape[1] % 128)))


def row_blocks(length, share):
    outer = length // INNER
    ids = np.arange(INNER)
    forward = np.exp(-2j * np.pi * (np.outer(ids, ids) % INNER) / INNER)
    blocks = []
    for k in range(outer):
        p = k + outer * ids
        freq = np.where(p < length // 2, p, p - length) / length
        block = forward.conj() @ (np.exp(-1j * share * diffraction * freq * freq)[:, None] / length * forward)
        blocks.append(np.stack(split_np(np.block([[block.real, -block.imag], [block.imag, block.real]]))))
    return np.stack(blocks)


def split(x):
    high = x.astype(BF16)
    return high, (x - high.astype(F32)).astype(BF16)


def times(a, b):
    return (a[0] * b[0] - a[1] * b[1], a[0] * b[1] + a[1] * b[0])


def small_fft(points, sign):
    count = len(points)
    if count == 1:
        return points
    even = small_fft(points[0::2], sign)
    odd = small_fft(points[1::2], sign)
    half = count // 2
    out = [None] * count
    for k in range(half):
        re, im = odd[k]
        if k == 0:
            turn = (re, im)
        elif 4 * k == count:
            turn = (-im, re) if sign > 0 else (im, -re)
        elif 8 * k == count:
            root = math.sqrt(0.5)
            turn = (root * (re - im), root * (im + re)) if sign > 0 else (root * (re + im), root * (im - re))
        elif 8 * k == 3 * count:
            root = math.sqrt(0.5)
            turn = (-root * (re + im), root * (re - im)) if sign > 0 else (root * (im - re), -root * (re + im))
        else:
            c = math.cos(2.0 * math.pi * k / count)
            s = sign * math.sin(2.0 * math.pi * k / count)
            turn = (c * re - s * im, s * re + c * im)
        out[k] = (even[k][0] + turn[0], even[k][1] + turn[1])
        out[k + half] = (even[k][0] - turn[0], even[k][1] - turn[1])
    return out


def cos_sin(x):
    turns = jnp.floor(x * (2.0 / math.pi) + 0.5)
    r = ((x - turns * 1.5703125) - turns * 4.837512969970703125e-4) - turns * 7.549789954891882e-8
    quad = turns.astype(jnp.int32)
    z = r * r
    s = r + r * z * (-1.6666654611e-1 + z * (8.3321608736e-3 - z * 1.9515295891e-4))
    c = 1.0 - 0.5 * z + z * z * (4.166664568298827e-2 + z * (-1.388731625493765e-3 + z * 2.443315711809948e-5))
    odd = (quad & 1) == 1
    sin_x = jnp.where(odd, c, s)
    cos_x = jnp.where(odd, s, c)
    sin_x = jnp.where((quad & 2) == 2, -sin_x, sin_x)
    cos_x = jnp.where(((quad + 1) & 2) == 2, -cos_x, cos_x)
    return cos_x, sin_x


def screened(value, screen):
    return times(value, cos_sin(screen))


def triple(a_high, a_low, b_high, b_low):
    dot = functools.partial(jnp.dot, preferred_element_type=F32)
    return dot(a_high, b_high) + dot(a_high, b_low) + dot(a_low, b_high)


def lower_ones(size):
    r = lax.broadcasted_iota(jnp.int32, (size, size), 0)
    c = lax.broadcasted_iota(jnp.int32, (size, size), 1)
    return jnp.where(r >= c, 1.0, 0.0).astype(BF16)


def chunks(count, body):
    def step(i, carry):
        for n in range(side):
            body(pl.multiple_of((side * i + n) * CHUNK, CHUNK))
        return carry

    side = 2 if count % (2 * CHUNK) == 0 else 1
    lax.fori_loop(0, count // (side * CHUNK), step, 0)


def along_rows(read, write, matrices, table, xh, z):
    outer = matrices.shape[0]
    width = z.shape[1] // outer
    lanes = lambda k: pl.ds(k * width, width)
    col = lambda part, off: table[pl.ds(off, CHUNK), part : part + 1]

    def first(off):
        for k, value in enumerate(small_fft([read(a, off) for a in range(outer)], -1)):
            if k:
                value = times(value, (col(k, off), col(outer + k, off)))
            for at, v in ((0, value[0]), (INNER, value[1])):
                high, low = split(v)
                xh[pl.ds(at + off, CHUNK), pl.ds(2 * k * width, width)] = high
                xh[pl.ds(at + off, CHUNK), pl.ds((2 * k + 1) * width, width)] = low

    def last(off):
        values = []
        for k in range(outer):
            value = (z[pl.ds(off, CHUNK), lanes(k)], z[pl.ds(INNER + off, CHUNK), lanes(k)])
            if k:
                value = times(value, (col(k, off), -col(outer + k, off)))
            values.append(value)
        for a, value in enumerate(small_fft(values, 1)):
            write(a, off, value)

    chunks(INNER, first)
    dot = functools.partial(jnp.dot, preferred_element_type=F32)
    for k in range(outer):
        both = dot(matrices[k, 0], xh[:, 2 * k * width : (2 * k + 2) * width])
        low = dot(matrices[k, 1], xh[:, 2 * k * width : (2 * k + 1) * width])
        z[:, k * width : (k + 1) * width] = both[:, :width] + both[:, width:] + low
    chunks(INNER, last)


def along_cols(main, read, writes, dft, table, xh, xl, y, z):
    outer = table.shape[0] // (2 * (1 + len(writes)))
    height = xh.shape[0] // outer

    def every(body):
        chunks(main, body)
        if height > main:
            body(main)

    row = lambda part: table[part : part + 1, :]

    def put(k, off, value):
        for at, v in ((0, value[0]), (INNER, value[1])):
            spot = (pl.ds(k * height + off, CHUNK), pl.ds(at, INNER))
            xh[spot], xl[spot] = split(v)

    def get(ref, k, off):
        return tuple(ref[pl.ds(k * height + off, CHUNK), pl.ds(at, INNER)] for at in (0, INNER))

    def first(off):
        for k, value in enumerate(small_fft([read(b, off) for b in range(outer)], -1)):
            if k:
                value = times(value, (row(k), row(outer + k)))
            put(k, off, value)

    every(first)
    y[...] = triple(xh[...], xl[...], dft[2], dft[3])
    for n, write in enumerate(writes):

        def middle(off, n=n):
            for k in range(outer):
                base = (2 + 2 * n) * outer + k
                put(k, off, times(get(y, k, off), (row(base), row(base + outer))))

        every(middle)
        z[...] = triple(xh[...], xl[...], dft[0], dft[1])

        def last(off, write=write):
            values = []
            for k in range(outer):
                value = get(z, k, off)
                if k:
                    value = times(value, (row(k), -row(outer + k)))
                values.append(value)
            for b, value in enumerate(small_fft(values, 1)):
                write(b, off, value)

        every(last)


class Plan:
    def __init__(self, rows_here, cols_here, wind, cross):
        self.wind, self.cross = wind, cross
        self.devices = wind * cross
        self.rows_here, self.cols_here = rows_here, cols_here
        self.height = rows_here // cross
        self.width = cols_here // wind
        self.rows, self.cols = rows_here * wind, cols_here * cross

    def local(self, w, c):
        return w + (c % 2) * (self.wind - 1 - 2 * w)

    def slot(self, block):
        c, i = block // self.wind, block % self.wind
        return self.local(i, c) * self.cross + c

    def home_a(self, ref, a, off):
        n = a * INNER
        src, at = n // self.rows_here, n % self.rows_here
        return tuple(ref[src, pl.ds(p * self.rows_here + at + off, CHUNK), :] for p in (0, 1))

    def spot_a(self, a, off):
        per = INNER // self.height
        return a * per + off // self.height, lax.rem(off, self.height)

    def flip_a(self, ref, a, off):
        s, at = self.spot_a(a, off)
        at = pl.multiple_of(at, CHUNK)
        return tuple(ref[s, pl.ds(p * self.height + at, CHUNK), :] for p in (0, 1))

    def send_a(self, ref, a, off, value):
        s, at = self.spot_a(a, off)
        at = pl.multiple_of(at, CHUNK)
        for p in (0, 1):
            ref[s, pl.ds(p * self.height + at, CHUNK), :] = value[p]

    def send_edges(self, ref):
        h = self.height
        for d in range(self.devices):
            for p in (0, 1):
                at = 2 * h + 4 * p
                before = ref[d - 1, p * h + h - 2 : p * h + h, :] if d else jnp.zeros((2, self.width), F32)
                after = ref[d + 1, p * h : p * h + 2, :] if d + 1 < self.devices else jnp.zeros((2, self.width), F32)
                ref[d, at : at + 2, :] = before
                ref[d, at + 2 : at + 4, :] = after

    def edges(self, value, left, right, at):
        turned = value.T
        left[:, at : at + INNER] = turned[0:8, :]
        right[:, at : at + INNER] = turned[self.width - 8 : self.width, :]

    def send_sides(self, ref):
        h, w = self.height, self.width
        last = self.devices - 1
        for b in range(self.devices):
            turned = ref[self.slot(b), 0 : 2 * h, :].T
            if b < last:
                ref[self.slot(b + 1), 2 * h : 2 * h + 2, :] = turned[w - 2 : w, :]
            if b:
                ref[self.slot(b - 1), 2 * h + 2 : 2 * h + 4, :] = turned[0:2, :]
        none = jnp.zeros((2, w), F32)
        ref[self.slot(0), 2 * h : 2 * h + 2, :] = none
        ref[self.slot(last), 2 * h + 2 : 2 * h + 4, :] = none

    def home_b(self, ref, b, off):
        per = self.cols_here // INNER
        return tuple(ref[b // per, pl.ds(p * self.height + off, CHUNK), pl.ds((b % per) * INNER, INNER)] for p in (0, 1))

    def wide_b(self, ref, b, off):
        if isinstance(off, int):
            extra = ref[self.slot(b), 2 * self.height : 2 * self.height + 8, :]
            turned = jnp.concatenate([extra[4:8], extra[0:4]], axis=0)
            return jnp.concatenate([extra, extra], axis=0), jnp.concatenate([turned, turned], axis=0)
        return self.flip_b(ref, b, off)

    def flip_b(self, ref, b, off):
        return tuple(ref[self.slot(b), pl.ds(p * self.height + off, CHUNK), :] for p in (0, 1))

    def send_b(self, ref, b, off, value):
        for p in (0, 1):
            ref[self.slot(b), pl.ds(p * self.height + off, CHUNK), :] = value[p]

    def back_b(self, ref, b, off, value):
        per = self.cols_here // INNER
        for p in (0, 1):
            ref[b // per, pl.ds(p * self.height + off, CHUNK), pl.ds((b % per) * INNER, INNER)] = value[p]

    @property
    def sent(self):
        return jax.ShapeDtypeStruct((self.devices, 2 * self.height, self.width), F32)

    def work_a(self):
        wide = (self.rows // INNER) * self.width
        return [
            pltpu.VMEM((2 * INNER, 2 * wide), BF16),
            pltpu.VMEM((2 * INNER, wide), F32),
        ]

    @property
    def sent_wide(self):
        return jax.ShapeDtypeStruct((self.devices, 2 * self.height + 8, self.width), F32)

    def work_b(self, extra=0):
        tall = (self.cols // INNER) * (self.height + extra)
        return [
            pltpu.VMEM((tall, 2 * INNER), BF16),
            pltpu.VMEM((tall, 2 * INNER), BF16),
            pltpu.VMEM((tall, 2 * INNER), F32),
            pltpu.VMEM((tall, 2 * INNER), F32),
        ]


def call(body, outs, scratch, near=(), near_outs=(), far=(), far_outs=()):
    def run(*args):
        specs = [SCALAR if a.size <= 16 else WHOLE for a in args]
        spaces = [pltpu.VMEM if i in near else pltpu.HBM if i in far else None for i in range(len(args))]
        args = [pltpu.with_memory_space_constraint(a, space) if space else a for a, space in zip(args, spaces)]
        return pl.pallas_call(
            body,
            out_shape=[
                pltpu.VMEM(o.shape, o.dtype) if i in near_outs else pltpu.HBM(o.shape, o.dtype) if i in far_outs else o
                for i, o in enumerate(outs)
            ],
            in_specs=specs,
            out_specs=[WHOLE] * len(outs),
            scratch_shapes=scratch,
            compiler_params=pltpu.CompilerParams(vmem_limit_bytes=14 * 1024 * 1024),
        )(*args)

    return run


def prepare_field(plan, field_real, field_imag, place):
    h = plan.height

    def body(real, imag, place, to_b, *to_a):
        for c in range(plan.cross):
            to_b[c, 0:h, :] = real[c * h : (c + 1) * h, :]
            to_b[c, h : 2 * h, :] = imag[c * h : (c + 1) * h, :]
        for t, out in enumerate(to_a):
            n = lax.rem(place[0] + t, plan.wind)
            lanes = pl.ds(pl.multiple_of(plan.local(n, place[1]) * plan.width, plan.width), plan.width)
            out[0 : plan.rows_here, :] = real[:, lanes]
            out[plan.rows_here : 2 * plan.rows_here, :] = imag[:, lanes]

    outs = [jax.ShapeDtypeStruct((plan.cross, 2 * h, plan.cols_here), F32)]
    outs += [jax.ShapeDtypeStruct((2 * plan.rows_here, plan.width), F32)] * plan.wind
    return call(body, outs, [], (), (), (0, 1))(field_real, field_imag, place)


def prepare(plan, zone_map, absorb_index, absorb_table, zone_conductivity, place):
    h = plan.height

    def picked(ids, count, level):
        value = jnp.zeros(ids.shape, F32)
        for n in range(count):
            value = jnp.where(ids == n, level(n), value)
        return value

    def body(zones, index, table, levels, place, *refs):
        to_b, (kappa, left, right, alpha_a, alpha) = refs[: plan.cross], refs[plan.cross :]
        w, c = place[0], place[1]

        def step(off):
            kappa[pl.ds(off, CHUNK), :] = picked(zones[pl.ds(off, CHUNK), :], levels.shape[0], lambda n: levels[n])

        chunks(plan.rows_here, step)
        alpha[...] = jnp.zeros_like(alpha)
        for layer in range(LAYERS):
            value = picked(index[layer : layer + 1, :], table.shape[1], lambda n: table[layer, n])
            alpha[layer : layer + 1, :] = value * (1.0 / plan.rows)
        alpha_a[...] = alpha[:, pl.ds(pl.multiple_of(plan.local(w, c) * plan.width, plan.width), plan.width)]
        for s, out in enumerate(to_b):
            out[0:h, :] = kappa[pl.ds(pl.multiple_of(lax.rem(c + s, plan.cross) * h, h), h), :]
            out[h:, :] = alpha[...]
        for at in range(0, plan.rows_here, INNER):
            left[0:8, at : at + INNER] = kappa[at : at + INNER, 0 : plan.width].T[0:8, :]
            right[0:8, at : at + INNER] = kappa[at : at + INNER, plan.cols_here - plan.width :].T[plan.width - 8 :, :]
        left[8:16, :] = jnp.zeros((8, plan.rows_here), F32)
        right[8:16, :] = jnp.zeros((8, plan.rows_here), F32)
        left[8:16, 0:INNER] = alpha[:, 0 : plan.width]
        right[8:16, 0:INNER] = alpha[:, plan.cols_here - plan.width :]

    edge = jax.ShapeDtypeStruct((16, plan.rows_here), F32)
    outs = [jax.ShapeDtypeStruct((h + 8, plan.cols_here), F32)] * plan.cross
    outs += [jax.ShapeDtypeStruct(zone_map.shape, F32), edge, edge, jax.ShapeDtypeStruct((8, plan.width), F32)]
    outs.append(jax.ShapeDtypeStruct((8, plan.cols_here), F32))
    return call(body, outs, [], (), (), (0,))(
        zone_map, absorb_index, absorb_table, zone_conductivity, place
    )


def home_kappa(plan, kappa, from_left, from_right, alpha, place):
    per = plan.rows_here // INNER

    def body(kappa, from_left, from_right, alpha, place, side_alpha, *refs):
        outs, edges = refs[: plan.wind], refs[-1]
        mine = plan.local(place[0], place[1])
        side_alpha[...] = jnp.zeros_like(side_alpha)
        for i in range(plan.wind):

            @pl.when(mine == i)
            def _():
                for layer in range(LAYERS):
                    line = slice(layer, layer + 1)
                    before = alpha[line, (i - 1) * plan.width : i * plan.width] if i else from_left[8 + layer : 9 + layer, 0:INNER]
                    last = i + 1 == plan.wind
                    after = from_right[8 + layer : 9 + layer, 0:INNER] if last else alpha[line, (i + 1) * plan.width : (i + 2) * plan.width]
                    for n, value in enumerate((before[:, -2:-1], before[:, -1:], after[:, 0:1], after[:, 1:2])):
                        side_alpha[layer, n : n + 1, :] = jnp.broadcast_to(value, (1, INNER))

        for at in range(per):
            n = slice(at * INNER, (at + 1) * INNER)
            edges[0, 8 * at : 8 * at + 8, :] = from_left[0:8, n]
            edges[plan.wind - 1, 8 * (per + at) : 8 * (per + at) + 8, :] = from_right[0:8, n]
            for i in range(plan.wind):
                turned = kappa[n, i * plan.width : (i + 1) * plan.width].T
                if i + 1 < plan.wind:
                    edges[i + 1, 8 * at : 8 * at + 8, :] = turned[plan.width - 8 :, :]
                if i:
                    edges[i - 1, 8 * (per + at) : 8 * (per + at) + 8, :] = turned[0:8, :]
        for t, out in enumerate(outs):
            i = plan.local(lax.rem(place[0] + t, plan.wind), place[1])
            out[0 : plan.rows_here, :] = kappa[:, pl.ds(pl.multiple_of(i * plan.width, plan.width), plan.width)]
            out[plan.rows_here :, :] = edges[i]

    outs = [jax.ShapeDtypeStruct((LAYERS, 8, INNER), F32)]
    outs += [jax.ShapeDtypeStruct((plan.rows_here + 16 * per, plan.width), F32)] * plan.wind
    scratch = [pltpu.VMEM((plan.wind, 16 * per, INNER), F32)]
    return call(body, outs, scratch)(
        kappa, from_left, from_right, alpha, place
    )


def home_rows(plan, parts, place):
    h = plan.height

    def body(*refs):
        place, kappa, alpha = refs[plan.cross :]
        for s, ref in enumerate(refs[: plan.cross]):
            c = lax.rem(place[1] + plan.cross - s, plan.cross)
            lanes = pl.ds(pl.multiple_of(c * plan.cols_here, plan.cols_here), plan.cols_here)
            kappa[:, lanes] = ref[0:h, :]
            alpha[:, lanes] = ref[h:, :]

    outs = [jax.ShapeDtypeStruct((h, plan.cols), F32), jax.ShapeDtypeStruct((8, plan.cols), F32)]
    return call(body, outs, [])(*parts, place)


def shifted(parts, axis):
    size = lax.axis_size(axis)
    return [parts[0]] + [lax.ppermute(parts[s], axis, [(i, (i + s) % size) for i in range(size)]) for s in range(1, size)]


def in_order(parts, place, which):
    size = len(parts)

    def body(*refs):
        place, out = refs[size], refs[-1]
        for s, ref in enumerate(refs[:size]):
            out[lax.rem(place[which] + size - s, size)] = ref[...]

    out = jax.ShapeDtypeStruct((size,) + parts[0].shape, F32)
    return call(body, [out], [], range(size))(*parts, place)[0]


def home_screen(plan, parts, place):
    h = plan.height

    def body(*refs):
        place, out = refs[plan.cross], refs[-1]
        for s, ref in enumerate(refs[: plan.cross]):
            c = lax.rem(place[1] + plan.cross - s, plan.cross)
            out[pl.ds(pl.multiple_of(c * h, h), h), :] = ref[...]

    out = jax.ShapeDtypeStruct((plan.rows_here, plan.cols_here), F32)
    return call(body, [out], [])(*parts, place)[0]


def rows_kappa(plan, parts, place):
    per = plan.rows_here // INNER

    def body(*refs):
        place, out, left, right = refs[plan.wind :]
        for t, ref in enumerate(refs[: plan.wind]):
            first = lax.rem(place[0] + plan.wind - t, plan.wind) * plan.rows_here
            out[pl.ds(pl.multiple_of(first, plan.rows_here), plan.rows_here), :] = ref[0 : plan.rows_here, :]
            for at in range(per):
                n = pl.ds(pl.multiple_of(first + at * INNER, INNER), INNER)
                line = plan.rows_here + 8 * at
                left[:, n] = ref[line : line + 8, :]
                right[:, n] = ref[line + 8 * per : line + 8 * per + 8, :]

    edge = jax.ShapeDtypeStruct((8, plan.rows), F32)
    outs = [jax.ShapeDtypeStruct((plan.rows, plan.width), F32), edge, edge]
    return call(body, outs, [], range(plan.wind))(*parts, place)


def rows_field(plan, read_field, dft, table, field):
    def body(dft, table, field, out, *work):
        along_rows(functools.partial(read_field, field), functools.partial(plan.send_a, out), dft, table, *work)

    return call(body, [plan.sent], plan.work_a(), (0, 1, 2), (0,))(dft, table, field)[0]


def cols_send(plan, read_field, back, dft, table, field, sides=False):
    out = plan.sent_wide if sides else plan.sent
    if back:
        out = jax.ShapeDtypeStruct((plan.cross, 2 * plan.height, plan.cols_here), F32)

    def body(dft, table, field, out, *work):
        put = plan.back_b if back else plan.send_b
        along_cols(plan.height, functools.partial(read_field, field), [functools.partial(put, out)], dft, table, *work)
        if sides:
            plan.send_sides(out)

    return call(body, [out], plan.work_b(), (0, 1, 2), () if back else (0,))(dft, table, field)[0]


def cols_heat(plan, layer, copies, dft, table, received, absorption):
    blocks = plan.cols // INNER
    h = plan.height

    def body(dft, table, received, absorption, part, beside, totals, xh, xl, y, z, dh, dl):
        def write(b, off, value):
            alpha = absorption[layer : layer + 1, pl.ds(b * INNER, INNER)]
            deposit = alpha * (value[0] * value[0] + value[1] * value[1])
            lanes = pl.ds(b * INNER, INNER)
            if isinstance(off, int):
                beside[:, lanes] = deposit[0:8]
                return
            spot = (pl.ds(off, CHUNK), lanes)
            dh[spot], dl[spot] = split(deposit)

        along_cols(h, functools.partial(plan.wide_b, received), [write], dft, table, xh, xl, y, z)
        ones = lower_ones(h)
        dot = functools.partial(jnp.dot, preferred_element_type=F32)
        part[...] = dot(ones, dh[...]) + dot(ones, dl[...])
        for b in range(blocks):
            total = part[h - 1 : h, b * INNER : (b + 1) * INNER]
            for d in range(copies):
                totals[d, b : b + 1, :] = total

    outs = [
        jax.ShapeDtypeStruct((h, plan.cols), F32),
        jax.ShapeDtypeStruct((8, plan.cols), F32),
        jax.ShapeDtypeStruct((copies, blocks, INNER), F32),
    ]
    scratch = plan.work_b(CHUNK) + [pltpu.VMEM((h, plan.cols), BF16), pltpu.VMEM((h, plan.cols), BF16)]
    return call(body, outs, scratch, (0, 1, 2), ())(dft, table, received, absorption)


def conducted(mid, up, down, left, right, k_mid, k_up, k_down, k_left, k_right):
    flux = (k_mid + k_up) * (up - mid) + (k_mid + k_down) * (down - mid)
    flux = flux + (k_mid + k_left) * (left - mid) + (k_mid + k_right) * (right - mid)
    return mid + (0.5 * conduct_rate) * flux


def cols_turn(plan, read_field, sets, dft, table, screen, field):
    def body(dft, table, screen, field, *refs):
        outs, work = refs[:sets], refs[sets:]

        def read(b, off):
            return screened(read_field(field, b, off), screen[pl.ds(off, CHUNK), pl.ds(b * INNER, INNER)])

        along_cols(plan.height, read, [functools.partial(plan.send_b, out) for out in outs], dft, table, *work)
        if sets > 1:
            plan.send_sides(outs[0])

    return call(body, [plan.sent_wide if sets > 1 and n == 0 else plan.sent for n in range(sets)], plan.work_b(), (0, 1, 2), range(sets))(
        dft, table, screen, field
    )


def cols_smooth(plan, keep, kappa, above, below, part, beside, *rest):
    blocks = plan.cols // INNER
    h = plan.height
    PAD = 16
    first, last = 0, plan.devices - 1

    def body(kappa, above, below, part, beside, *refs):
        count = plan.cross + 1 if keep else 1
        sums, me, outs, (h0, h1, kx, kept) = refs[: -5 - count], refs[-5 - count], refs[-4 - count : -4], refs[-4:]
        place = me[0] * plan.cross + me[1]
        zeros = jnp.zeros((PAD, plan.cols), F32)
        for ref in (h0, kx, h1):
            ref[0:PAD, :] = zeros
            ref[h + PAD : h + 2 * PAD, :] = zeros
        kx[PAD - 8 : PAD, :] = above[...]
        kx[PAD : PAD + h, :] = kappa[...]
        kx[PAD + h : PAD + h + 8, :] = below[...]
        upstream = jnp.zeros((blocks, INNER), F32)
        if len(sums) == 1:
            for d in range(plan.devices):
                upstream = upstream + jnp.where(d < place, sums[0][d], 0.0)
        else:
            for s in range(1, plan.cross):
                upstream = upstream + jnp.where(s <= me[1], sums[s - 1][...], 0.0)
            for t in range(1, plan.wind):
                upstream = upstream + jnp.where(t <= me[0], sums[plan.cross + t - 2][...], 0.0)
        has_next = jnp.where(place < last, 1.0, 0.0)
        for b in range(blocks):
            lanes = slice(b * INNER, (b + 1) * INNER)
            base = upstream[b : b + 1, :]
            h0[PAD : PAD + h, lanes] = part[:, lanes] + base
            h0[PAD - 1 : PAD, lanes] = base
            h0[PAD - 2 : PAD - 1, lanes] = base - beside[1:2, lanes]
            value = base + part[h - 1 : h, lanes] + beside[2:3, lanes]
            h0[PAD + h : PAD + h + 1, lanes] = value * has_next
            h0[PAD + h + 1 : PAD + h + 2, lanes] = (value + beside[3:4, lanes]) * has_next
        lane = lax.broadcasted_iota(jnp.int32, (8, plan.cols), 1)
        row = lax.broadcasted_iota(jnp.int32, (8, plan.cols), 0)

        def sides(x):
            left = jnp.where(lane == 0, 0.0, pltpu.roll(x, 1, 1))
            right = jnp.where(lane == plan.cols - 1, 0.0, pltpu.roll(x, plan.cols - 1, 1))
            return left, right

        def smooth(src, dst, low, count, masked):
            def one(base):
                value = src[pl.ds(base - 8, 24), :]
                kap = kx[pl.ds(base - 8, 24), :]
                mid, k_mid = value[8:16], kap[8:16]
                left, right = sides(mid)
                k_left, k_right = sides(k_mid)
                new = conducted(
                    mid, value[7:15], value[9:17], left, right, k_mid, kap[7:15], kap[9:17], k_left, k_right
                )
                if masked:
                    n = row + base
                    bad = ((n < PAD) & (place == first)) | ((n >= PAD + h) & (place == last))
                    new = jnp.where(bad, 0.0, new)
                if masked:
                    dst[pl.ds(base, 8), :] = new
                else:
                    at = pl.ds(base - PAD, 8)
                    if not keep:
                        outs[0][at, :] = -new
                        return
                    for b in range(blocks):
                        outs[0][plan.slot(b), at, :] = -new[:, b * INNER : (b + 1) * INNER]
                    kept[pl.ds(base - PAD, 8), :] = -new
                return

            def step(i, carry):
                for n in range(2):
                    one(pl.multiple_of(low + (2 * i + n) * 8, 8))
                return carry

            lax.fori_loop(0, count // 2, step, 0)

        refs = [h0, h1]
        for n in range(SMOOTH):
            if n < SMOOTH - 1:
                smooth(refs[n % 2], refs[(n + 1) % 2], PAD - 8, (h + 16) // 8, True)
            else:
                smooth(refs[n % 2], refs[(n + 1) % 2], PAD, h // 8, False)
        if keep:
            for s, out in enumerate(outs[1:]):
                c = lax.rem(me[1] + s, plan.cross)
                lanes = pl.ds(pl.multiple_of(c * plan.cols_here, plan.cols_here), plan.cols_here)
                out[...] = kept[:, lanes]

    tall = pltpu.VMEM((h + 2 * PAD, plan.cols), F32)
    flat = (h, plan.cols)
    if keep:
        outs = [jax.ShapeDtypeStruct((plan.devices, h, plan.width), F32)]
        outs += [jax.ShapeDtypeStruct((h, plan.cols_here), F32)] * plan.cross
    else:
        outs = [jax.ShapeDtypeStruct(flat, F32)]
    return call(body, outs, [tall] * 3 + [pltpu.VMEM(flat, F32)], (), () if keep else (0,), (), range(len(outs)) if keep else ())(
        kappa, above, below, part, beside, *rest
    )


def rows_heat(plan, matrices, table, received, alpha, side_table, side_alpha):
    width = plan.width
    outer = plan.rows // INNER
    per = INNER // plan.height
    two_rows = lambda a, b: lax.dot_general(a, b, (((1,), (1,)), ((), ())), preferred_element_type=F32)

    def sides(matrices, received, side_table, side_alpha, from_left, from_right):
        h = plan.height
        lane = lax.broadcasted_iota(jnp.int32, (8, INNER), 1)
        row = lambda part: side_table[part : part + 1, :]
        points = []
        for a in range(outer):
            re = jnp.zeros((8, INNER), F32)
            im = re
            for j in range(per):
                part = received[a * per + j, 2 * h : 2 * h + 8, :]
                here = (lane >= j * h) & (lane < (j + 1) * h)
                re = jnp.where(here, pltpu.roll(part, j * h, 1) if j else part, re)
                im = jnp.where(here, pltpu.roll(part, (j * h + INNER - h) % INNER, 1), im)
            points.append((re, im))
        values = []
        for k, value in enumerate(small_fft(points, -1)):
            if k:
                value = times(value, (row(k), row(outer + k)))
            high, low = split(jnp.concatenate(value, axis=1))
            both = two_rows(jnp.concatenate([high, low], axis=0), matrices[k, 0])
            value = both[0:8] + both[8:16] + two_rows(jnp.concatenate([high, high], axis=0), matrices[k, 1])[0:8]
            value = (value[:, :INNER], value[:, INNER:])
            if k:
                value = times(value, (row(k), -row(outer + k)))
            values.append(value)
        deposits = [side_alpha[...] * (re * re + im * im) for re, im in small_fft(values, 1)]
        high, low = split(jnp.concatenate(deposits, axis=0))
        ones = lower_ones(INNER)
        sums = two_rows(high, ones) + two_rows(low, ones)
        carry = jnp.zeros((8, 1), F32)
        none = jnp.zeros((6, INNER), F32)
        for a in range(outer):
            part = sums[8 * a : 8 * a + 8] + carry
            carry = part[:, INNER - 1 : INNER]
            n = slice(a * INNER, (a + 1) * INNER)
            from_left[:, n] = jnp.concatenate([none, part[0:2]], axis=0)
            from_right[:, n] = jnp.concatenate([part[2:4], none], axis=0)

    def body(matrices, table, received, alpha, side_table, side_alpha, heat, from_left, from_right, xh, z, dep):
        def write(a, off, value):
            deposit = alpha[...] * (value[0] * value[0] + value[1] * value[1])
            rows = pl.ds(a * INNER + off, CHUNK)
            dep[rows, 0:width], dep[rows, width : 2 * width] = split(deposit)

        sides(matrices, received, side_table, side_alpha, from_left, from_right)
        along_rows(functools.partial(plan.flip_a, received), write, matrices, table, xh, z)
        tile = 2 * INNER
        ones = lower_ones(tile)
        carry = jnp.zeros((1, width), F32)
        for g in range(plan.rows // tile):
            both = jnp.dot(ones, dep[g * tile : (g + 1) * tile, :], preferred_element_type=F32)
            value = both[:, :width] + both[:, width:] + carry
            heat[g * tile : (g + 1) * tile, :] = value
            carry = value[tile - 1 : tile, :]

    edge = jax.ShapeDtypeStruct((8, plan.rows), F32)
    outs = [jax.ShapeDtypeStruct((plan.rows, width), F32), edge, edge]
    scratch = plan.work_a() + [pltpu.VMEM((plan.rows, 2 * width), BF16)]
    return call(body, outs, scratch, (0, 1, 2), ())(matrices, table, received, alpha, side_table, side_alpha)


def rows_turn(plan, read_field, wide, dft, table, screen, field, far=False):
    def body(dft, table, screen, field, out, *work):
        def read(a, off):
            return screened(read_field(field, a, off), screen[pl.ds(a * INNER + off, CHUNK), :])

        along_rows(read, functools.partial(plan.send_a, out), dft, table, *work)
        if wide:
            plan.send_edges(out)

    out = plan.sent_wide if wide else plan.sent
    return call(body, [out], plan.work_a(), (0, 1, 2), () if far else (0,), (), (0,) if far else ())(dft, table, screen, field)[0]


def rows_smooth(plan, heat, from_left, from_right, kappa, kappa_left, kappa_right, me, *ahead):
    width = plan.width
    PAD = 8
    step_rows = 32

    def body(heat, from_left, from_right, kappa, kappa_left, kappa_right, me, *refs):
        screen, h0, h1, kx = refs[-4:]

        place = me[1] * plan.wind + plan.local(me[0], me[1])
        zeros = jnp.zeros((PAD, 2 * width), F32)
        for ref in (h0, h1, kx):
            ref[0:PAD, :] = zeros
            ref[plan.rows + PAD : plan.rows + 2 * PAD, :] = zeros
        for g in range(plan.rows // INNER):
            n = slice(g * INNER, (g + 1) * INNER)
            spot = slice(PAD + g * INNER, PAD + (g + 1) * INNER)
            for ref, value, left, right in ((h0, heat, from_left, from_right), (kx, kappa, kappa_left, kappa_right)):
                ref[spot, 0:width] = value[n, :]
                beside = [right[:, n], jnp.zeros((width - 16, INNER), F32), left[:, n]]
                ref[spot, width : 2 * width] = jnp.concatenate(beside, axis=0).T
        wide = lax.broadcasted_iota(jnp.int32, (step_rows, 2 * width), 1)
        bad = (wide >= width) & (wide < width + width // 2) & (place == plan.devices - 1)
        bad = bad | ((wide >= width + width // 2) & (place == 0))

        def smooth(src, dst):
            def one(base):
                value = src[pl.ds(base, step_rows + 16), :]
                kap = kx[pl.ds(base, step_rows + 16), :]
                mid, k_mid = value[8:-8], kap[8:-8]
                new = conducted(
                    mid, value[7:-9], value[9:-7], pltpu.roll(mid, 1, 1), pltpu.roll(mid, 2 * width - 1, 1),
                    k_mid, kap[7:-9], kap[9:-7], pltpu.roll(k_mid, 1, 1), pltpu.roll(k_mid, 2 * width - 1, 1),
                )
                dst(base, jnp.where(bad, 0.0, new))

            def step(i, carry):
                for n in range(4):
                    one(pl.multiple_of((4 * i + n) * step_rows, step_rows))
                return carry

            lax.fori_loop(0, plan.rows // (4 * step_rows), step, 0)

        def into(ref):
            def put(base, value):
                ref[pl.ds(base + PAD, step_rows), :] = value

            return put

        def into_screen(base, value):
            screen[pl.ds(base, step_rows), :] = -value[:, :width]

        refs = [h0, h1]
        for n in range(SMOOTH):
            smooth(refs[n % 2], into(refs[(n + 1) % 2]) if n < SMOOTH - 1 else into_screen)

    tall = pltpu.VMEM((plan.rows + 2 * PAD, 2 * width), F32)
    outs = [jax.ShapeDtypeStruct((plan.rows, width), F32)]
    return call(body, outs, [tall] * 3, range(7, 7 + len(ahead)), (0,))(
        heat, from_left, from_right, kappa, kappa_left, kappa_right, me, *ahead
    )[0]


def next_prev(value_up, value_down, axes, order):
    up = list(zip(order[:-1], order[1:]))
    down = [(j, i) for i, j in up]
    return lax.ppermute(value_up, axes, up), lax.ppermute(value_down, axes, down)


def extended(shard, sides, width):
    for axis, dim in sides:
        size, length = (lax.axis_size(axis), shard.shape[dim])
        up = [(i, (i + 1) % size) for i in range(size - 1)]
        down = [(j, i) for i, j in up]
        last = lax.slice_in_dim(shard, length - width, length, axis=dim)
        initial = lax.slice_in_dim(shard, 0, width, axis=dim)
        before = lax.ppermute(last, axis, up)
        after = lax.ppermute(initial, axis, down)
        shard = jnp.concatenate([before, shard, after], axis=dim)
    return shard


def carried_in(part, axis, combine, identity):
    place = lax.axis_index(axis)
    gathered = lax.all_gather(part, axis)
    state = jnp.zeros_like(part) + jnp.asarray(identity, part.dtype)

    def one(turn, state):
        return combine(state, lax.dynamic_index_in_dim(gathered, turn, 0, False))

    return lax.fori_loop(0, place, one, state)


def signed_freq(indices, length):
    shifted = jnp.where(indices < length // 2, indices, indices - length)
    return shifted.astype(jnp.float32) / length


def trig_table(first_ids, second_ids, length, sign_value):
    product = first_ids * second_ids % length
    phase_angle = product.astype(jnp.float32) * (sign_value * 2.0 * math.pi / length)
    return (jnp.cos(phase_angle), jnp.sin(phase_angle))


def complex_product(formula, real_part, imag_part, cosine, sine):
    highest = lax.Precision.HIGHEST
    out_real = jnp.einsum(formula, real_part, cosine, precision=highest) - jnp.einsum(
        formula, imag_part, sine, precision=highest
    )
    out_imag = jnp.einsum(formula, real_part, sine, precision=highest) + jnp.einsum(
        formula, imag_part, cosine, precision=highest
    )
    return (out_real, out_imag)


def transform(stacked, axis_dim, inverse):
    full_shape = stacked.shape
    length = full_shape[axis_dim]
    inner_len = math.gcd(length, 128)
    outer_len = length // inner_len
    leading = full_shape[1] if axis_dim == 2 else 1
    trailing = full_shape[2] if axis_dim == 1 else 1
    blocks = stacked.reshape(2, leading, outer_len, inner_len, trailing)
    sign_value = 1.0 if inverse else -1.0
    outer_ids = jnp.arange(outer_len, dtype=jnp.int32)
    inner_ids = jnp.arange(inner_len, dtype=jnp.int32)
    cos_outer, sin_outer = trig_table(outer_ids[:, None], outer_ids[None, :], outer_len, sign_value)
    first_real, first_imag = complex_product(
        "pabq,ak->pkbq", blocks[0], blocks[1], cos_outer, sin_outer
    )
    cos_twist, sin_twist = trig_table(outer_ids[:, None], inner_ids[None, :], length, sign_value)
    cos_twist = cos_twist[None, :, :, None]
    sin_twist = sin_twist[None, :, :, None]
    twist_real = first_real * cos_twist - first_imag * sin_twist
    twist_imag = first_real * sin_twist + first_imag * cos_twist
    cos_inner, sin_inner = trig_table(inner_ids[:, None], inner_ids[None, :], inner_len, sign_value)
    second_real, second_imag = complex_product(
        "pkbq,bm->pkmq", twist_real, twist_imag, cos_inner, sin_inner
    )
    result = jnp.stack([second_real, second_imag]).transpose(0, 1, 3, 2, 4).reshape(full_shape)
    if inverse:
        result = result * (1.0 / length)
    return result


def apply_phase(stacked, phase_angle):
    cosine = jnp.cos(phase_angle)
    sine = jnp.sin(phase_angle)
    return jnp.stack(
        [stacked[0] * cosine - stacked[1] * sine, stacked[0] * sine + stacked[1] * cosine]
    )


def along_joint(stacked, phase_rate, row_freq, col_freq):
    cross_count = lax.axis_size("cross")
    stacked = lax.all_to_all(stacked, ("wind", "cross"), split_axis=2, concat_axis=1, tiled=True)
    stacked = transform(stacked, 1, False)
    col_width = stacked.shape[2]
    joint_block = lax.axis_index("wind") * cross_count + lax.axis_index("cross")
    cols_held = lax.dynamic_slice_in_dim(col_freq, joint_block * col_width, col_width)
    phase_angle = -phase_rate * (
        row_freq[:, None] * row_freq[:, None] + cols_held[None, :] * cols_held[None, :]
    )
    stacked = apply_phase(stacked, phase_angle)
    stacked = transform(stacked, 1, True)
    return lax.all_to_all(stacked, ("wind", "cross"), split_axis=1, concat_axis=2, tiled=True)


def propagate_slab(slab_pair, share_step):
    rows_total = slab_pair.shape[1] * lax.axis_size("wind") * lax.axis_size("cross")
    cols_total = slab_pair.shape[2]
    phase_rate = share_step * diffraction
    row_freq = signed_freq(jnp.arange(rows_total, dtype=jnp.int32), rows_total)
    col_freq = signed_freq(jnp.arange(cols_total, dtype=jnp.int32), cols_total)
    stacked = transform(slab_pair, 2, False)
    stacked = along_joint(stacked, phase_rate, row_freq, col_freq)
    return transform(stacked, 2, True)


def conduct_core(padded, kappa_pad):
    height = padded.shape[0] - 2
    breadth = padded.shape[1] - 2
    center = padded[1:-1, 1:-1]
    kappa_mid = kappa_pad[1:-1, 1:-1]
    flux_sum = jnp.zeros_like(center)
    for offset_row, offset_col in ((0, 1), (2, 1), (1, 0), (1, 2)):
        neighbour = padded[offset_row : offset_row + height, offset_col : offset_col + breadth]
        kappa_side = kappa_pad[offset_row : offset_row + height, offset_col : offset_col + breadth]
        flux_sum = flux_sum + 0.5 * (kappa_mid + kappa_side) * (neighbour - center)
    return center + conduct_rate * flux_sum


def add_terms(earlier, later_term):
    return earlier + later_term


def layer_absorption(index_row, table_row, level_ids):
    one_hot = (index_row[:, None] == level_ids[None, :]).astype(jnp.float32)
    return jnp.sum(one_hot * table_row[None, :], axis=1)


def wide_device(field_real, field_imag, absorb_index, absorb_table, zone_map, zone_conductivity):
    rows_here, cols_here = field_real.shape
    conductivity = jnp.zeros((rows_here, cols_here), jnp.float32)
    for zone_no in range(zone_conductivity.shape[0]):
        conductivity = jnp.where(zone_map == zone_no, zone_conductivity[zone_no], conductivity)
    level_ids = jnp.arange(absorb_table.shape[1], dtype=jnp.int32)
    combined = lax.all_to_all(
        jnp.stack([field_real, field_imag, conductivity]),
        "cross",
        split_axis=1,
        concat_axis=2,
        tiled=True,
    )
    slab_pair = combined[:2]
    kappa_rows = extended(combined[2], ((("wind", "cross"), 0),), 1)
    kappa_pad = jnp.pad(kappa_rows, ((0, 0), (1, 1)))
    index_full = lax.all_gather(absorb_index, "cross", axis=1, tiled=True)
    slab_rows = slab_pair.shape[1]
    rows_total = slab_rows * lax.axis_size("wind") * lax.axis_size("cross")
    slab_ids = jnp.arange(slab_rows, dtype=jnp.int32)
    lower_slab = (slab_ids[:, None] >= slab_ids[None, :]).astype(jnp.float32)
    screen_phase = jnp.zeros((slab_rows, slab_pair.shape[2]), jnp.float32)
    for layer_no in range(LAYERS):
        absorption = layer_absorption(index_full[layer_no], absorb_table[layer_no], level_ids)
        screen_phase = jnp.zeros((slab_rows, slab_pair.shape[2]), jnp.float32)
        for _ in range(ITERS):
            middle = propagate_slab(apply_phase(slab_pair, screen_phase), 0.5)
            intensity = middle[0] * middle[0] + middle[1] * middle[1]
            deposit = absorption[None, :] * intensity * (1.0 / rows_total)
            partial_heat = jnp.dot(lower_slab, deposit, precision=lax.Precision.HIGHEST)
            totals = partial_heat[-1]
            upstream = carried_in(totals, ("wind", "cross"), add_terms, jnp.zeros_like(totals))
            heat_field = partial_heat + upstream[None, :]
            for _ in range(SMOOTH):
                padded = extended(heat_field, ((("wind", "cross"), 0),), 1)
                padded = jnp.pad(padded, ((0, 0), (1, 1)))
                heat_field = conduct_core(padded, kappa_pad)
            screen_phase = -heat_field
        slab_pair = propagate_slab(apply_phase(slab_pair, screen_phase), 1.0)
    returned = lax.all_to_all(
        jnp.stack([slab_pair[0], slab_pair[1], screen_phase]),
        "cross",
        split_axis=2,
        concat_axis=1,
        tiled=True,
    )
    return (returned[0], returned[1], returned[2])


def on_device(field_real, field_imag, absorb_index, absorb_table, zone_map, zone_conductivity):
    plan = Plan(*field_real.shape, lax.axis_size("wind"), lax.axis_size("cross"))
    fits = plan.width == INNER and INNER % plan.height == 0 and plan.height % CHUNK == 0
    if not fits or plan.rows_here % INNER or plan.rows % (2 * INNER):
        return wide_device(field_real, field_imag, absorb_index, absorb_table, zone_map, zone_conductivity)
    return tiled_device(plan, field_real, field_imag, absorb_index, absorb_table, zone_map, zone_conductivity)


def tiled_device(plan, field_real, field_imag, absorb_index, absorb_table, zone_map, zone_conductivity):
    cross = plan.cross
    w, c = lax.axis_index("wind"), lax.axis_index("cross")
    place = jnp.stack([w, c]).astype(jnp.int32)
    grid_axes = ("wind", "cross")

    def exchange(x, axes):
        return lax.all_to_all(x, axes, split_axis=0, concat_axis=0, tiled=True)

    def flip(x):
        return exchange(x, grid_axes)

    to_b, *field_blocks = prepare_field(plan, field_real, field_imag, place)
    home_b = exchange(to_b, "cross")
    field_blocks = shifted(field_blocks, "wind")
    *across, kappa, left, right, alpha_a, alpha = prepare(
        plan, zone_map, absorb_index, absorb_table, zone_conductivity, place
    )
    side_alpha, *along = home_kappa(plan, kappa, *next_prev(right, left, "cross", list(range(cross))), alpha, place)

    dft = jnp.asarray(dft_matrices())
    tab_a = lambda share: (jnp.asarray(row_blocks(plan.rows, share)), jnp.asarray(row_table(plan.rows)))
    tab_b_of = lambda length: jnp.asarray(chirp_columns(length, ()))
    tab_b = lambda *shares: jnp.asarray(chirp_columns(plan.cols, shares))

    def smooth_a(layer, share, received, *ahead):
        heat, from_left, from_right = rows_heat(
            plan, *tab_a(share), received, alpha_a[layer : layer + 1], tab_b_of(plan.rows), side_alpha[layer]
        )
        return rows_smooth(plan, heat, from_left, from_right, *kappas, place, *ahead)

    def smooth_b(layer, keep, received):
        part, beside, totals = cols_heat(plan, layer, plan.devices, dft, tab_b(0.5), received, alpha_b)
        return cols_smooth(plan, keep, kappa_b, above, below, part, beside, flip(totals), place)

    home_b, across = lax.optimization_barrier((home_b, across))
    sent = cols_send(plan, plan.home_b, False, dft, tab_b(0.5), home_b, True)
    kappa_b, alpha_b = home_rows(plan, shifted(across, "cross"), place)
    above, below = next_prev(kappa_b[-8:], kappa_b[:8], grid_axes, list(range(plan.devices)))
    received, along = lax.optimization_barrier((flip(sent), along))
    along = shifted(along, "wind")
    kappas = rows_kappa(plan, along, place)
    home_a = in_order(field_blocks, place, 0)
    screen = smooth_a(0, 0.5, received)
    sent = rows_turn(plan, plan.home_a, True, *tab_a(0.5), screen, home_a, True)
    received, above, below = lax.optimization_barrier((flip(sent), above, below))
    (screen,) = smooth_b(0, False, received)
    sent_middle, sent_field = cols_turn(plan, plan.home_b, 2, dft, tab_b(1.5, 1.0), screen, home_b)
    middle = flip(sent_middle)
    field = flip(sent_field)
    whole_share = tab_a(1.0)
    screen = smooth_a(1, 1.5, middle, whole_share[0])
    field, screen = lax.optimization_barrier((field, screen))
    field = rows_field(plan, plan.flip_a, *whole_share, field)
    sent = rows_turn(plan, plan.flip_a, True, *tab_a(0.5), screen, field)
    screen, *home_parts = smooth_b(1, True, flip(sent))
    home_parts = shifted(home_parts, "cross")
    screen = flip(screen).reshape(plan.rows, plan.width)
    sent = rows_turn(plan, plan.flip_a, False, *whole_share, screen, field)
    back = cols_send(plan, plan.flip_b, True, dft, tab_b(1.0), flip(sent))
    screen = home_screen(plan, home_parts, place)
    back = exchange(back, "cross")
    out_real = back[:, : plan.height].reshape(field_real.shape)
    out_imag = back[:, plan.height :].reshape(field_real.shape)
    return (out_real, out_imag, screen)


def solution(mesh):
    in_specs = (
        P(("beams", "wind"), "cross"),
        P(("beams", "wind"), "cross"),
        P(None, "cross"),
        P(),
        P("wind", "cross"),
        P(),
    )
    out_specs = (
        P(("beams", "wind"), "cross"),
        P(("beams", "wind"), "cross"),
        P(("beams", "wind"), "cross"),
    )
    return jax.shard_map(on_device, mesh=mesh, in_specs=in_specs, out_specs=out_specs, check_vma=False)
```
